512 devices in a mesh: dp: 16 (over x_lo, y), tensor: 32 (over x_hi, z, core).
Axes of the slice: x: 4 (x_hi: 2, x_lo: 2; x = x_hi * 2 + x_lo), y: 8, z: 8, core: 2. Of those that a mesh axis runs over, the one named last changes fastest.
Arguments:
- tokens: bfloat16 [4096, 14336], P('dp', 'tensor'), may hold values from -6 to 6
- base_weight: bfloat16 [14336, 4096], P('tensor'), may hold values from -0.5 to 0.5
- adapter_down: bfloat16 [16, 14336, 16], P(None, 'tensor'), may hold values from -0.046875 to 0.046875
- adapter_up: bfloat16 [16, 16, 4096], P(None, None, 'tensor'), may hold values from -1.5 to 1.5
- magnitude: bfloat16 [16, 4096], P(None, 'tensor'), may hold values from 0.5 to 2
- seg_lengths: int32 [16], replicated, may hold values from 1 to 2048, 4096 in all
- cotangent: bfloat16 [4096, 4096], P('dp', 'tensor'), may hold values from -6 to 6
Outputs:
- projected: bfloat16 [4096, 4096], P('dp', 'tensor')
- grad_tokens: bfloat16 [4096, 14336], P('dp', 'tensor')
- grad_down: bfloat16 [16, 14336, 16], P(None, 'tensor')
- grad_up: float32 [16, 16, 4096], P(None, None, 'tensor')
- grad_magnitude: float32 [16, 4096], P(None, 'tensor')
The draws below stay inside these ranges and needn't reach their ends.
Inputs may be any that keep to these rules, and one draw needn't show every extreme that they name: The segments cover all 4096 tokens in order: seg_lengths sums to 4096.
All inputs are finite; a program needn't handle non-finite values.
Results may differ from the reference program's by a relative error of at most 0.019.
Values may be sent and summed in bfloat16 or wider, within the bound.
No kernel may reach another device: no remote copies, remote signals or barrier semaphores. Data moves between devices by JAX's collectives and lax.ppermute only.
A program may use at most 64 MiB of HBM per device.

```python
import math
import jax
import jax.numpy as jnp
import numpy as np
from jax import lax

D = 4096
FF = 14336
ADAPTERS = 16
RANK = 16
TOKENS = 4096
N_TENSOR = 32


def draw_base_weight(key, part):
    entry_key, row_key = jax.random.split(jax.random.fold_in(key, 11))
    fraction = jnp.arange(FF, dtype=jnp.float32) / (FF - 1)
    entries = jax.random.normal(entry_key, (FF, D), jnp.float32)
    row_scale = jnp.exp(jax.random.uniform(row_key, (FF, 1), jnp.float32, 0.0, math.log(10.0)))
    mean_square = 99.0 / (2.0 * math.log(10.0))
    rising = jnp.sqrt(1.0 + 2.0 * fraction)[:, None]
    values = entries * row_scale * rising / jnp.sqrt(2.0 * mean_square * FF)
    return jnp.clip(values, -0.5, 0.5).astype(jnp.bfloat16)


def steps_of(rng, extent, pieces, smallest, high):
    loudness = 1.0
    for dim, blocks in pieces:
        heights = jax.random.uniform(jax.random.fold_in(jax.random.fold_in(rng, 6), dim), (blocks,), jnp.float32, smallest / len(pieces), high / len(pieces))
        loudness = loudness * jnp.repeat(jnp.exp(heights), extent[dim] // blocks).reshape((-1,) + (1,) * (len(extent) - 1 - dim))
    return loudness


def split_up(amount, total, limit, skew):
    weights = [(1 << 20) // math.isqrt(standing ** skew) + 1 for standing in range(2, amount + 1)]
    spare, given = total - limit - (amount - 1), [1] * (amount - 1)
    while spare > 0:
        free = [i for i in range(amount - 1) if given[i] < limit]
        pool, remaining = sum([weights[i] for i in free]), spare
        for i in free:
            more = min(limit - given[i], max(1, remaining * weights[i] // pool), spare)
            given[i] = given[i] + more
            spare = spare - more
    return np.array([limit] + given)


def ragged(own_key, number_of, total, most, skew):
    if number_of == 2:
        one = jax.random.randint(own_key, (), max(1, total - most), min(most, total - 1) + 1)
        return jnp.stack([one, total - one])
    lengths = jnp.asarray(split_up(number_of, total, most, skew), jnp.int32)
    twos = (number_of - 1) // 2
    donor, sink = lengths[1:1 + 2 * twos:2], lengths[2:2 + 2 * twos:2]
    room = jnp.minimum(donor - 1, most - sink)
    moved = jax.random.randint(jax.random.fold_in(own_key, 1), (twos,), 0, 1 << 20) % (room + 1)
    lengths = lengths.at[1:1 + 2 * twos:2].set(donor - moved).at[2:2 + 2 * twos:2].set(sink + moved)
    return lengths[jax.random.permutation(jax.random.fold_in(own_key, 2), number_of)]


def gaussian(stream_key, extent, scale, most, pieces=(), kind=jnp.bfloat16):
    values = jax.random.normal(stream_key, extent, jnp.float32) * scale
    if len(pieces) > 0:
        values = steps_of(stream_key, extent, pieces, -0.22, 0.18) * values
    return jnp.clip(values, min=-most, max=most).astype(kind)


def setup_inputs(seed: int = 0) -> dict:
    streams_of = jax.random.split(jax.random.key(seed), 8)
    tokens = gaussian(streams_of[0], (TOKENS, FF), 1.0, 6.0, ((0, 16), (1, 32)))
    base_weight = draw_base_weight(jax.random.fold_in(streams_of[7], 71), 0)
    adapter_down = gaussian(streams_of[2], (ADAPTERS, FF, RANK), FF ** -0.5, 0.046875, ((1, 32),))
    adapter_up = gaussian(streams_of[3], (ADAPTERS, RANK, D), RANK ** -0.5, 1.5, ((2, 32),))
    magnitude = jnp.clip(jnp.exp(math.log(2.0) - 1.3862944 * jax.random.uniform(streams_of[4], (ADAPTERS, D), jnp.float32) ** steps_of(streams_of[4], (ADAPTERS, D), ((1, 32),), -0.2, 0.2)), 0.5, 2.0).astype(jnp.bfloat16)
    seg_lengths = ragged(streams_of[5], ADAPTERS, TOKENS, TOKENS // 2, 2).astype(jnp.int32)
    cotangent = gaussian(streams_of[6], (TOKENS, D), 1.0, 6.0, ((0, 16), (1, 32)))
    return {"tokens": tokens, "base_weight": base_weight, "adapter_down": adapter_down, "adapter_up": adapter_up, "magnitude": magnitude, "seg_lengths": seg_lengths, "cotangent": cotangent}


HIGHEST_MODE = lax.Precision.HIGHEST
EPSILON = 1e-06

def member_table(seg_lengths, first_token, token_count):
    seg_ends = jnp.cumsum(seg_lengths).astype(jnp.int32)
    seg_starts = seg_ends - seg_lengths
    positions = first_token + jnp.arange(token_count, dtype=jnp.int32)[:, None]
    return ((positions >= seg_starts[None, :]) & (positions < seg_ends[None, :])).astype(jnp.float32)

def pick_rank(member, spread):
    token_count, adapter_count = member.shape
    return jnp.einsum('ta,tar->tr', member, spread.reshape(token_count, adapter_count, -1), precision=HIGHEST_MODE)

def expand_rank(member, low_rounded):
    widened = member[:, :, None] * low_rounded.astype(jnp.float32)[:, None, :]
    return widened.reshape(member.shape[0], -1).astype(jnp.bfloat16)

def reference(tokens, base_weight, adapter_down, adapter_up, magnitude, seg_lengths, cotangent):
    member = member_table(seg_lengths, 0, TOKENS)

    def column_square(pair):
        merged = base_weight.astype(jnp.float32) + jnp.dot(pair[0], pair[1], preferred_element_type=jnp.float32)
        return lax.optimization_barrier(jnp.sum(merged * merged, axis=0))
    col_norms = jnp.sqrt(lax.map(column_square, (adapter_down, adapter_up)) + EPSILON)
    col_scale = magnitude.astype(jnp.float32) / col_norms
    token_scale = jnp.dot(member, col_scale, precision=HIGHEST_MODE)
    shard_rows = FF // N_TENSOR
    token_blocks = jnp.transpose(tokens.reshape(TOKENS, N_TENSOR, shard_rows), (1, 0, 2))
    weight_blocks = base_weight.reshape(N_TENSOR, shard_rows, D)

    def add_shard(running, pair):
        term = jnp.dot(pair[0], pair[1], preferred_element_type=jnp.float32).astype(jnp.bfloat16)
        term = lax.optimization_barrier(term)
        return (running + term.astype(jnp.float32), None)
    base_sum, _ = lax.scan(add_shard, jnp.zeros((TOKENS, D), jnp.float32), (token_blocks, weight_blocks))
    down_flat = jnp.transpose(adapter_down, (1, 0, 2)).reshape(FF, ADAPTERS * RANK)
    up_flat = adapter_up.reshape(ADAPTERS * RANK, D)
    low_rank = pick_rank(member, jnp.dot(tokens, down_flat, preferred_element_type=jnp.float32))
    low_wide = expand_rank(member, low_rank.astype(jnp.bfloat16))
    hidden = base_sum + jnp.dot(low_wide, up_flat, preferred_element_type=jnp.float32)
    projected = (hidden * token_scale).astype(jnp.bfloat16)
    grad_in = cotangent.astype(jnp.float32)
    grad_magnitude = jnp.dot(member.T, grad_in * hidden, precision=HIGHEST_MODE) / col_norms
    grad_hidden = (grad_in * token_scale).astype(jnp.bfloat16)
    grad_up = jnp.dot(low_wide.T, grad_hidden, preferred_element_type=jnp.float32).reshape(ADAPTERS, RANK, D)
    back_rank = pick_rank(member, jnp.dot(grad_hidden, up_flat.T, preferred_element_type=jnp.float32))
    back_wide = expand_rank(member, back_rank.astype(jnp.bfloat16))
    grad_tokens = jnp.dot(grad_hidden, base_weight.T, preferred_element_type=jnp.float32)
    grad_tokens = (grad_tokens + jnp.dot(back_wide, down_flat.T, preferred_element_type=jnp.float32)).astype(jnp.bfloat16)
    grad_down = jnp.dot(tokens.T, back_wide, preferred_element_type=jnp.float32).reshape(FF, ADAPTERS, RANK)
    grad_down = jnp.transpose(grad_down, (1, 0, 2)).astype(jnp.bfloat16)
    return (projected, grad_tokens, grad_down, grad_up, grad_magnitude)
```

```python
import jax
import jax.numpy as jnp
from jax import lax
from jax.sharding import PartitionSpec as P

HIGHEST_MODE = lax.Precision.HIGHEST
EPSILON = 1e-06
F32 = jnp.float32
BF16 = jnp.bfloat16
LANES = 128


def member_table(seg_lengths, first_token, token_count):
    ends = jnp.cumsum(seg_lengths)
    starts = ends - seg_lengths
    at = first_token + jnp.arange(token_count, dtype=jnp.int32)[None, :]
    return ((at >= starts[:, None]) & (at < ends[:, None])).astype(F32)


def picked(spread, member):
    count, tokens = member.shape
    return jnp.sum(spread.reshape(count, -1, tokens) * member[:, None, :], axis=0)


def widened(member, rank_rows):
    wide = member[:, None, :] * rank_rows.astype(F32)[None, :, :]
    return wide.reshape(-1, member.shape[1]).astype(BF16)


def packed(rows):
    return jnp.concatenate([rows[:, :LANES], rows[:, LANES:]], axis=0)


def unpacked(rows):
    half = rows.shape[0] // 2
    return jnp.concatenate([rows[:half], rows[half:]], axis=1)


def dot(a, b, ca, cb, precision=None):
    return lax.dot_general(
        a, b, (((ca,), (cb,)), ((), ())), precision=precision, preferred_element_type=F32
    )


def exchange(blocks, axis, groups=None):
    return lax.all_to_all(blocks, axis, 0, 0, tiled=True, axis_index_groups=groups)


def local(tokens, base_weight, adapter_down, adapter_up, magnitude, seg_lengths, cotangent):
    token_count, own_rows = tokens.shape
    adapters, _, rank = adapter_down.shape
    own_width = adapter_up.shape[2]
    full_width = base_weight.shape[1]
    size = full_width // own_width
    ZS = size // 4
    me_dp = lax.axis_index("dp")
    me = lax.axis_index("tensor")
    core, hi = me % 2, me // (2 * ZS)
    core_pairs = [(i, i ^ 1) for i in range(size)]
    hi_pairs = [(i, (i + size // 2) % size) for i in range(size)]
    z_groups = [[h * 2 * ZS + z * 2 + c for z in range(ZS)] for h in range(2) for c in range(2)]

    member = member_table(seg_lengths, me_dp * token_count, token_count)
    down_rows = jnp.transpose(adapter_down, (0, 2, 1))
    down_flat = down_rows.reshape(adapters * rank, own_rows)
    up_own = adapter_up.reshape(adapters * rank, own_width)

    down_mine = lax.dynamic_index_in_dim(down_rows, me_dp, 0, keepdims=False)
    cross = dot(down_mine, base_weight, 1, 0)
    gram = dot(down_mine, down_mine, 1, 1)
    share = 32
    pieces = own_rows // share
    part_rows = lax.dynamic_slice_in_dim(
        base_weight, jnp.minimum(me_dp, pieces - 1) * share, share, 0
    ).astype(F32)
    squares = jnp.sum(part_rows * part_rows, axis=0) * (me_dp < pieces).astype(F32)
    first = jnp.concatenate(
        [
            cross.astype(BF16).reshape(rank, size, own_width).transpose(1, 0, 2),
            squares.astype(BF16).reshape(size, 1, own_width),
            jnp.broadcast_to(
                gram.astype(BF16).reshape(1, rank * rank // own_width, own_width),
                (size, rank * rank // own_width, own_width),
            ),
        ],
        axis=1,
    )
    first = jnp.sum(exchange(first, "tensor").astype(F32), axis=0)

    low_part = picked(dot(down_flat, tokens, 1, 1), member)
    base = dot(tokens, base_weight, 1, 0).astype(BF16)
    base = base.reshape(token_count, size // 2, 2, own_width).transpose(2, 1, 0, 3)
    keep = lax.dynamic_index_in_dim(base, core, 0, keepdims=False)
    give = lax.dynamic_index_in_dim(base, 1 - core, 0, keepdims=False)
    got = lax.ppermute(give, "tensor", core_pairs)
    base = (keep.astype(F32) + got.astype(F32)).astype(BF16)
    base = base.reshape(2, ZS, token_count, own_width)
    keep = lax.dynamic_index_in_dim(base, hi, 0, keepdims=False)
    give = lax.dynamic_index_in_dim(base, 1 - hi, 0, keepdims=False)
    got = lax.ppermute(give, "tensor", hi_pairs)
    base = (keep.astype(F32) + got.astype(F32)).astype(BF16)

    up_mine = lax.dynamic_index_in_dim(adapter_up, me_dp, 0, keepdims=False).astype(F32)
    gram = first[rank + 1 :].reshape(rank, rank)
    mine = jnp.sum(
        up_mine * (2.0 * first[:rank] + dot(gram, up_mine, 1, 0, HIGHEST_MODE)), axis=0
    )
    second = jnp.stack([mine, first[rank]])
    second = exchange(jnp.broadcast_to(second[None], (adapters, *second.shape)), "dp")
    squares = second[:, 0] + jnp.sum(second[:, 1], axis=0)[None, :]
    col_norms = jnp.sqrt(jnp.maximum(squares, 0.0) + EPSILON)
    col_scale = magnitude.astype(F32) / col_norms

    token_scale = dot(member, col_scale, 0, 0, HIGHEST_MODE)
    grad_in = cotangent.astype(F32)
    grad_own = (grad_in * token_scale).astype(BF16)
    back_part = picked(dot(up_own, grad_own, 1, 1), member)

    every = jnp.concatenate(
        [grad_own, packed(low_part.astype(BF16)), packed(back_part.astype(BF16))], axis=0
    )
    third = jnp.concatenate([base, jnp.broadcast_to(every[None], (ZS, *every.shape))], axis=1)
    third = exchange(third, "tensor", z_groups)
    ranks = jnp.sum(third[:, 2 * token_count :].astype(F32), axis=0)
    ranks = ranks + lax.ppermute(ranks.astype(BF16), "tensor", hi_pairs).astype(F32)
    ranks = ranks + lax.ppermute(ranks.astype(BF16), "tensor", core_pairs).astype(F32)
    low_wide = widened(member, unpacked(ranks[: 2 * rank]).astype(BF16))
    back_wide = widened(member, unpacked(ranks[2 * rank :]).astype(BF16))

    hidden = jnp.sum(third[:, :token_count].astype(F32), axis=0) + dot(low_wide, up_own, 0, 0)
    projected = (hidden * token_scale).astype(BF16)
    mag_part = dot(member, grad_in * hidden, 1, 0, HIGHEST_MODE)
    up_part = dot(low_wide, grad_own, 1, 0)
    down_part = dot(back_wide, tokens, 1, 0)

    pad = -own_rows % LANES
    mag_rows = own_width // pad
    fourth = jnp.concatenate(
        [
            down_part.astype(BF16).reshape(adapters, rank, own_rows),
            jnp.pad(
                mag_part.astype(BF16).reshape(adapters, mag_rows, pad),
                ((0, 0), (0, rank - mag_rows), (0, 0)),
            ),
            up_part.astype(BF16).reshape(adapters, rank, own_width),
        ],
        axis=2,
    )
    fourth = jnp.sum(exchange(fourth, "dp").astype(F32), axis=0).astype(BF16)
    fifth = exchange(jnp.broadcast_to(fourth[None], (adapters, *fourth.shape)), "dp")
    grad_down = jnp.transpose(fifth[:, :, :own_rows], (0, 2, 1))
    grad_up = fifth[:, :, own_rows + pad :].astype(F32)
    mag_sum = fifth[:, :mag_rows, own_rows : own_rows + pad].astype(F32)
    grad_magnitude = mag_sum.reshape(adapters, own_width) / col_norms

    gathered = third[:, token_count : 2 * token_count]
    other = lax.ppermute(gathered, "tensor", hi_pairs)
    gathered = jnp.where(
        hi == 0, jnp.stack([gathered, other]), jnp.stack([other, gathered])
    ).reshape(2 * ZS, token_count, own_width)
    other = lax.ppermute(gathered, "tensor", core_pairs)
    whole = jnp.where(
        core == 0, jnp.stack([gathered, other], 1), jnp.stack([other, gathered], 1)
    )
    whole = whole.transpose(2, 0, 1, 3).reshape(token_count, full_width)
    grad_tokens = dot(whole, base_weight, 1, 1) + dot(back_wide, down_flat, 0, 0)
    return (projected, grad_tokens.astype(BF16), grad_down, grad_up, grad_magnitude)


def solution(mesh):
    placed = (
        P("dp", "tensor"),
        P("tensor", None),
        P(None, "tensor", None),
        P(None, None, "tensor"),
        P(None, "tensor"),
        P(),
        P("dp", "tensor"),
    )
    return jax.shard_map(
        local,
        mesh=mesh,
        in_specs=placed,
        out_specs=(
            P("dp", "tensor"),
            P("dp", "tensor"),
            P(None, "tensor", None),
            P(None, None, "tensor"),
            P(None, "tensor"),
        ),
        check_vma=False,
    )
```

```python
import jax
import jax.numpy as jnp
from jax import lax
from jax.experimental import pallas as pl
from jax.experimental.pallas import tpu as pltpu
from jax.sharding import PartitionSpec as P


HIGHEST_MODE = lax.Precision.HIGHEST
EPSILON = 1e-06
F32 = jnp.float32
BF16 = jnp.bfloat16
I32 = jnp.int32
LANES = 128
HEAD = 24


def dot(a, b, ca, cb, precision=None):
    return lax.dot_general(
        a, b, (((ca,), (cb,)), ((), ())), precision=precision, preferred_element_type=F32
    )


def iota(shape, dim):
    return lax.broadcasted_iota(I32, shape, dim)


def shaped(*dims, dtype=BF16):
    return jax.ShapeDtypeStruct(dims, dtype)


def bounds(seg, adapters, first_token):
    marks, at = [], -first_token
    for a in range(adapters):
        marks.append((at, at + seg[a]))
        at = at + seg[a]
    return marks


def picked(spread, marks):
    rank = spread.shape[0] // len(marks)
    at = iota((rank, spread.shape[1]), 1)
    total = jnp.zeros((rank, spread.shape[1]), F32)
    for a, (lo, hi) in enumerate(marks):
        total += jnp.where((at >= lo) & (at < hi), spread[a * rank : (a + 1) * rank], 0.0)
    return total


def widened(rank_rows, marks):
    at = iota(rank_rows.shape, 1)
    wide = [jnp.where((at >= lo) & (at < hi), rank_rows, 0.0) for lo, hi in marks]
    return jnp.concatenate(wide, axis=0).astype(BF16)


def packed(rows):
    return jnp.concatenate([rows[:, :LANES], rows[:, LANES:]], axis=0)


def unpacked(rows):
    half = rows.shape[0] // 2
    return jnp.concatenate([rows[:half], rows[half:]], axis=1)


def token_scale_of(col_scale, marks, token_count):
    at = iota((token_count, LANES), 0)
    total = jnp.zeros((token_count, LANES), F32)
    for a, (lo, hi) in enumerate(marks):
        total += jnp.where((at >= lo) & (at < hi), col_scale[a : a + 1], 0.0)
    return total


def shift(block, pairs):
    return lax.ppermute(block, "tensor", pairs)


def call(kernel, out_shape, scalars=0, grid=(), in_specs=None, out_specs=None, scratch=(),
         flops=0, moved=0):
    return pl.pallas_call(
        kernel,
        out_shape=out_shape,
        grid_spec=pltpu.PrefetchScalarGridSpec(
            num_scalar_prefetch=scalars,
            grid=grid,
            in_specs=in_specs,
            out_specs=out_specs,
            scratch_shapes=list(scratch),
        ),
        cost_estimate=pl.CostEstimate(flops=flops, bytes_accessed=moved, transcendentals=0),
        compiler_params=pltpu.CompilerParams(vmem_limit_bytes=16 * 2**20),
    )


def whole(*dims):
    return pl.BlockSpec(dims, lambda *ids: (0,) * len(dims))


def first_kernel(where, tokens, weight, down, head, keep, give, gram, lines):
    rank = down.shape[1]
    count = tokens.shape[1]

    @pl.when(pl.program_id(0) == 0)
    def _():
        mine = down[0]
        lines[:count] = tokens[...].T
        lines[count:] = mine
        square = dot(mine, mine, 1, 1)
        tile = (iota((rank, LANES), 1) % rank == iota((rank, LANES), 0)).astype(F32)
        spread = dot(square, tile, 1, 0, HIGHEST_MODE)
        rows, cols = iota((rank, LANES), 0), iota((rank, LANES), 1)
        spread = jnp.where(cols // rank == rows % 8, spread, 0.0)
        gram[0:1, :] = jnp.sum(spread[:8], axis=0, keepdims=True)
        gram[1:2, :] = jnp.sum(spread[8:], axis=0, keepdims=True)

    block = weight[...]
    both = dot(lines[...], block, 1, 0)
    share = 32
    pieces = weight.shape[0] // share
    part = weight[pl.ds(pl.multiple_of(jnp.minimum(where[0], pieces - 1) * share, share), share), :]
    part = part.astype(F32)
    squares = jnp.sum(part * part, axis=0, keepdims=True) * (where[0] < pieces).astype(F32)
    row = iota((8, LANES), 0)
    for k in range(4):
        lanes = slice(k * LANES, (k + 1) * LANES)
        tail = jnp.where(
            row == 0,
            squares[:, lanes],
            jnp.where(row == 1, gram[0:1, :], jnp.where(row == 2, gram[1:2, :], 0.0)),
        )
        head[k] = jnp.concatenate([both[count:, lanes], tail], axis=0).astype(BF16)

    base = both[:count].astype(BF16)

    @pl.when(where[1] == 0)
    def _():
        for k in range(2):
            keep[k] = base[:, 2 * k * LANES : (2 * k + 1) * LANES]
            give[k] = base[:, (2 * k + 1) * LANES : (2 * k + 2) * LANES]

    @pl.when(where[1] != 0)
    def _():
        for k in range(2):
            give[k] = base[:, 2 * k * LANES : (2 * k + 1) * LANES]
            keep[k] = base[:, (2 * k + 1) * LANES : (2 * k + 2) * LANES]


def low_kernel(where, seg, tokens, down, low):
    marks = bounds(seg, seg.shape[0], where[0] * tokens.shape[1])
    spread = dot(down[...], tokens[...], 1, 0)
    low[...] = packed(picked(spread, marks)).astype(BF16)


def halves_kernel(where, keep_a, got_a, keep_b, got_b, keep, give):
    keep[...] = (keep_a[...].astype(F32) + got_a[...].astype(F32)).astype(BF16)
    give[...] = (keep_b[...].astype(F32) + got_b[...].astype(F32)).astype(BF16)


def squares_kernel(where, head, up, second):
    rank = up.shape[1]
    total = jnp.sum(head[...].astype(F32), axis=0)
    factor = up[0].astype(F32)
    rows, cols = iota((rank, LANES), 0), iota((rank, LANES), 1)
    spread = jnp.where(rows < 8, total[rank + 1 : rank + 2], total[rank + 2 : rank + 3])
    spread = jnp.where(cols // rank == rows % 8, spread, 0.0)
    tiled = jnp.concatenate([factor] * (LANES // rank), axis=0)
    gram_up = dot(spread, tiled, 1, 0, HIGHEST_MODE)
    mine = jnp.sum(factor * (2.0 * total[:rank] + gram_up), axis=0, keepdims=True)
    both = jnp.concatenate([mine, total[rank : rank + 1]], axis=0)
    second[...] = jnp.broadcast_to(both[None], second.shape)


def scale_kernel(where, seg, second, magnitude, cotangent, up, low, keep, got,
                 third, scaled, norms, every):
    count = cotangent.shape[0]

    @pl.when(pl.program_id(0) == 0)
    def _():
        marks = bounds(seg, seg.shape[0], where[0] * count)
        parts = second[...]
        squares = parts[:, 0, :] + jnp.sum(parts[:, 1, :], axis=0, keepdims=True)
        col_norms = jnp.sqrt(jnp.maximum(squares, 0.0) + EPSILON)
        norms[...] = col_norms
        scale = token_scale_of(magnitude[...].astype(F32) / col_norms, marks, count)
        grad = (cotangent[...].astype(F32) * scale).astype(BF16)
        scaled[...] = grad
        spread = dot(up[...], grad, 1, 1)
        back = packed(picked(spread, marks)).astype(BF16)
        every[...] = jnp.concatenate([grad, low[...], back], axis=0)

    third[0, :count] = (keep[0].astype(F32) + got[0].astype(F32)).astype(BF16)
    third[0, count:] = every[...]


def sums_kernel(rank_rows, base_rows, ranks, base):
    ranks[...] = jnp.sum(rank_rows[...].astype(F32), axis=0).astype(BF16)
    base[...] = jnp.sum(base_rows[...].astype(F32), axis=0)


def grads_kernel(where, seg, ranks, got, base, norms, magnitude, cotangent, scaled, up, tokens,
                 fourth, projected, back_wide):
    adapters = seg.shape[0]
    own_rows, count = tokens.shape
    rank = up.shape[0] // adapters
    marks = bounds(seg, adapters, where[0] * count)
    total = ranks[...].astype(F32) + got[...].astype(F32)
    low = widened(unpacked(total[: 2 * rank]), marks)
    back = widened(unpacked(total[2 * rank :]), marks)
    back_wide[...] = back
    hidden = base[...] + dot(low, up[...], 0, 0)
    scale = token_scale_of(magnitude[...].astype(F32) / norms[...], marks, count)
    projected[...] = (hidden * scale).astype(BF16)
    weighted = cotangent[...].astype(F32) * hidden
    at = iota((count, LANES), 0)
    row = iota((rank, LANES // 2), 0)
    down_part = dot(back, tokens[...], 1, 1).astype(BF16)
    up_part = dot(low, scaled[...], 1, 0).astype(BF16)
    pad = -own_rows % LANES
    for a, (lo, hi) in enumerate(marks):
        mag = jnp.sum(jnp.where((at >= lo) & (at < hi), weighted, 0.0), axis=0, keepdims=True)
        halves = jnp.where(row == 0, mag[:, :pad], jnp.where(row == 1, mag[:, pad:], 0.0))
        lines = slice(a * rank, (a + 1) * rank)
        fourth[a] = jnp.concatenate(
            [down_part[lines], halves.astype(BF16), up_part[lines]], axis=1
        )


def total_kernel(arrived, fifth):
    total = jnp.sum(arrived[...].astype(F32), axis=0).astype(BF16)
    fifth[...] = jnp.broadcast_to(total[None], fifth.shape)


def final_kernel(fifth, norms, grad_down, grad_up, grad_magnitude):
    own_rows = grad_down.shape[2]
    pad = -own_rows % LANES
    grad_down[...] = fifth[:, :, :own_rows]
    grad_up[...] = fifth[:, :, own_rows + pad :].astype(F32)
    halves = fifth[:, :, own_rows : own_rows + pad].astype(F32)
    total = jnp.concatenate([halves[:, 0, :], halves[:, 1, :]], axis=1)
    grad_magnitude[...] = total / norms[...]


def tokens_kernel(where, a0, a1, b0, b1, w0, w1, w2, w3, back, down, out, total):
    step = pl.program_id(0)

    @pl.when(step == 0)
    def _():
        total[...] = dot(down[...], back[...], 0, 0)

    left = jnp.concatenate([a0[0], a1[0], b0[0], b1[0]], axis=1)
    right = jnp.concatenate([w0[...], w1[...], w2[...], w3[...]], axis=1)
    total[...] += dot(right, left, 1, 1)

    @pl.when(step == pl.num_programs(0) - 1)
    def _():
        out[...] = total[...].astype(BF16)


def exchange(blocks, axis, groups=None):
    return lax.all_to_all(blocks, axis, 0, 0, tiled=True, axis_index_groups=groups)


def local(tokens, base_weight, adapter_down, adapter_up, magnitude, seg_lengths, cotangent):
    count, own_rows = tokens.shape
    adapters, _, rank = adapter_down.shape
    width = adapter_up.shape[2]
    full = base_weight.shape[1]
    size = full // width
    zs = size // 4
    wide = adapters * rank
    me_dp = lax.axis_index("dp")
    me = lax.axis_index("tensor")
    core, hi = me % 2, me // (2 * zs)
    where = jnp.stack([me_dp, core, hi]).astype(I32)
    core_pairs = [(i, i ^ 1) for i in range(size)]
    hi_pairs = [(i, (i + size // 2) % size) for i in range(size)]
    z_groups = [[h * 2 * zs + z * 2 + c for z in range(zs)] for h in range(2) for c in range(2)]

    turned = tokens.T
    down_rows = jnp.transpose(adapter_down, (0, 2, 1))
    down_flat = down_rows.reshape(wide, own_rows)
    up_own = adapter_up.reshape(wide, width)

    head, keep, give = call(
        first_kernel,
        [shaped(size, HEAD, width), shaped(size // 2, count, width), shaped(size // 2, count, width)],
        scalars=1,
        grid=(size // 4,),
        in_specs=[
            whole(own_rows, count),
            pl.BlockSpec((own_rows, 4 * width), lambda i, s: (0, i)),
            pl.BlockSpec((1, rank, own_rows), lambda i, s: (s[0], 0, 0)),
        ],
        out_specs=[
            pl.BlockSpec((4, HEAD, width), lambda i, s: (i, 0, 0)),
            pl.BlockSpec((2, count, width), lambda i, s: (i, 0, 0)),
            pl.BlockSpec((2, count, width), lambda i, s: (i, 0, 0)),
        ],
        scratch=[pltpu.VMEM((8, width), F32), pltpu.VMEM((count + rank, own_rows), BF16)],
        flops=2 * count * own_rows * full,
        moved=2 * own_rows * full,
    )(where, turned, base_weight, down_rows)
    head = exchange(head, "tensor")
    got = shift(give, core_pairs)
    low = call(
        low_kernel,
        shaped(2 * rank, width),
        scalars=2,
        grid=(1,),
        in_specs=[whole(own_rows, count), whole(wide, own_rows)],
        out_specs=whole(2 * rank, width),
        flops=2 * count * own_rows * wide,
        moved=4 * count * own_rows,
    )(where, seg_lengths, turned, down_flat)

    mine = pl.BlockSpec((2, count, width), lambda i, s: (s[2] * (zs // 2) + i, 0, 0))
    theirs = pl.BlockSpec((2, count, width), lambda i, s: ((1 - s[2]) * (zs // 2) + i, 0, 0))
    out = pl.BlockSpec((2, count, width), lambda i, s: (i, 0, 0))
    keep, give = call(
        halves_kernel,
        [shaped(zs, count, width)] * 2,
        scalars=1,
        grid=(zs // 2,),
        in_specs=[mine, mine, theirs, theirs],
        out_specs=[out, out],
        moved=12 * zs * count * width,
    )(where, keep, got, keep, got)
    got = shift(give, hi_pairs)

    second = call(
        squares_kernel,
        shaped(adapters, 2, width, dtype=F32),
        scalars=1,
        grid=(1,),
        in_specs=[
            whole(size, HEAD, width),
            pl.BlockSpec((1, rank, width), lambda i, s: (s[0], 0, 0)),
        ],
        out_specs=whole(adapters, 2, width),
        moved=2 * size * HEAD * width,
    )(where, head, adapter_up)
    second = exchange(second, "dp")

    rows = 2 * count + 4 * rank
    third, scaled, norms = call(
        scale_kernel,
        [shaped(zs, rows, width), shaped(count, width), shaped(adapters, width, dtype=F32)],
        scalars=2,
        grid=(zs,),
        in_specs=[
            whole(adapters, 2, width),
            whole(adapters, width),
            whole(count, width),
            whole(wide, width),
            whole(2 * rank, width),
            pl.BlockSpec((1, count, width), lambda i, *s: (i, 0, 0)),
            pl.BlockSpec((1, count, width), lambda i, *s: (i, 0, 0)),
        ],
        out_specs=[
            pl.BlockSpec((1, rows, width), lambda i, *s: (i, 0, 0)),
            whole(count, width),
            whole(adapters, width),
        ],
        scratch=[pltpu.VMEM((count + 4 * rank, width), BF16)],
        flops=2 * count * wide * width,
        moved=2 * zs * rows * width,
    )(where, seg_lengths, second, magnitude, cotangent, up_own, low, keep, got)
    third = exchange(third, "tensor", z_groups)

    ranks, base = call(
        sums_kernel,
        [shaped(4 * rank, width), shaped(count, width, dtype=F32)],
        grid=(1,),
        in_specs=[
            pl.BlockSpec((zs, 4 * rank, width), lambda i: (0, 2 * count // (4 * rank), 0)),
            pl.BlockSpec((zs, count, width), lambda i: (0, 0, 0)),
        ],
        out_specs=[whole(4 * rank, width), whole(count, width)],
        moved=2 * zs * count * width,
    )(third, third)
    ranks = (ranks.astype(F32) + shift(ranks, hi_pairs).astype(F32)).astype(BF16)
    other = shift(ranks, core_pairs)
    gather_a = third[:, count : 2 * count]
    gather_b = shift(gather_a, hi_pairs)

    blocks = rank * 40
    fourth, projected, back_wide = call(
        grads_kernel,
        [shaped(adapters, rank, blocks), shaped(count, width), shaped(wide, count)],
        scalars=2,
        grid=(1,),
        in_specs=[
            whole(4 * rank, width),
            whole(4 * rank, width),
            whole(count, width),
            whole(adapters, width),
            whole(adapters, width),
            whole(count, width),
            whole(count, width),
            whole(wide, width),
            whole(own_rows, count),
        ],
        out_specs=[whole(adapters, rank, blocks), whole(count, width), whole(wide, count)],
        flops=2 * count * wide * (own_rows + 2 * width),
        moved=4 * adapters * rank * blocks,
    )(where, seg_lengths, ranks, other, base, norms, magnitude, cotangent, scaled, up_own, turned)
    fourth = exchange(fourth, "dp")
    gather_c = shift(gather_a, core_pairs)
    gather_d = shift(gather_b, core_pairs)

    fifth = call(
        total_kernel,
        shaped(adapters, rank, blocks),
        grid=(1,),
        in_specs=[whole(adapters, rank, blocks)],
        out_specs=whole(adapters, rank, blocks),
        moved=4 * adapters * rank * blocks,
    )(fourth)
    fifth = exchange(fifth, "dp")

    def column(x_bit, c_bit):
        return pl.BlockSpec(
            (own_rows, width),
            lambda i, s: (0, (s[2] ^ x_bit) * (2 * zs) + i * 2 + (s[1] ^ c_bit)),
        )

    block = pl.BlockSpec((1, count, width), lambda i, s: (i, 0, 0))
    grad_tokens = call(
        tokens_kernel,
        shaped(own_rows, count),
        scalars=1,
        grid=(zs,),
        in_specs=[block] * 4
        + [column(0, 0), column(1, 0), column(0, 1), column(1, 1)]
        + [whole(wide, count), whole(wide, own_rows)],
        out_specs=whole(own_rows, count),
        scratch=[pltpu.VMEM((own_rows, count), F32)],
        flops=2 * count * own_rows * (full + wide),
        moved=2 * own_rows * full,
    )(where, gather_a, gather_b, gather_c, gather_d, *[base_weight] * 4, back_wide, down_flat)

    grad_down, grad_up, grad_magnitude = call(
        final_kernel,
        [
            shaped(adapters, rank, own_rows),
            shaped(adapters, rank, width, dtype=F32),
            shaped(adapters, width, dtype=F32),
        ],
        grid=(1,),
        in_specs=[whole(adapters, rank, blocks), whole(adapters, width)],
        out_specs=[
            whole(adapters, rank, own_rows),
            whole(adapters, rank, width),
            whole(adapters, width),
        ],
        moved=4 * adapters * rank * blocks,
    )(fifth, norms)
    return (projected, grad_tokens.T, jnp.transpose(grad_down, (0, 2, 1)), grad_up, grad_magnitude)


def solution(mesh):
    placed = (
        P("dp", "tensor"),
        P("tensor", None),
        P(None, "tensor", None),
        P(None, None, "tensor"),
        P(None, "tensor"),
        P(),
        P("dp", "tensor"),
    )
    return jax.shard_map(
        local,
        mesh=mesh,
        in_specs=placed,
        out_specs=(
            P("dp", "tensor"),
            P("dp", "tensor"),
            P(None, "tensor", None),
            P(None, None, "tensor"),
            P(None, "tensor"),
        ),
        check_vma=False,
    )
```

```python
import jax
import jax.numpy as jnp
from jax import lax
from jax.experimental import pallas as pl
from jax.experimental.pallas import tpu as pltpu
from jax.sharding import PartitionSpec as P


HIGHEST_MODE = lax.Precision.HIGHEST
EPSILON = 1e-06
F32 = jnp.float32
BF16 = jnp.bfloat16
I32 = jnp.int32
LANES = 128
HEAD = 24


def dot(a, b, ca, cb, precision=None):
    return lax.dot_general(
        a, b, (((ca,), (cb,)), ((), ())), precision=precision, preferred_element_type=F32
    )


def iota(shape, dim):
    return lax.broadcasted_iota(I32, shape, dim)


def shaped(*dims, dtype=BF16):
    return jax.ShapeDtypeStruct(dims, dtype)


def bounds(seg, adapters, first_token):
    marks, at = [], -first_token
    for a in range(adapters):
        marks.append((at, at + seg[a]))
        at = at + seg[a]
    return marks


def picked(spread, marks):
    rank = spread.shape[0] // len(marks)
    at = iota((rank, spread.shape[1]), 1)
    total = jnp.zeros((rank, spread.shape[1]), F32)
    for a, (lo, hi) in enumerate(marks):
        total += jnp.where((at >= lo) & (at < hi), spread[a * rank : (a + 1) * rank], 0.0)
    return total


def widened(rank_rows, marks):
    at = iota(rank_rows.shape, 1)
    wide = [jnp.where((at >= lo) & (at < hi), rank_rows, 0.0) for lo, hi in marks]
    return jnp.concatenate(wide, axis=0).astype(BF16)


def packed(rows):
    return jnp.concatenate([rows[:, :LANES], rows[:, LANES:]], axis=0)


def unpacked(rows):
    half = rows.shape[0] // 2
    return jnp.concatenate([rows[:half], rows[half:]], axis=1)


def token_scale_of(col_scale, marks, token_count):
    at = iota((token_count, LANES), 0)
    total = jnp.zeros((token_count, LANES), F32)
    for a, (lo, hi) in enumerate(marks):
        total += jnp.where((at >= lo) & (at < hi), col_scale[a : a + 1], 0.0)
    return total


def shift(block, pairs):
    return lax.ppermute(block, "tensor", pairs)


def call(kernel, out_shape, scalars=0, grid=(), in_specs=None, out_specs=None, scratch=(),
         flops=0, moved=0):
    return pl.pallas_call(
        kernel,
        out_shape=out_shape,
        grid_spec=pltpu.PrefetchScalarGridSpec(
            num_scalar_prefetch=scalars,
            grid=grid,
            in_specs=in_specs,
            out_specs=out_specs,
            scratch_shapes=list(scratch),
        ),
        cost_estimate=pl.CostEstimate(flops=flops, bytes_accessed=moved, transcendentals=0),
        compiler_params=pltpu.CompilerParams(vmem_limit_bytes=16 * 2**20),
    )


def in_hbm(array):
    return pltpu.with_memory_space_constraint(array, pltpu.HBM)


def whole(*dims):
    return pl.BlockSpec(dims, lambda *ids: (0,) * len(dims))


def first_kernel(where, tokens, weight, down, head, keep, give, gram, lines):
    rank = down.shape[1]
    count = tokens.shape[1]

    @pl.when(pl.program_id(0) == 0)
    def _():
        mine = down[0]
        lines[:count] = tokens[...].T
        lines[count:] = mine
        square = dot(mine, mine, 1, 1)
        tile = (iota((rank, LANES), 1) % rank == iota((rank, LANES), 0)).astype(F32)
        spread = dot(square, tile, 1, 0, HIGHEST_MODE)
        rows, cols = iota((rank, LANES), 0), iota((rank, LANES), 1)
        spread = jnp.where(cols // rank == rows % 8, spread, 0.0)
        gram[0:1, :] = jnp.sum(spread[:8], axis=0, keepdims=True)
        gram[1:2, :] = jnp.sum(spread[8:], axis=0, keepdims=True)

    block = weight[...]
    both = dot(lines[...], block, 1, 0)
    share = 32
    pieces = weight.shape[0] // share
    part = weight[pl.ds(pl.multiple_of(jnp.minimum(where[0], pieces - 1) * share, share), share), :]
    part = part.astype(F32)
    squares = jnp.sum(part * part, axis=0, keepdims=True) * (where[0] < pieces).astype(F32)
    row = iota((8, LANES), 0)
    for k in range(4):
        lanes = slice(k * LANES, (k + 1) * LANES)
        tail = jnp.where(
            row == 0,
            squares[:, lanes],
            jnp.where(row == 1, gram[0:1, :], jnp.where(row == 2, gram[1:2, :], 0.0)),
        )
        head[k] = jnp.concatenate([both[count:, lanes], tail], axis=0).astype(BF16)

    base = both[:count].astype(BF16)

    @pl.when(where[1] == 0)
    def _():
        for k in range(2):
            keep[k] = base[:, 2 * k * LANES : (2 * k + 1) * LANES]
            give[k] = base[:, (2 * k + 1) * LANES : (2 * k + 2) * LANES]

    @pl.when(where[1] != 0)
    def _():
        for k in range(2):
            give[k] = base[:, 2 * k * LANES : (2 * k + 1) * LANES]
            keep[k] = base[:, (2 * k + 1) * LANES : (2 * k + 2) * LANES]


def low_kernel(where, seg, tokens, down, low):
    marks = bounds(seg, seg.shape[0], where[0] * tokens.shape[1])
    spread = dot(down[...], tokens[...], 1, 0)
    low[...] = packed(picked(spread, marks)).astype(BF16)


def halves_kernel(where, keep_a, got_a, keep_b, got_b, keep, give):
    keep[...] = (keep_a[...].astype(F32) + got_a[...].astype(F32)).astype(BF16)
    give[...] = (keep_b[...].astype(F32) + got_b[...].astype(F32)).astype(BF16)


def squares_kernel(where, head, up, second):
    rank = up.shape[1]
    total = jnp.sum(head[...].astype(F32), axis=0)
    factor = up[0].astype(F32)
    rows, cols = iota((rank, LANES), 0), iota((rank, LANES), 1)
    spread = jnp.where(rows < 8, total[rank + 1 : rank + 2], total[rank + 2 : rank + 3])
    spread = jnp.where(cols // rank == rows % 8, spread, 0.0)
    tiled = jnp.concatenate([factor] * (LANES // rank), axis=0)
    gram_up = dot(spread, tiled, 1, 0, HIGHEST_MODE)
    mine = jnp.sum(factor * (2.0 * total[:rank] + gram_up), axis=0, keepdims=True)
    both = jnp.concatenate([mine, total[rank : rank + 1]], axis=0)
    second[...] = jnp.broadcast_to(both[None], second.shape)


def lift_kernel(where, keep, got, up, down, near):
    count = keep.shape[0]
    for out, first in ((up, 2), (down, count - 3), (near, count - 1)):
        for i in range(out.shape[0]):
            at = (where[3] + first + i) % count
            out[i] = (keep[at].astype(F32) + got[at].astype(F32)).astype(BF16)


def near_kernel(near, up, down, before, after, own):
    before[...] = (near[0].astype(F32) + up[0].astype(F32)).astype(BF16)
    after[...] = (near[2].astype(F32) + up[2].astype(F32) + down[1].astype(F32)).astype(BF16)
    own[...] = near[1].astype(F32) + up[1].astype(F32) + down[0].astype(F32)


def trio_kernel(before, own, after, trio, pair):
    trio[0] = before[...]
    trio[1] = own[...]
    trio[2] = after[...]
    pair[0] = before[...]
    pair[1] = own[...]


def scale_kernel(where, seg, second, magnitude, cotangent, up, low, third, scaled, norms):
    count = cotangent.shape[0]
    marks = bounds(seg, seg.shape[0], where[0] * count)
    parts = second[...]
    squares = parts[:, 0, :] + jnp.sum(parts[:, 1, :], axis=0, keepdims=True)
    col_norms = jnp.sqrt(jnp.maximum(squares, 0.0) + EPSILON)
    norms[...] = col_norms
    scale = token_scale_of(magnitude[...].astype(F32) / col_norms, marks, count)
    grad = (cotangent[...].astype(F32) * scale).astype(BF16)
    scaled[...] = grad
    back = packed(picked(dot(up[...], grad, 1, 1), marks)).astype(BF16)
    every = jnp.concatenate([low[...], back], axis=0)
    third[...] = jnp.broadcast_to(every[None], third.shape)


def sums_kernel(rank_rows, ranks):
    ranks[...] = jnp.sum(rank_rows[...].astype(F32), axis=0).astype(BF16)


def grads_kernel(where, seg, ranks, got, base, base_a, base_b, norms, magnitude, cotangent, scaled, up, tokens,
                 fourth, projected, back_wide):
    adapters = seg.shape[0]
    own_rows, count = tokens.shape
    rank = up.shape[0] // adapters
    marks = bounds(seg, adapters, where[0] * count)
    total = ranks[...].astype(F32) + got[...].astype(F32)
    low = widened(unpacked(total[: 2 * rank]), marks)
    back = widened(unpacked(total[2 * rank :]), marks)
    back_wide[...] = back
    hidden = base[...] + base_a[...].astype(F32) + base_b[...].astype(F32)
    hidden = hidden + dot(low, up[...], 0, 0)
    scale = token_scale_of(magnitude[...].astype(F32) / norms[...], marks, count)
    projected[...] = (hidden * scale).astype(BF16)
    weighted = cotangent[...].astype(F32) * hidden
    at = iota((count, LANES), 0)
    row = iota((rank, LANES // 2), 0)
    down_part = dot(back, tokens[...], 1, 1).astype(BF16)
    up_part = dot(low, scaled[...], 1, 0).astype(BF16)
    pad = -own_rows % LANES
    for a, (lo, hi) in enumerate(marks):
        mag = jnp.sum(jnp.where((at >= lo) & (at < hi), weighted, 0.0), axis=0, keepdims=True)
        halves = jnp.where(row == 0, mag[:, :pad], jnp.where(row == 1, mag[:, pad:], 0.0))
        lines = slice(a * rank, (a + 1) * rank)
        fourth[a] = jnp.concatenate(
            [down_part[lines], halves.astype(BF16), up_part[lines]], axis=1
        )


def total_kernel(arrived, fifth):
    total = jnp.sum(arrived[...].astype(F32), axis=0).astype(BF16)
    fifth[...] = jnp.broadcast_to(total[None], fifth.shape)


def final_kernel(fifth, norms, grad_down, grad_up, grad_magnitude):
    own_rows = grad_down.shape[2]
    pad = -own_rows % LANES
    grad_down[...] = fifth[:, :, :own_rows]
    grad_up[...] = fifth[:, :, own_rows + pad :].astype(F32)
    halves = fifth[:, :, own_rows : own_rows + pad].astype(F32)
    total = jnp.concatenate([halves[:, 0, :], halves[:, 1, :]], axis=1)
    grad_magnitude[...] = total / norms[...]


def tokens_kernel(where, a0, a1, b0, b1, w0, w1, w2, w3, back, down, out, total):
    step = pl.program_id(0)

    @pl.when(step == 0)
    def _():
        total[...] = dot(down[...], back[...], 0, 0)

    left = jnp.concatenate([a0[0], a1[0], b0[0], b1[0]], axis=1)
    right = jnp.concatenate([w0[...], w1[...], w2[...], w3[...]], axis=1)
    total[...] += dot(right, left, 1, 1)

    @pl.when(step == pl.num_programs(0) - 1)
    def _():
        out[...] = total[...].astype(BF16)


def exchange(blocks, axis, groups=None):
    return lax.all_to_all(blocks, axis, 0, 0, tiled=True, axis_index_groups=groups)


def local(tokens, base_weight, adapter_down, adapter_up, magnitude, seg_lengths, cotangent):
    count, own_rows = tokens.shape
    adapters, _, rank = adapter_down.shape
    width = adapter_up.shape[2]
    full = base_weight.shape[1]
    size = full // width
    zs = size // 4
    wide = adapters * rank
    me_dp = lax.axis_index("dp")
    me = lax.axis_index("tensor")
    core, hi = me % 2, me // (2 * zs)
    z = (me // 2) % zs
    where = jnp.stack([me_dp, core, hi, z]).astype(I32)
    core_pairs = [(i, i ^ 1) for i in range(size)]
    hi_pairs = [(i, (i + size // 2) % size) for i in range(size)]
    z_groups = [[h * 2 * zs + z * 2 + c for z in range(zs)] for h in range(2) for c in range(2)]

    turned = tokens.T
    down_rows = jnp.transpose(adapter_down, (0, 2, 1))
    down_flat = down_rows.reshape(wide, own_rows)
    up_own = adapter_up.reshape(wide, width)

    head, keep, give = call(
        first_kernel,
        [shaped(size, HEAD, width), shaped(size // 2, count, width), shaped(size // 2, count, width)],
        scalars=1,
        grid=(size // 4,),
        in_specs=[
            whole(own_rows, count),
            pl.BlockSpec((own_rows, 4 * width), lambda i, s: (0, i)),
            pl.BlockSpec((1, rank, own_rows), lambda i, s: (s[0], 0, 0)),
        ],
        out_specs=[
            pl.BlockSpec((4, HEAD, width), lambda i, s: (i, 0, 0)),
            pl.BlockSpec((2, count, width), lambda i, s: (i, 0, 0)),
            pl.BlockSpec((2, count, width), lambda i, s: (i, 0, 0)),
        ],
        scratch=[pltpu.VMEM((8, width), F32), pltpu.VMEM((count + rank, own_rows), BF16)],
        flops=2 * count * own_rows * full,
        moved=2 * own_rows * full,
    )(where, in_hbm(turned), in_hbm(base_weight), in_hbm(down_rows))
    head = exchange(head, "tensor")
    got = shift(give, core_pairs)
    low = call(
        low_kernel,
        shaped(2 * rank, width),
        scalars=2,
        grid=(1,),
        in_specs=[whole(own_rows, count), whole(wide, own_rows)],
        out_specs=whole(2 * rank, width),
        flops=2 * count * own_rows * wide,
        moved=4 * count * own_rows,
    )(where, seg_lengths, turned, down_flat)

    mine = pl.BlockSpec((2, count, width), lambda i, s: (s[2] * (zs // 2) + i, 0, 0))
    theirs = pl.BlockSpec((2, count, width), lambda i, s: ((1 - s[2]) * (zs // 2) + i, 0, 0))
    out = pl.BlockSpec((2, count, width), lambda i, s: (i, 0, 0))
    keep, give = call(
        halves_kernel,
        [shaped(zs, count, width)] * 2,
        scalars=1,
        grid=(zs // 2,),
        in_specs=[mine, mine, theirs, theirs],
        out_specs=[out, out],
        moved=12 * zs * count * width,
    )(where, keep, got, keep, got)
    got = shift(give, hi_pairs)

    def along_z(step):
        return [
            (h * 2 * zs + a * 2 + c, h * 2 * zs + (a + step) % zs * 2 + c)
            for h in range(2)
            for a in range(zs)
            for c in range(2)
        ]

    second = call(
        squares_kernel,
        shaped(adapters, 2, width, dtype=F32),
        scalars=1,
        grid=(1,),
        in_specs=[
            whole(size, HEAD, width),
            pl.BlockSpec((1, rank, width), lambda i, s: (s[0], 0, 0)),
        ],
        out_specs=whole(adapters, 2, width),
        moved=2 * size * HEAD * width,
    )(where, head, adapter_up)
    second = exchange(second, "dp")

    up3, down2, near = call(
        lift_kernel,
        [shaped(n, count, width) for n in (3, 2, 3)],
        scalars=1,
        grid=(1,),
        in_specs=[whole(zs, count, width)] * 2,
        out_specs=[whole(n, count, width) for n in (3, 2, 3)],
        moved=6 * zs * count * width,
    )(where, keep, got)
    up3 = shift(up3, along_z(3))
    down2 = shift(down2, along_z(-3))

    third, scaled, norms = call(
        scale_kernel,
        [shaped(zs, 4 * rank, width), shaped(count, width), shaped(adapters, width, dtype=F32)],
        scalars=2,
        grid=(1,),
        in_specs=[
            whole(adapters, 2, width),
            whole(adapters, width),
            whole(count, width),
            whole(wide, width),
            whole(2 * rank, width),
        ],
        out_specs=[whole(zs, 4 * rank, width), whole(count, width), whole(adapters, width)],
        flops=2 * count * wide * width,
        moved=8 * count * width,
    )(where, seg_lengths, second, magnitude, cotangent, up_own, low)
    third = exchange(third, "tensor", z_groups)
    from_below = shift(scaled, along_z(1))
    from_above = shift(scaled, along_z(-1))

    before, after, base = call(
        near_kernel,
        [shaped(count, width), shaped(count, width), shaped(count, width, dtype=F32)],
        grid=(1,),
        in_specs=[whole(3, count, width), whole(3, count, width), whole(2, count, width)],
        out_specs=[whole(count, width)] * 3,
        moved=24 * count * width,
    )(near, up3, down2)
    base_a = shift(before, along_z(-1))
    base_b = shift(after, along_z(1))

    ranks = call(
        sums_kernel,
        shaped(4 * rank, width),
        grid=(1,),
        in_specs=[whole(zs, 4 * rank, width)],
        out_specs=whole(4 * rank, width),
        moved=2 * zs * 4 * rank * width,
    )(third)
    ranks = (ranks.astype(F32) + shift(ranks, hi_pairs).astype(F32)).astype(BF16)
    other = shift(ranks, core_pairs)
    trio, pair = call(
        trio_kernel,
        [shaped(3, count, width), shaped(2, count, width)],
        grid=(1,),
        in_specs=[whole(count, width)] * 3,
        out_specs=[whole(3, count, width), whole(2, count, width)],
        moved=16 * count * width,
    )(from_below, scaled, from_above)
    far_up = shift(trio, along_z(3))
    far_down = shift(pair, along_z(-3))
    gather_a = jnp.concatenate([trio, far_up, far_down], axis=0)
    gather_b = shift(gather_a, hi_pairs)

    blocks = rank * 40
    fourth, projected, back_wide = call(
        grads_kernel,
        [shaped(adapters, rank, blocks), shaped(count, width), shaped(wide, count)],
        scalars=2,
        grid=(1,),
        in_specs=[
            whole(4 * rank, width),
            whole(4 * rank, width),
            whole(count, width),
            whole(count, width),
            whole(count, width),
            whole(adapters, width),
            whole(adapters, width),
            whole(count, width),
            whole(count, width),
            whole(wide, width),
            whole(own_rows, count),
        ],
        out_specs=[whole(adapters, rank, blocks), whole(count, width), whole(wide, count)],
        flops=2 * count * wide * (own_rows + 2 * width),
        moved=4 * adapters * rank * blocks,
    )(where, seg_lengths, ranks, other, base, base_a, base_b, norms, magnitude, cotangent, scaled, up_own, turned)
    fourth = exchange(fourth, "dp")
    gather_c = shift(gather_a, core_pairs)
    gather_d = shift(gather_b, core_pairs)

    fifth = call(
        total_kernel,
        shaped(adapters, rank, blocks),
        grid=(1,),
        in_specs=[whole(adapters, rank, blocks)],
        out_specs=whole(adapters, rank, blocks),
        moved=4 * adapters * rank * blocks,
    )(fourth)
    fifth = exchange(fifth, "dp")

    def column(x_bit, c_bit):
        def at(i, s):
            off = jnp.where(i < 3, i - 1, jnp.where(i < 6, i - 7, i - 4))
            block = (s[3] + off + zs) % zs
            return (0, (s[2] ^ x_bit) * (2 * zs) + block * 2 + (s[1] ^ c_bit))

        return pl.BlockSpec((own_rows, width), at)

    block = pl.BlockSpec((1, count, width), lambda i, s: (i, 0, 0))
    grad_tokens = call(
        tokens_kernel,
        shaped(own_rows, count),
        scalars=1,
        grid=(zs,),
        in_specs=[block] * 4
        + [column(0, 0), column(1, 0), column(0, 1), column(1, 1)]
        + [whole(wide, count), whole(wide, own_rows)],
        out_specs=whole(own_rows, count),
        scratch=[pltpu.VMEM((own_rows, count), F32)],
        flops=2 * count * own_rows * (full + wide),
        moved=2 * own_rows * full,
    )(where, gather_a, gather_b, gather_c, gather_d, *[in_hbm(base_weight)] * 4, back_wide, down_flat)

    grad_down, grad_up, grad_magnitude = call(
        final_kernel,
        [
            shaped(adapters, rank, own_rows),
            shaped(adapters, rank, width, dtype=F32),
            shaped(adapters, width, dtype=F32),
        ],
        grid=(1,),
        in_specs=[whole(adapters, rank, blocks), whole(adapters, width)],
        out_specs=[
            whole(adapters, rank, own_rows),
            whole(adapters, rank, width),
            whole(adapters, width),
        ],
        moved=4 * adapters * rank * blocks,
    )(fifth, norms)
    return (projected, grad_tokens.T, jnp.transpose(grad_down, (0, 2, 1)), grad_up, grad_magnitude)


def solution(mesh):
    placed = (
        P("dp", "tensor"),
        P("tensor", None),
        P(None, "tensor", None),
        P(None, None, "tensor"),
        P(None, "tensor"),
        P(),
        P("dp", "tensor"),
    )
    return jax.shard_map(
        local,
        mesh=mesh,
        in_specs=placed,
        out_specs=(
            P("dp", "tensor"),
            P("dp", "tensor"),
            P(None, "tensor", None),
            P(None, None, "tensor"),
            P(None, "tensor"),
        ),
        check_vma=False,
    )
```

```python
import jax
import jax.numpy as jnp
from jax import lax
from jax.experimental import pallas as pl
from jax.experimental.pallas import tpu as pltpu
from jax.sharding import PartitionSpec as P


HIGHEST_MODE = lax.Precision.HIGHEST
EPSILON = 1e-06
F32 = jnp.float32
BF16 = jnp.bfloat16
I32 = jnp.int32
LANES = 128
HEAD = 24


def dot(a, b, ca, cb, precision=None):
    return lax.dot_general(
        a, b, (((ca,), (cb,)), ((), ())), precision=precision, preferred_element_type=F32
    )


def iota(shape, dim):
    return lax.broadcasted_iota(I32, shape, dim)


def shaped(*dims, dtype=BF16):
    return jax.ShapeDtypeStruct(dims, dtype)


def bounds(seg, adapters, first_token):
    marks, at = [], -first_token
    for a in range(adapters):
        marks.append((at, at + seg[a]))
        at = at + seg[a]
    return marks


def picked(spread, marks):
    rank = spread.shape[0] // len(marks)
    at = iota((rank, spread.shape[1]), 1)
    total = jnp.zeros((rank, spread.shape[1]), F32)
    for a, (lo, hi) in enumerate(marks):
        total += jnp.where((at >= lo) & (at < hi), spread[a * rank : (a + 1) * rank], 0.0)
    return total


def widened(rank_rows, marks):
    at = iota(rank_rows.shape, 1)
    wide = [jnp.where((at >= lo) & (at < hi), rank_rows, 0.0) for lo, hi in marks]
    return jnp.concatenate(wide, axis=0).astype(BF16)


def packed(rows):
    return jnp.concatenate([rows[:, :LANES], rows[:, LANES:]], axis=0)


def unpacked(rows):
    half = rows.shape[0] // 2
    return jnp.concatenate([rows[:half], rows[half:]], axis=1)


def token_scale_of(col_scale, marks, token_count):
    at = iota((token_count, LANES), 0)
    total = jnp.zeros((token_count, LANES), F32)
    for a, (lo, hi) in enumerate(marks):
        total += jnp.where((at >= lo) & (at < hi), col_scale[a : a + 1], 0.0)
    return total


def shift(block, pairs):
    return lax.ppermute(block, "tensor", pairs)


def call(kernel, out_shape, scalars=0, grid=(), in_specs=None, out_specs=None, scratch=(),
         flops=0, moved=0):
    return pl.pallas_call(
        kernel,
        out_shape=out_shape,
        grid_spec=pltpu.PrefetchScalarGridSpec(
            num_scalar_prefetch=scalars,
            grid=grid,
            in_specs=in_specs,
            out_specs=out_specs,
            scratch_shapes=list(scratch),
        ),
        cost_estimate=pl.CostEstimate(flops=flops, bytes_accessed=moved, transcendentals=0),
        compiler_params=pltpu.CompilerParams(vmem_limit_bytes=16 * 2**20),
    )


def in_hbm(array):
    return pltpu.with_memory_space_constraint(array, pltpu.HBM)


def whole(*dims):
    return pl.BlockSpec(dims, lambda *ids: (0,) * len(dims))


def first_kernel(where, tokens, weight, down, head, keep, give, gram, lines):
    rank = down.shape[1]
    count = tokens.shape[1]

    @pl.when(pl.program_id(0) == 0)
    def _():
        mine = down[0]
        lines[:count] = tokens[...].T
        lines[count:] = mine
        square = dot(mine, mine, 1, 1)
        tile = (iota((rank, LANES), 1) % rank == iota((rank, LANES), 0)).astype(F32)
        spread = dot(square, tile, 1, 0, HIGHEST_MODE)
        rows, cols = iota((rank, LANES), 0), iota((rank, LANES), 1)
        spread = jnp.where(cols // rank == rows % 8, spread, 0.0)
        gram[0:1, :] = jnp.sum(spread[:8], axis=0, keepdims=True)
        gram[1:2, :] = jnp.sum(spread[8:], axis=0, keepdims=True)

    share = 32
    pieces = weight.shape[0] // share
    part = weight[pl.ds(pl.multiple_of(jnp.minimum(where[0], pieces - 1) * share, share), share), :]
    part = part.astype(F32)
    squares = jnp.sum(part * part, axis=0, keepdims=True) * (where[0] < pieces).astype(F32)
    row = iota((8, LANES), 0)
    for block in range(0, weight.shape[1], 4 * LANES):
        both = dot(lines[...], weight[:, block : block + 4 * LANES], 1, 0)
        base = both[:count].astype(BF16)
        for k in range(4):
            lanes = slice(k * LANES, (k + 1) * LANES)
            tail = jnp.where(
                row == 0,
                squares[:, block + k * LANES : block + (k + 1) * LANES],
                jnp.where(row == 1, gram[0:1, :], jnp.where(row == 2, gram[1:2, :], 0.0)),
            )
            head[block // LANES + k] = jnp.concatenate([both[count:, lanes], tail], 0).astype(BF16)
        for k in range(2):
            at = block // LANES // 2 + k
            even = base[:, 2 * k * LANES : (2 * k + 1) * LANES]
            odd = base[:, (2 * k + 1) * LANES : (2 * k + 2) * LANES]

            @pl.when(where[1] == 0)
            def _():
                keep[at] = even
                give[at] = odd

            @pl.when(where[1] != 0)
            def _():
                keep[at] = odd
                give[at] = even


def low_kernel(where, seg, tokens, down, low):
    marks = bounds(seg, seg.shape[0], where[0] * tokens.shape[1])
    spread = dot(down[...], tokens[...], 1, 0)
    low[...] = packed(picked(spread, marks)).astype(BF16)


def halves_kernel(where, keep_a, got_a, keep_b, got_b, keep, give):
    keep[...] = (keep_a[...].astype(F32) + got_a[...].astype(F32)).astype(BF16)
    give[...] = (keep_b[...].astype(F32) + got_b[...].astype(F32)).astype(BF16)


def squares_kernel(where, head, up, second):
    rank = up.shape[1]
    total = jnp.sum(head[...].astype(F32), axis=0)
    factor = up[0].astype(F32)
    rows, cols = iota((rank, LANES), 0), iota((rank, LANES), 1)
    spread = jnp.where(rows < 8, total[rank + 1 : rank + 2], total[rank + 2 : rank + 3])
    spread = jnp.where(cols // rank == rows % 8, spread, 0.0)
    tiled = jnp.concatenate([factor] * (LANES // rank), axis=0)
    gram_up = dot(spread, tiled, 1, 0, HIGHEST_MODE)
    mine = jnp.sum(factor * (2.0 * total[:rank] + gram_up), axis=0, keepdims=True)
    both = jnp.concatenate([mine, total[rank : rank + 1]], axis=0)
    second[...] = jnp.broadcast_to(both[None], second.shape)


def lift_kernel(where, keep, got, up, down, near):
    count = keep.shape[0]
    for out, first in ((up, 2), (down, count - 3), (near, count - 1)):
        for i in range(out.shape[0]):
            at = (where[3] + first + i) % count
            out[i] = (keep[at].astype(F32) + got[at].astype(F32)).astype(BF16)


def near_kernel(near, up, down, scaled, before, after, own):
    before[0] = (near[0].astype(F32) + up[0].astype(F32)).astype(BF16)
    before[1] = scaled[...]
    after[0] = (near[2].astype(F32) + up[2].astype(F32) + down[1].astype(F32)).astype(BF16)
    after[1] = scaled[...]
    own[...] = near[1].astype(F32) + up[1].astype(F32) + down[0].astype(F32)


def trio_kernel(before, own, after, trio, pair):
    trio[0] = before[0]
    trio[1] = own[...]
    trio[2] = after[0]
    pair[0] = before[0]
    pair[1] = own[...]


def join_kernel(near, up, down, out):
    out[:3] = near[...]
    out[3:6] = up[...]
    out[6:] = down[...]


def scale_kernel(where, seg, second, magnitude, cotangent, up, low, third, scaled, norms):
    count = cotangent.shape[0]
    marks = bounds(seg, seg.shape[0], where[0] * count)
    parts = second[...]
    squares = parts[:, 0, :] + jnp.sum(parts[:, 1, :], axis=0, keepdims=True)
    col_norms = jnp.sqrt(jnp.maximum(squares, 0.0) + EPSILON)
    norms[...] = col_norms
    scale = token_scale_of(magnitude[...].astype(F32) / col_norms, marks, count)
    grad = (cotangent[...].astype(F32) * scale).astype(BF16)
    scaled[...] = grad
    back = packed(picked(dot(up[...], grad, 1, 1), marks)).astype(BF16)
    every = jnp.concatenate([low[...], back], axis=0)
    third[...] = jnp.broadcast_to(every[None], third.shape)


def grads_kernel(where, seg, ranks, base, base_a, base_b, norms, magnitude, cotangent, scaled, up, tokens,
                 fourth, projected, back_wide):
    adapters = seg.shape[0]
    own_rows, count = tokens.shape
    rank = up.shape[0] // adapters
    marks = bounds(seg, adapters, where[0] * count)
    total = jnp.sum(ranks[...].astype(F32), axis=0)
    low = widened(unpacked(total[: 2 * rank]), marks)
    back = widened(unpacked(total[2 * rank :]), marks)
    back_wide[...] = back
    hidden = base[...] + base_a[0].astype(F32) + base_b[0].astype(F32)
    hidden = hidden + dot(low, up[...], 0, 0)
    scale = token_scale_of(magnitude[...].astype(F32) / norms[...], marks, count)
    projected[...] = (hidden * scale).astype(BF16)
    weighted = cotangent[...].astype(F32) * hidden
    at = iota((count, LANES), 0)
    row = iota((rank, LANES // 2), 0)
    down_part = dot(back, tokens[...], 1, 1).astype(BF16)
    up_part = dot(low, scaled[...], 1, 0).astype(BF16)
    pad = -own_rows % LANES
    for a, (lo, hi) in enumerate(marks):
        mag = jnp.sum(jnp.where((at >= lo) & (at < hi), weighted, 0.0), axis=0, keepdims=True)
        halves = jnp.where(row == 0, mag[:, :pad], jnp.where(row == 1, mag[:, pad:], 0.0))
        lines = slice(a * rank, (a + 1) * rank)
        fourth[a] = jnp.concatenate(
            [down_part[lines], halves.astype(BF16), up_part[lines]], axis=1
        )


def total_kernel(arrived, fifth):
    total = jnp.sum(arrived[...].astype(F32), axis=0).astype(BF16)
    fifth[...] = jnp.broadcast_to(total[None], fifth.shape)


def final_kernel(fifth, norms, grad_down, grad_up, grad_magnitude):
    own_rows = grad_down.shape[2]
    pad = -own_rows % LANES
    grad_down[...] = fifth[:, :, :own_rows]
    grad_up[...] = fifth[:, :, own_rows + pad :].astype(F32)
    halves = fifth[:, :, own_rows : own_rows + pad].astype(F32)
    total = jnp.concatenate([halves[:, 0, :], halves[:, 1, :]], axis=1)
    grad_magnitude[...] = total / norms[...]


def tokens_kernel(where, a0, a1, b0, b1, *rest):
    *columns, back, down, out, total = rest
    step = pl.program_id(0)

    @pl.when(step == 0)
    def _():
        total[...] = dot(down[...], back[...], 0, 0)

    left = [block[i] for i in range(a0.shape[0]) for block in (a0, a1, b0, b1)]
    right = [column[...] for column in columns]
    total[...] += dot(jnp.concatenate(right, axis=1), jnp.concatenate(left, axis=1), 1, 1)

    @pl.when(step == pl.num_programs(0) - 1)
    def _():
        out[...] = total[...].astype(BF16)


def exchange(blocks, axis, groups=None):
    return lax.all_to_all(blocks, axis, 0, 0, tiled=True, axis_index_groups=groups)


def local(tokens, base_weight, adapter_down, adapter_up, magnitude, seg_lengths, cotangent):
    count, own_rows = tokens.shape
    adapters, _, rank = adapter_down.shape
    width = adapter_up.shape[2]
    full = base_weight.shape[1]
    size = full // width
    zs = size // 4
    wide = adapters * rank
    me_dp = lax.axis_index("dp")
    me = lax.axis_index("tensor")
    core, hi = me % 2, me // (2 * zs)
    z = (me // 2) % zs
    where = jnp.stack([me_dp, core, hi, z]).astype(I32)
    core_pairs = [(i, i ^ 1) for i in range(size)]
    hi_pairs = [(i, (i + size // 2) % size) for i in range(size)]

    turned = tokens.T
    down_rows = jnp.transpose(adapter_down, (0, 2, 1))
    down_flat = down_rows.reshape(wide, own_rows)
    up_own = adapter_up.reshape(wide, width)

    head, keep, give = call(
        first_kernel,
        [shaped(size, HEAD, width), shaped(size // 2, count, width), shaped(size // 2, count, width)],
        scalars=1,
        grid=(2,),
        in_specs=[
            whole(own_rows, count),
            pl.BlockSpec((own_rows, full // 2), lambda i, s: (0, i)),
            pl.BlockSpec((1, rank, own_rows), lambda i, s: (s[0], 0, 0)),
        ],
        out_specs=[
            pl.BlockSpec((size // 2, HEAD, width), lambda i, s: (i, 0, 0)),
            pl.BlockSpec((size // 4, count, width), lambda i, s: (i, 0, 0)),
            pl.BlockSpec((size // 4, count, width), lambda i, s: (i, 0, 0)),
        ],
        scratch=[pltpu.VMEM((8, width), F32), pltpu.VMEM((count + rank, own_rows), BF16)],
        flops=2 * count * own_rows * full,
        moved=2 * own_rows * full,
    )(where, in_hbm(turned), in_hbm(base_weight), in_hbm(down_rows))
    head = exchange(head, "tensor")
    got = shift(give, core_pairs)
    low = call(
        low_kernel,
        shaped(2 * rank, width),
        scalars=2,
        grid=(1,),
        in_specs=[whole(own_rows, count), whole(wide, own_rows)],
        out_specs=whole(2 * rank, width),
        flops=2 * count * own_rows * wide,
        moved=4 * count * own_rows,
    )(where, seg_lengths, turned, down_flat)

    mine = pl.BlockSpec((2, count, width), lambda i, s: (s[2] * (zs // 2) + i, 0, 0))
    theirs = pl.BlockSpec((2, count, width), lambda i, s: ((1 - s[2]) * (zs // 2) + i, 0, 0))
    out = pl.BlockSpec((2, count, width), lambda i, s: (i, 0, 0))
    keep, give = call(
        halves_kernel,
        [shaped(zs, count, width)] * 2,
        scalars=1,
        grid=(zs // 2,),
        in_specs=[mine, mine, theirs, theirs],
        out_specs=[out, out],
        moved=12 * zs * count * width,
    )(where, keep, got, keep, got)
    got = shift(give, hi_pairs)

    def along_z(step):
        return [
            (h * 2 * zs + a * 2 + c, h * 2 * zs + (a + step) % zs * 2 + c)
            for h in range(2)
            for a in range(zs)
            for c in range(2)
        ]

    second = call(
        squares_kernel,
        shaped(adapters, 2, width, dtype=F32),
        scalars=1,
        grid=(1,),
        in_specs=[
            whole(size, HEAD, width),
            pl.BlockSpec((1, rank, width), lambda i, s: (s[0], 0, 0)),
        ],
        out_specs=whole(adapters, 2, width),
        moved=2 * size * HEAD * width,
    )(where, head, adapter_up)
    second = exchange(second, "dp")

    up3, down2, near = call(
        lift_kernel,
        [shaped(n, count, width) for n in (3, 2, 3)],
        scalars=1,
        grid=(1,),
        in_specs=[whole(zs, count, width)] * 2,
        out_specs=[whole(n, count, width) for n in (3, 2, 3)],
        moved=6 * zs * count * width,
    )(where, keep, got)
    up3 = shift(up3, along_z(3))
    down2 = shift(down2, along_z(-3))

    third, scaled, norms = call(
        scale_kernel,
        [shaped(size, 4 * rank, width), shaped(count, width), shaped(adapters, width, dtype=F32)],
        scalars=2,
        grid=(1,),
        in_specs=[
            whole(adapters, 2, width),
            whole(adapters, width),
            whole(count, width),
            whole(wide, width),
            whole(2 * rank, width),
        ],
        out_specs=[whole(size, 4 * rank, width), whole(count, width), whole(adapters, width)],
        flops=2 * count * wide * width,
        moved=8 * count * width,
    )(where, seg_lengths, second, magnitude, cotangent, up_own, low)
    third = exchange(third, "tensor")

    before, after, base = call(
        near_kernel,
        [shaped(2, count, width), shaped(2, count, width), shaped(count, width, dtype=F32)],
        grid=(1,),
        in_specs=[whole(n, count, width) for n in (3, 3, 2)] + [whole(count, width)],
        out_specs=[whole(2, count, width), whole(2, count, width), whole(count, width)],
        moved=24 * count * width,
    )(near, up3, down2, scaled)
    from_above = shift(before, along_z(-1))
    from_below = shift(after, along_z(1))

    second_block = pl.BlockSpec((1, count, width), lambda i: (1, 0, 0))
    trio, pair = call(
        trio_kernel,
        [shaped(3, count, width), shaped(2, count, width)],
        grid=(1,),
        in_specs=[second_block, whole(count, width), second_block],
        out_specs=[whole(3, count, width), whole(2, count, width)],
        moved=16 * count * width,
    )(from_below, scaled, from_above)
    far_up = shift(trio, along_z(3))
    far_down = shift(pair, along_z(-3))
    gather_a = call(
        join_kernel,
        shaped(zs, count, width),
        grid=(1,),
        in_specs=[whole(n, count, width) for n in (3, 3, 2)],
        out_specs=whole(zs, count, width),
        moved=4 * zs * count * width,
    )(trio, far_up, far_down)
    gather_b = shift(gather_a, hi_pairs)

    first_block = pl.BlockSpec((1, count, width), lambda i, *s: (0, 0, 0))
    blocks = rank * 40
    fourth, projected, back_wide = call(
        grads_kernel,
        [shaped(adapters, rank, blocks), shaped(count, width), shaped(wide, count)],
        scalars=2,
        grid=(1,),
        in_specs=[
            whole(size, 4 * rank, width),
            whole(count, width),
            first_block,
            first_block,
            whole(adapters, width),
            whole(adapters, width),
            whole(count, width),
            whole(count, width),
            whole(wide, width),
            whole(own_rows, count),
        ],
        out_specs=[whole(adapters, rank, blocks), whole(count, width), whole(wide, count)],
        flops=2 * count * wide * (own_rows + 2 * width),
        moved=4 * adapters * rank * blocks,
    )(where, seg_lengths, third, base, from_below, from_above, norms, magnitude, cotangent, scaled, up_own, turned)
    fourth = exchange(fourth, "dp")
    gather_c = shift(gather_a, core_pairs)
    gather_d = shift(gather_b, core_pairs)

    fifth = call(
        total_kernel,
        shaped(adapters, rank, blocks),
        grid=(1,),
        in_specs=[whole(adapters, rank, blocks)],
        out_specs=whole(adapters, rank, blocks),
        moved=4 * adapters * rank * blocks,
    )(fourth)
    fifth = exchange(fifth, "dp")

    per = 4

    def column(k, x_bit, c_bit):
        def at(i, s):
            slot = i * per + k
            off = jnp.where(slot < 3, slot - 1, jnp.where(slot < 6, slot - 7, slot - 4))
            block = (s[3] + off + zs) % zs
            return (0, (s[2] ^ x_bit) * (2 * zs) + block * 2 + (s[1] ^ c_bit))

        return pl.BlockSpec((own_rows, width), at)

    columns = [
        column(k, x, c) for k in range(per) for x, c in ((0, 0), (1, 0), (0, 1), (1, 1))
    ]
    block = pl.BlockSpec((per, count, width), lambda i, s: (i, 0, 0))
    grad_tokens = call(
        tokens_kernel,
        shaped(own_rows, count),
        scalars=1,
        grid=(zs // per,),
        in_specs=[block] * 4
        + columns
        + [whole(wide, count), whole(wide, own_rows)],
        out_specs=whole(own_rows, count),
        scratch=[pltpu.VMEM((own_rows, count), F32)],
        flops=2 * count * own_rows * (full + wide),
        moved=2 * own_rows * full,
    )(where, gather_a, gather_b, gather_c, gather_d, *[in_hbm(base_weight)] * (4 * per), back_wide, down_flat)

    grad_down, grad_up, grad_magnitude = call(
        final_kernel,
        [
            shaped(adapters, rank, own_rows),
            shaped(adapters, rank, width, dtype=F32),
            shaped(adapters, width, dtype=F32),
        ],
        grid=(1,),
        in_specs=[whole(adapters, rank, blocks), whole(adapters, width)],
        out_specs=[
            whole(adapters, rank, own_rows),
            whole(adapters, rank, width),
            whole(adapters, width),
        ],
        moved=4 * adapters * rank * blocks,
    )(fifth, norms)
    return (projected, grad_tokens.T, jnp.transpose(grad_down, (0, 2, 1)), grad_up, grad_magnitude)


def solution(mesh):
    placed = (
        P("dp", "tensor"),
        P("tensor", None),
        P(None, "tensor", None),
        P(None, None, "tensor"),
        P(None, "tensor"),
        P(),
        P("dp", "tensor"),
    )
    return jax.shard_map(
        local,
        mesh=mesh,
        in_specs=placed,
        out_specs=(
            P("dp", "tensor"),
            P("dp", "tensor"),
            P(None, "tensor", None),
            P(None, None, "tensor"),
            P(None, "tensor"),
        ),
        check_vma=False,
    )
```

```python
import jax
import jax.numpy as jnp
from jax import lax
from jax.experimental import pallas as pl
from jax.experimental.pallas import tpu as pltpu
from jax.sharding import PartitionSpec as P


HIGHEST_MODE = lax.Precision.HIGHEST
EPSILON = 1e-06
F32 = jnp.float32
BF16 = jnp.bfloat16
I32 = jnp.int32
LANES = 128
HEAD = 24


def dot(a, b, ca, cb, precision=None):
    return lax.dot_general(
        a, b, (((ca,), (cb,)), ((), ())), precision=precision, preferred_element_type=F32
    )


def iota(shape, dim):
    return lax.broadcasted_iota(I32, shape, dim)


def shaped(*dims, dtype=BF16):
    return jax.ShapeDtypeStruct(dims, dtype)


def bounds(seg, adapters, first_token):
    marks, at = [], -first_token
    for a in range(adapters):
        marks.append((at, at + seg[a]))
        at = at + seg[a]
    return marks


def picked(spread, marks):
    rank = spread.shape[0] // len(marks)
    at = iota((rank, spread.shape[1]), 1)
    total = jnp.zeros((rank, spread.shape[1]), F32)
    for a, (lo, hi) in enumerate(marks):
        total += jnp.where((at >= lo) & (at < hi), spread[a * rank : (a + 1) * rank], 0.0)
    return total


def widened(rank_rows, marks):
    at = iota(rank_rows.shape, 1)
    wide = [jnp.where((at >= lo) & (at < hi), rank_rows, 0.0) for lo, hi in marks]
    return jnp.concatenate(wide, axis=0).astype(BF16)


def packed(rows):
    return jnp.concatenate([rows[:, :LANES], rows[:, LANES:]], axis=0)


def unpacked(rows):
    half = rows.shape[0] // 2
    return jnp.concatenate([rows[:half], rows[half:]], axis=1)


def token_scale_of(col_scale, marks, token_count):
    at = iota((token_count, LANES), 0)
    total = jnp.zeros((token_count, LANES), F32)
    for a, (lo, hi) in enumerate(marks):
        total += jnp.where((at >= lo) & (at < hi), col_scale[a : a + 1], 0.0)
    return total


def shift(block, pairs):
    return lax.ppermute(block, "tensor", pairs)


def call(kernel, out_shape, scalars=0, grid=(), in_specs=None, out_specs=None, scratch=(),
         flops=0, moved=0):
    return pl.pallas_call(
        kernel,
        out_shape=out_shape,
        grid_spec=pltpu.PrefetchScalarGridSpec(
            num_scalar_prefetch=scalars,
            grid=grid,
            in_specs=in_specs,
            out_specs=out_specs,
            scratch_shapes=list(scratch),
        ),
        cost_estimate=pl.CostEstimate(flops=flops, bytes_accessed=moved, transcendentals=0),
        compiler_params=pltpu.CompilerParams(vmem_limit_bytes=16 * 2**20),
    )


def in_hbm(array):
    return pltpu.with_memory_space_constraint(array, pltpu.HBM)


def whole(*dims):
    return pl.BlockSpec(dims, lambda *ids: (0,) * len(dims))


def first_kernel(where, tokens, weight, down, head, keep, give, gram, lines):
    rank = down.shape[1]
    count = tokens.shape[1]

    @pl.when(pl.program_id(0) == 0)
    def _():
        mine = down[0]
        lines[:count] = tokens[...].T
        lines[count:] = mine
        square = dot(mine, mine, 1, 1)
        tile = (iota((rank, LANES), 1) % rank == iota((rank, LANES), 0)).astype(F32)
        spread = dot(square, tile, 1, 0, HIGHEST_MODE)
        rows, cols = iota((rank, LANES), 0), iota((rank, LANES), 1)
        spread = jnp.where(cols // rank == rows % 8, spread, 0.0)
        gram[0:1, :] = jnp.sum(spread[:8], axis=0, keepdims=True)
        gram[1:2, :] = jnp.sum(spread[8:], axis=0, keepdims=True)

    share = 32
    pieces = weight.shape[0] // share
    part = weight[pl.ds(pl.multiple_of(jnp.minimum(where[0], pieces - 1) * share, share), share), :]
    part = part.astype(F32)
    squares = jnp.sum(part * part, axis=0, keepdims=True) * (where[0] < pieces).astype(F32)
    row = iota((8, LANES), 0)
    for block in range(0, weight.shape[1], 4 * LANES):
        both = dot(lines[...], weight[:, block : block + 4 * LANES], 1, 0)
        base = both[:count].astype(BF16)
        for k in range(4):
            lanes = slice(k * LANES, (k + 1) * LANES)
            tail = jnp.where(
                row == 0,
                squares[:, block + k * LANES : block + (k + 1) * LANES],
                jnp.where(row == 1, gram[0:1, :], jnp.where(row == 2, gram[1:2, :], 0.0)),
            )
            head[block // LANES + k] = jnp.concatenate([both[count:, lanes], tail], 0).astype(BF16)
        for k in range(2):
            at = block // LANES // 2 + k
            even = base[:, 2 * k * LANES : (2 * k + 1) * LANES]
            odd = base[:, (2 * k + 1) * LANES : (2 * k + 2) * LANES]

            @pl.when(where[1] == 0)
            def _():
                keep[at] = even
                give[at] = odd

            @pl.when(where[1] != 0)
            def _():
                keep[at] = odd
                give[at] = even


def low_kernel(where, seg, tokens, down, low):
    marks = bounds(seg, seg.shape[0], where[0] * tokens.shape[1])
    spread = dot(down[...], tokens[...], 1, 0)
    low[...] = packed(picked(spread, marks)).astype(BF16)


def halves_kernel(where, keep_a, got_a, keep_b, got_b, keep, give):
    keep[...] = (keep_a[...].astype(F32) + got_a[...].astype(F32)).astype(BF16)
    give[...] = (keep_b[...].astype(F32) + got_b[...].astype(F32)).astype(BF16)


def squares_kernel(where, head, up, second):
    rank = up.shape[1]
    total = jnp.sum(head[...].astype(F32), axis=0)
    factor = up[0].astype(F32)
    rows, cols = iota((rank, LANES), 0), iota((rank, LANES), 1)
    spread = jnp.where(rows < 8, total[rank + 1 : rank + 2], total[rank + 2 : rank + 3])
    spread = jnp.where(cols // rank == rows % 8, spread, 0.0)
    tiled = jnp.concatenate([factor] * (LANES // rank), axis=0)
    gram_up = dot(spread, tiled, 1, 0, HIGHEST_MODE)
    mine = jnp.sum(factor * (2.0 * total[:rank] + gram_up), axis=0, keepdims=True)
    both = jnp.concatenate([mine, total[rank : rank + 1]], axis=0)
    second[...] = jnp.broadcast_to(both[None], second.shape)


def lift_kernel(where, keep, got, up, down, near):
    count = keep.shape[0]
    for out, first in ((up, 2), (down, count - 3), (near, count - 1)):
        for i in range(out.shape[0]):
            at = (where[3] + first + i) % count
            out[i] = (keep[at].astype(F32) + got[at].astype(F32)).astype(BF16)


def pack_kernel(near, up, down, scaled, below, above, before, after, own):
    before[0] = (near[0].astype(F32) + up[0].astype(F32)).astype(BF16)
    before[1] = scaled[...]
    before[2] = below[...]
    after[0] = (near[2].astype(F32) + up[2].astype(F32) + down[1].astype(F32)).astype(BF16)
    after[1] = scaled[...]
    after[2] = below[...]
    after[3] = above[...]
    own[...] = near[1].astype(F32) + up[1].astype(F32) + down[0].astype(F32)


def join_kernel(after, from_below, from_above, out):
    out[:3] = after[1:]
    out[3:6] = from_below[1:]
    out[6:] = from_above[1:]


def scale_kernel(where, seg, second, magnitude, cotangent, up, low, third, scaled, norms):
    count = cotangent.shape[0]
    marks = bounds(seg, seg.shape[0], where[0] * count)
    parts = second[...]
    squares = parts[:, 0, :] + jnp.sum(parts[:, 1, :], axis=0, keepdims=True)
    col_norms = jnp.sqrt(jnp.maximum(squares, 0.0) + EPSILON)
    norms[...] = col_norms
    scale = token_scale_of(magnitude[...].astype(F32) / col_norms, marks, count)
    grad = (cotangent[...].astype(F32) * scale).astype(BF16)
    scaled[...] = grad
    back = packed(picked(dot(up[...], grad, 1, 1), marks)).astype(BF16)
    every = jnp.concatenate([low[...], back], axis=0)
    third[...] = jnp.broadcast_to(every[None], third.shape)


def sums_kernel(rank_rows, ranks):
    ranks[...] = jnp.sum(rank_rows[...].astype(F32), axis=0).astype(BF16)


def grads_kernel(where, seg, ranks, got, scaled, up, tokens, fourth, low_wide, back_wide):
    adapters = seg.shape[0]
    own_rows, count = tokens.shape
    rank = up.shape[0] // adapters
    marks = bounds(seg, adapters, where[0] * count)
    total = ranks[...].astype(F32) + got[...].astype(F32)
    low = widened(unpacked(total[: 2 * rank]), marks)
    back = widened(unpacked(total[2 * rank :]), marks)
    low_wide[...] = low
    back_wide[...] = back
    down_part = dot(back, tokens[...], 1, 1).astype(BF16)
    up_part = dot(low, scaled[...], 1, 0).astype(BF16)
    pad = jnp.zeros((rank, -own_rows % LANES), BF16)
    for a in range(adapters):
        lines = slice(a * rank, (a + 1) * rank)
        fourth[a] = jnp.concatenate([down_part[lines], pad, up_part[lines]], axis=1)


def hidden_kernel(where, seg, base, base_a, base_b, low, up, norms, magnitude, cotangent,
                  projected, mag):
    count = cotangent.shape[0]
    marks = bounds(seg, seg.shape[0], where[0] * count)
    hidden = base[...] + base_a[0].astype(F32) + base_b[0].astype(F32)
    hidden = hidden + dot(low[...], up[...], 0, 0)
    scale = token_scale_of(magnitude[...].astype(F32) / norms[...], marks, count)
    projected[...] = (hidden * scale).astype(BF16)
    weighted = cotangent[...].astype(F32) * hidden
    at = iota((count, LANES), 0)
    sums = [
        jnp.sum(jnp.where((at >= lo) & (at < hi), weighted, 0.0), axis=0, keepdims=True)
        for lo, hi in marks
    ]
    mag[...] = jnp.concatenate(sums, axis=0).astype(BF16)


def total_kernel(arrived, mag, fifth):
    total = jnp.sum(arrived[...].astype(F32), axis=0).astype(BF16)
    both = jnp.concatenate([total, mag[...]], axis=1)
    fifth[...] = jnp.broadcast_to(both[None], fifth.shape)


def final_kernel(fifth, norms, grad_down, grad_up, grad_magnitude):
    own_rows = grad_down.shape[2]
    edge = own_rows + -own_rows % LANES
    grad_down[...] = fifth[:, :, :own_rows]
    grad_up[...] = fifth[:, :, edge : edge + LANES].astype(F32)
    total = jnp.sum(fifth[:, :, edge + LANES :].astype(F32), axis=0)
    grad_magnitude[...] = total / norms[...]


def tokens_kernel(where, x0, x1, *rest):
    *columns, first, second, out, total = rest
    step = pl.program_id(0)

    @pl.when(step == 0)
    def _():
        total[...] = dot(first[...], second[...], 0, 0)

    left = [block[i] for i in range(x0.shape[0]) for block in (x0, x1)]
    right = [column[...] for column in columns]
    total[...] += dot(jnp.concatenate(right, axis=1), jnp.concatenate(left, axis=1), 1, 1)

    @pl.when(step == pl.num_programs(0) - 1)
    def _():
        out[...] = total[...]


def tokens_rest_kernel(where, x0, x1, *rest):
    *columns, part, out, total = rest
    step = pl.program_id(0)

    @pl.when(step == 0)
    def _():
        total[...] = part[...]

    left = [block[i] for i in range(x0.shape[0]) for block in (x0, x1)]
    right = [column[...] for column in columns]
    total[...] += dot(jnp.concatenate(right, axis=1), jnp.concatenate(left, axis=1), 1, 1)

    @pl.when(step == pl.num_programs(0) - 1)
    def _():
        out[...] = total[...].astype(BF16)


def exchange(blocks, axis, groups=None):
    return lax.all_to_all(blocks, axis, 0, 0, tiled=True, axis_index_groups=groups)


def local(tokens, base_weight, adapter_down, adapter_up, magnitude, seg_lengths, cotangent):
    count, own_rows = tokens.shape
    adapters, _, rank = adapter_down.shape
    width = adapter_up.shape[2]
    full = base_weight.shape[1]
    size = full // width
    zs = size // 4
    wide = adapters * rank
    me_dp = lax.axis_index("dp")
    me = lax.axis_index("tensor")
    core, hi = me % 2, me // (2 * zs)
    z = (me // 2) % zs
    where = jnp.stack([me_dp, core, hi, z]).astype(I32)
    core_pairs = [(i, i ^ 1) for i in range(size)]
    hi_pairs = [(i, (i + size // 2) % size) for i in range(size)]

    turned = tokens.T
    z_groups = [[h * 2 * zs + a * 2 + c for a in range(zs)] for h in range(2) for c in range(2)]
    down_rows = jnp.transpose(adapter_down, (0, 2, 1))
    down_flat = down_rows.reshape(wide, own_rows)
    up_own = adapter_up.reshape(wide, width)

    head, keep, give = call(
        first_kernel,
        [shaped(size, HEAD, width), shaped(size // 2, count, width), shaped(size // 2, count, width)],
        scalars=1,
        grid=(2,),
        in_specs=[
            whole(own_rows, count),
            pl.BlockSpec((own_rows, full // 2), lambda i, s: (0, i)),
            pl.BlockSpec((1, rank, own_rows), lambda i, s: (s[0], 0, 0)),
        ],
        out_specs=[
            pl.BlockSpec((size // 2, HEAD, width), lambda i, s: (i, 0, 0)),
            pl.BlockSpec((size // 4, count, width), lambda i, s: (i, 0, 0)),
            pl.BlockSpec((size // 4, count, width), lambda i, s: (i, 0, 0)),
        ],
        scratch=[pltpu.VMEM((8, width), F32), pltpu.VMEM((count + rank, own_rows), BF16)],
        flops=2 * count * own_rows * full,
        moved=2 * own_rows * full,
    )(where, in_hbm(turned), in_hbm(base_weight), in_hbm(down_rows))
    head = exchange(head, "tensor")
    got = shift(give, core_pairs)
    low = call(
        low_kernel,
        shaped(2 * rank, width),
        scalars=2,
        grid=(1,),
        in_specs=[whole(own_rows, count), whole(wide, own_rows)],
        out_specs=whole(2 * rank, width),
        flops=2 * count * own_rows * wide,
        moved=4 * count * own_rows,
    )(where, seg_lengths, turned, down_flat)

    mine = pl.BlockSpec((2, count, width), lambda i, s: (s[2] * (zs // 2) + i, 0, 0))
    theirs = pl.BlockSpec((2, count, width), lambda i, s: ((1 - s[2]) * (zs // 2) + i, 0, 0))
    out = pl.BlockSpec((2, count, width), lambda i, s: (i, 0, 0))
    keep, give = call(
        halves_kernel,
        [shaped(zs, count, width)] * 2,
        scalars=1,
        grid=(zs // 2,),
        in_specs=[mine, mine, theirs, theirs],
        out_specs=[out, out],
        moved=12 * zs * count * width,
    )(where, keep, got, keep, got)
    got = shift(give, hi_pairs)

    def along_z(step):
        return [
            (h * 2 * zs + a * 2 + c, h * 2 * zs + (a + step) % zs * 2 + c)
            for h in range(2)
            for a in range(zs)
            for c in range(2)
        ]

    second = call(
        squares_kernel,
        shaped(adapters, 2, width, dtype=F32),
        scalars=1,
        grid=(1,),
        in_specs=[
            whole(size, HEAD, width),
            pl.BlockSpec((1, rank, width), lambda i, s: (s[0], 0, 0)),
        ],
        out_specs=whole(adapters, 2, width),
        moved=2 * size * HEAD * width,
    )(where, head, adapter_up)
    second = exchange(second, "dp")

    up3, down2, near = call(
        lift_kernel,
        [shaped(n, count, width) for n in (3, 2, 3)],
        scalars=1,
        grid=(1,),
        in_specs=[whole(zs, count, width)] * 2,
        out_specs=[whole(n, count, width) for n in (3, 2, 3)],
        moved=6 * zs * count * width,
    )(where, keep, got)
    up3 = shift(up3, along_z(3))
    down2 = shift(down2, along_z(-3))

    third, scaled, norms = call(
        scale_kernel,
        [shaped(zs, 4 * rank, width), shaped(count, width), shaped(adapters, width, dtype=F32)],
        scalars=2,
        grid=(1,),
        in_specs=[
            whole(adapters, 2, width),
            whole(adapters, width),
            whole(count, width),
            whole(wide, width),
            whole(2 * rank, width),
        ],
        out_specs=[whole(zs, 4 * rank, width), whole(count, width), whole(adapters, width)],
        flops=2 * count * wide * width,
        moved=8 * count * width,
    )(where, seg_lengths, second, magnitude, cotangent, up_own, low)
    third = exchange(third, "tensor", z_groups)
    below = shift(scaled, along_z(3))
    above = shift(scaled, along_z(-3))
    ranks = call(
        sums_kernel,
        shaped(4 * rank, width),
        grid=(1,),
        in_specs=[whole(zs, 4 * rank, width)],
        out_specs=whole(4 * rank, width),
        moved=2 * zs * 4 * rank * width,
    )(third)
    ranks = (ranks.astype(F32) + shift(ranks, hi_pairs).astype(F32)).astype(BF16)
    other = shift(ranks, core_pairs)

    before, after, base = call(
        pack_kernel,
        [shaped(3, count, width), shaped(4, count, width), shaped(count, width, dtype=F32)],
        grid=(1,),
        in_specs=[whole(n, count, width) for n in (3, 3, 2)] + [whole(count, width)] * 3,
        out_specs=[whole(3, count, width), whole(4, count, width), whole(count, width)],
        moved=36 * count * width,
    )(near, up3, down2, scaled, below, above)
    from_below = shift(after, along_z(1))
    from_above = shift(before, along_z(-1))
    gather_a = call(
        join_kernel,
        shaped(zs, count, width),
        grid=(1,),
        in_specs=[whole(n, count, width) for n in (4, 4, 3)],
        out_specs=whole(zs, count, width),
        moved=4 * zs * count * width,
    )(after, from_below, from_above)
    gather_b = shift(gather_a, hi_pairs)
    gather_c = shift(gather_a, core_pairs)
    gather_d = shift(gather_b, core_pairs)

    edge = own_rows + -own_rows % LANES
    blocks = edge + width
    fourth, low_wide, back_wide = call(
        grads_kernel,
        [shaped(adapters, rank, blocks), shaped(wide, count), shaped(wide, count)],
        scalars=2,
        grid=(1,),
        in_specs=[
            whole(4 * rank, width),
            whole(4 * rank, width),
            whole(count, width),
            whole(wide, width),
            whole(own_rows, count),
        ],
        out_specs=[whole(adapters, rank, blocks), whole(wide, count), whole(wide, count)],
        flops=2 * count * wide * (own_rows + width),
        moved=4 * adapters * rank * blocks,
    )(where, seg_lengths, ranks, other, scaled, up_own, turned)
    fourth = exchange(fourth, "dp")

    first_block = pl.BlockSpec((1, count, width), lambda i, *s: (0, 0, 0))
    projected, mag = call(
        hidden_kernel,
        [shaped(count, width), shaped(adapters, width)],
        scalars=2,
        grid=(1,),
        in_specs=[
            whole(count, width),
            first_block,
            first_block,
            whole(wide, count),
            whole(wide, width),
            whole(adapters, width),
            whole(adapters, width),
            whole(count, width),
        ],
        out_specs=[whole(count, width), whole(adapters, width)],
        flops=2 * count * wide * width,
        moved=16 * count * width,
    )(where, seg_lengths, base, from_below, from_above, low_wide, up_own, norms, magnitude,
      cotangent)

    fifth = call(
        total_kernel,
        shaped(adapters, rank, blocks + width),
        grid=(1,),
        in_specs=[whole(adapters, rank, blocks), whole(adapters, width)],
        out_specs=whole(adapters, rank, blocks + width),
        moved=4 * adapters * rank * blocks,
    )(fourth, mag)
    fifth = exchange(fifth, "dp")

    per = 4
    offsets = (0, -3, 3, -1, -4, 2, 1, -2)

    def column(k, x_bit, c_bit):
        def at(i, s):
            off = jnp.where(i == 0, offsets[k], offsets[per + k])
            block = (s[3] + off + zs) % zs
            return (0, (s[2] ^ x_bit) * (2 * zs) + block * 2 + (s[1] ^ c_bit))

        return pl.BlockSpec((own_rows, width), at)

    def columns(x_bit):
        return [column(k, x_bit, c) for k in range(per) for c in range(2)]

    block = pl.BlockSpec((per, count, width), lambda i, s: (i, 0, 0))
    weights = [in_hbm(base_weight)] * (2 * per)
    part = call(
        tokens_kernel,
        shaped(own_rows, count, dtype=F32),
        scalars=1,
        grid=(zs // per,),
        in_specs=[block] * 2 + columns(0) + [whole(wide, own_rows), whole(wide, count)],
        out_specs=whole(own_rows, count),
        scratch=[pltpu.VMEM((own_rows, count), F32)],
        flops=count * own_rows * (full + 2 * wide),
        moved=own_rows * full,
    )(where, gather_a, gather_c, *weights, down_flat, back_wide)
    grad_tokens = call(
        tokens_rest_kernel,
        shaped(own_rows, count),
        scalars=1,
        grid=(zs // per,),
        in_specs=[block] * 2 + columns(1) + [whole(own_rows, count)],
        out_specs=whole(own_rows, count),
        scratch=[pltpu.VMEM((own_rows, count), F32)],
        flops=count * own_rows * full,
        moved=own_rows * full,
    )(where, gather_b, gather_d, *weights, part)

    grad_down, grad_up, grad_magnitude = call(
        final_kernel,
        [
            shaped(adapters, rank, own_rows),
            shaped(adapters, rank, width, dtype=F32),
            shaped(adapters, width, dtype=F32),
        ],
        grid=(1,),
        in_specs=[whole(adapters, rank, blocks + width), whole(adapters, width)],
        out_specs=[
            whole(adapters, rank, own_rows),
            whole(adapters, rank, width),
            whole(adapters, width),
        ],
        moved=4 * adapters * rank * blocks,
    )(fifth, norms)
    return (projected, grad_tokens.T, jnp.transpose(grad_down, (0, 2, 1)), grad_up, grad_magnitude)


def solution(mesh):
    placed = (
        P("dp", "tensor"),
        P("tensor", None),
        P(None, "tensor", None),
        P(None, None, "tensor"),
        P(None, "tensor"),
        P(),
        P("dp", "tensor"),
    )
    return jax.shard_map(
        local,
        mesh=mesh,
        in_specs=placed,
        out_specs=(
            P("dp", "tensor"),
            P("dp", "tensor"),
            P(None, "tensor", None),
            P(None, None, "tensor"),
            P(None, "tensor"),
        ),
        check_vma=False,
    )
```

```python
import jax
import jax.numpy as jnp
from jax import lax
from jax.experimental import pallas as pl
from jax.experimental.pallas import tpu as pltpu
from jax.sharding import PartitionSpec as P


HIGHEST_MODE = lax.Precision.HIGHEST
EPSILON = 1e-06
F32 = jnp.float32
BF16 = jnp.bfloat16
I32 = jnp.int32
LANES = 128
HEAD = 24


def dot(a, b, ca, cb, precision=None):
    return lax.dot_general(
        a, b, (((ca,), (cb,)), ((), ())), precision=precision, preferred_element_type=F32
    )


def iota(shape, dim):
    return lax.broadcasted_iota(I32, shape, dim)


def shaped(*dims, dtype=BF16):
    return jax.ShapeDtypeStruct(dims, dtype)


def bounds(seg, adapters, first_token):
    marks, at = [], -first_token
    for a in range(adapters):
        marks.append((at, at + seg[a]))
        at = at + seg[a]
    return marks


def picked(spread, marks):
    rank = spread.shape[0] // len(marks)
    at = iota((rank, spread.shape[1]), 1)
    total = jnp.zeros((rank, spread.shape[1]), F32)
    for a, (lo, hi) in enumerate(marks):
        total += jnp.where((at >= lo) & (at < hi), spread[a * rank : (a + 1) * rank], 0.0)
    return total


def widened(rank_rows, marks):
    at = iota(rank_rows.shape, 1)
    wide = [jnp.where((at >= lo) & (at < hi), rank_rows, 0.0) for lo, hi in marks]
    return jnp.concatenate(wide, axis=0).astype(BF16)


def packed(rows):
    return jnp.concatenate([rows[:, :LANES], rows[:, LANES:]], axis=0)


def unpacked(rows):
    half = rows.shape[0] // 2
    return jnp.concatenate([rows[:half], rows[half:]], axis=1)


def token_scale_of(col_scale, marks, token_count):
    at = iota((token_count, LANES), 0)
    total = jnp.zeros((token_count, LANES), F32)
    for a, (lo, hi) in enumerate(marks):
        total += jnp.where((at >= lo) & (at < hi), col_scale[a : a + 1], 0.0)
    return total


def shift(block, pairs):
    return lax.ppermute(block, "tensor", pairs)


def call(kernel, out_shape, scalars=0, grid=(), in_specs=None, out_specs=None, scratch=(),
         flops=0, moved=0):
    return pl.pallas_call(
        kernel,
        out_shape=out_shape,
        grid_spec=pltpu.PrefetchScalarGridSpec(
            num_scalar_prefetch=scalars,
            grid=grid,
            in_specs=in_specs,
            out_specs=out_specs,
            scratch_shapes=list(scratch),
        ),
        cost_estimate=pl.CostEstimate(flops=flops, bytes_accessed=moved, transcendentals=0),
        compiler_params=pltpu.CompilerParams(vmem_limit_bytes=16 * 2**20),
    )


def in_hbm(array):
    return pltpu.with_memory_space_constraint(array, pltpu.HBM)


def whole(*dims):
    return pl.BlockSpec(dims, lambda *ids: (0,) * len(dims))


def first_kernel(where, tokens, weight, down, head, keep, give, gram, lines):
    rank = down.shape[1]
    count = tokens.shape[1]

    @pl.when(pl.program_id(0) == 0)
    def _():
        mine = down[0]
        lines[:count] = tokens[...].T
        lines[count:] = mine
        square = dot(mine, mine, 1, 1)
        tile = (iota((rank, LANES), 1) % rank == iota((rank, LANES), 0)).astype(F32)
        spread = dot(square, tile, 1, 0, HIGHEST_MODE)
        rows, cols = iota((rank, LANES), 0), iota((rank, LANES), 1)
        spread = jnp.where(cols // rank == rows % 8, spread, 0.0)
        gram[0:1, :] = jnp.sum(spread[:8], axis=0, keepdims=True)
        gram[1:2, :] = jnp.sum(spread[8:], axis=0, keepdims=True)

    share = 32
    pieces = weight.shape[0] // share
    part = weight[pl.ds(pl.multiple_of(jnp.minimum(where[0], pieces - 1) * share, share), share), :]
    part = part.astype(F32)
    squares = jnp.sum(part * part, axis=0, keepdims=True) * (where[0] < pieces).astype(F32)
    row = iota((8, LANES), 0)
    for block in range(0, weight.shape[1], 4 * LANES):
        both = dot(lines[...], weight[:, block : block + 4 * LANES], 1, 0)
        base = both[:count].astype(BF16)
        for k in range(4):
            lanes = slice(k * LANES, (k + 1) * LANES)
            tail = jnp.where(
                row == 0,
                squares[:, block + k * LANES : block + (k + 1) * LANES],
                jnp.where(row == 1, gram[0:1, :], jnp.where(row == 2, gram[1:2, :], 0.0)),
            )
            head[block // LANES + k] = jnp.concatenate([both[count:, lanes], tail], 0).astype(BF16)
        for k in range(2):
            at = block // LANES // 2 + k
            even = base[:, 2 * k * LANES : (2 * k + 1) * LANES]
            odd = base[:, (2 * k + 1) * LANES : (2 * k + 2) * LANES]

            @pl.when(where[1] == 0)
            def _():
                keep[at] = even
                give[at] = odd

            @pl.when(where[1] != 0)
            def _():
                keep[at] = odd
                give[at] = even


def low_kernel(where, seg, tokens, down, low):
    marks = bounds(seg, seg.shape[0], where[0] * tokens.shape[1])
    spread = dot(down[...], tokens[...], 1, 0)
    low[...] = packed(picked(spread, marks)).astype(BF16)


def halves_kernel(where, keep_a, got_a, keep_b, got_b, keep, give):
    keep[...] = (keep_a[...].astype(F32) + got_a[...].astype(F32)).astype(BF16)
    give[...] = (keep_b[...].astype(F32) + got_b[...].astype(F32)).astype(BF16)


def squares_kernel(where, head, up, second):
    rank = up.shape[1]
    total = jnp.sum(head[...].astype(F32), axis=0)
    factor = up[0].astype(F32)
    rows, cols = iota((rank, LANES), 0), iota((rank, LANES), 1)
    spread = jnp.where(rows < 8, total[rank + 1 : rank + 2], total[rank + 2 : rank + 3])
    spread = jnp.where(cols // rank == rows % 8, spread, 0.0)
    tiled = jnp.concatenate([factor] * (LANES // rank), axis=0)
    gram_up = dot(spread, tiled, 1, 0, HIGHEST_MODE)
    mine = jnp.sum(factor * (2.0 * total[:rank] + gram_up), axis=0, keepdims=True)
    both = jnp.concatenate([mine, total[rank : rank + 1]], axis=0)
    second[...] = jnp.broadcast_to(both[None], second.shape)


def lift_kernel(where, keep, got, up, down, near):
    count = keep.shape[0]
    for out, steps in ((up, (1, 4, -2)), (down, (-1, 2)), (near, (0, 3, -3))):
        for i, step in enumerate(steps):
            at = (where[3] + step + count) % count
            out[i] = (keep[at].astype(F32) + got[at].astype(F32)).astype(BF16)


def scale_kernel(where, seg, second, magnitude, cotangent, up, low, share, norms):
    count = cotangent.shape[0]
    marks = bounds(seg, seg.shape[0], where[0] * count)
    parts = second[...]
    squares = parts[:, 0, :] + jnp.sum(parts[:, 1, :], axis=0, keepdims=True)
    col_norms = jnp.sqrt(jnp.maximum(squares, 0.0) + EPSILON)
    norms[...] = col_norms
    scale = token_scale_of(magnitude[...].astype(F32) / col_norms, marks, count)
    grad = (cotangent[...].astype(F32) * scale).astype(BF16)
    share[:count] = grad
    back = packed(picked(dot(up[...], grad, 1, 1), marks)).astype(BF16)
    share[count:] = jnp.concatenate([low[...], back], axis=0)


def third_kernel(share, other, third):
    total = (share[...].astype(F32) + other[...].astype(F32)).astype(BF16)
    third[...] = jnp.broadcast_to(total[None], third.shape)


def far_kernel(near, up, down, share, other, to_up, to_down, own):
    own[...] = near[0].astype(F32) + up[0].astype(F32) + down[0].astype(F32)
    to_up[0] = (near[1].astype(F32) + up[1].astype(F32) + down[1].astype(F32)).astype(BF16)
    to_down[0] = (near[2].astype(F32) + up[2].astype(F32)).astype(BF16)
    for out in (to_up, to_down):
        out[1] = share[...]
        out[2] = other[...]


def pack_kernel(share, other, below, above, before, after):
    for out in (before, after):
        out[0] = share[...]
        out[1] = other[...]
        out[2:4] = below[1:]
    after[4:6] = above[1:]


def join_kernel(after, from_below, from_above, out):
    out[:6] = after[...]
    out[6:12] = from_below[...]
    out[12:] = from_above[...]


def sums_kernel(rank_rows, ranks):
    ranks[...] = jnp.sum(rank_rows[...].astype(F32), axis=0).astype(BF16)


def grads_kernel(where, seg, ranks, got, scaled, up, tokens, fourth, low_wide, back_wide):
    adapters = seg.shape[0]
    own_rows, count = tokens.shape
    rank = up.shape[0] // adapters
    marks = bounds(seg, adapters, where[0] * count)
    total = ranks[...].astype(F32) + got[...].astype(F32)
    low = widened(unpacked(total[: 2 * rank]), marks)
    back = widened(unpacked(total[2 * rank :]), marks)
    low_wide[...] = low
    back_wide[...] = back
    down_part = dot(back, tokens[...], 1, 1).astype(BF16)
    up_part = dot(low, scaled[...], 1, 0).astype(BF16)
    pad = jnp.zeros((rank, -own_rows % LANES), BF16)
    for a in range(adapters):
        lines = slice(a * rank, (a + 1) * rank)
        fourth[a] = jnp.concatenate([down_part[lines], pad, up_part[lines]], axis=1)


def hidden_kernel(where, seg, base, base_a, base_b, low, up, norms, magnitude, cotangent,
                  projected, mag):
    count = cotangent.shape[0]
    marks = bounds(seg, seg.shape[0], where[0] * count)
    hidden = base[...] + base_a[0].astype(F32) + base_b[0].astype(F32)
    hidden = hidden + dot(low[...], up[...], 0, 0)
    scale = token_scale_of(magnitude[...].astype(F32) / norms[...], marks, count)
    projected[...] = (hidden * scale).astype(BF16)
    weighted = cotangent[...].astype(F32) * hidden
    at = iota((count, LANES), 0)
    sums = [
        jnp.sum(jnp.where((at >= lo) & (at < hi), weighted, 0.0), axis=0, keepdims=True)
        for lo, hi in marks
    ]
    mag[...] = jnp.concatenate(sums, axis=0).astype(BF16)


def total_kernel(arrived, mag, fifth):
    total = jnp.sum(arrived[...].astype(F32), axis=0).astype(BF16)
    both = jnp.concatenate([total, mag[...]], axis=1)
    fifth[...] = jnp.broadcast_to(both[None], fifth.shape)


def final_kernel(fifth, norms, grad_down, grad_up, grad_magnitude):
    own_rows = grad_down.shape[2]
    edge = own_rows + -own_rows % LANES
    grad_down[...] = fifth[:, :, :own_rows]
    grad_up[...] = fifth[:, :, edge : edge + LANES].astype(F32)
    total = jnp.sum(fifth[:, :, edge + LANES :].astype(F32), axis=0)
    grad_magnitude[...] = total / norms[...]


def tokens_kernel(where, blocks, *rest):
    *columns, first, second, out, total = rest
    step = pl.program_id(0)

    @pl.when(step == 0)
    def _():
        total[...] = dot(first[...], second[...], 0, 0)

    left = [blocks[i] for i in range(blocks.shape[0])]
    right = [column[...] for column in columns]
    total[...] += dot(jnp.concatenate(right, axis=1), jnp.concatenate(left, axis=1), 1, 1)

    @pl.when(step == pl.num_programs(0) - 1)
    def _():
        out[...] = total[...]


def tokens_rest_kernel(where, blocks, *rest):
    *columns, part, out, total = rest
    step = pl.program_id(0)

    @pl.when(step == 0)
    def _():
        total[...] = part[...]

    left = [blocks[i] for i in range(blocks.shape[0])]
    right = [column[...] for column in columns]
    total[...] += dot(jnp.concatenate(right, axis=1), jnp.concatenate(left, axis=1), 1, 1)

    @pl.when(step == pl.num_programs(0) - 1)
    def _():
        out[...] = total[...].astype(BF16)


def exchange(blocks, axis, groups=None):
    return lax.all_to_all(blocks, axis, 0, 0, tiled=True, axis_index_groups=groups)


def local(tokens, base_weight, adapter_down, adapter_up, magnitude, seg_lengths, cotangent):
    count, own_rows = tokens.shape
    adapters, _, rank = adapter_down.shape
    width = adapter_up.shape[2]
    full = base_weight.shape[1]
    size = full // width
    zs = size // 4
    wide = adapters * rank
    me_dp = lax.axis_index("dp")
    me = lax.axis_index("tensor")
    core, hi = me % 2, me // (2 * zs)
    z = (me // 2) % zs
    where = jnp.stack([me_dp, core, hi, z]).astype(I32)
    core_pairs = [(i, i ^ 1) for i in range(size)]
    hi_pairs = [(i, (i + size // 2) % size) for i in range(size)]

    turned = tokens.T
    z_groups = [[h * 2 * zs + a * 2 + c for a in range(zs)] for h in range(2) for c in range(2)]
    down_rows = jnp.transpose(adapter_down, (0, 2, 1))
    down_flat = down_rows.reshape(wide, own_rows)
    up_own = adapter_up.reshape(wide, width)

    head, keep, give = call(
        first_kernel,
        [shaped(size, HEAD, width), shaped(size // 2, count, width), shaped(size // 2, count, width)],
        scalars=1,
        grid=(2,),
        in_specs=[
            whole(own_rows, count),
            pl.BlockSpec((own_rows, full // 2), lambda i, s: (0, i)),
            pl.BlockSpec((1, rank, own_rows), lambda i, s: (s[0], 0, 0)),
        ],
        out_specs=[
            pl.BlockSpec((size // 2, HEAD, width), lambda i, s: (i, 0, 0)),
            pl.BlockSpec((size // 4, count, width), lambda i, s: (i, 0, 0)),
            pl.BlockSpec((size // 4, count, width), lambda i, s: (i, 0, 0)),
        ],
        scratch=[pltpu.VMEM((8, width), F32), pltpu.VMEM((count + rank, own_rows), BF16)],
        flops=2 * count * own_rows * full,
        moved=2 * own_rows * full,
    )(where, in_hbm(turned), in_hbm(base_weight), in_hbm(down_rows))
    head = exchange(head, "tensor")
    got = shift(give, core_pairs)
    low = call(
        low_kernel,
        shaped(2 * rank, width),
        scalars=2,
        grid=(1,),
        in_specs=[whole(own_rows, count), whole(wide, own_rows)],
        out_specs=whole(2 * rank, width),
        flops=2 * count * own_rows * wide,
        moved=4 * count * own_rows,
    )(where, seg_lengths, turned, down_flat)

    mine = pl.BlockSpec((2, count, width), lambda i, s: (s[2] * (zs // 2) + i, 0, 0))
    theirs = pl.BlockSpec((2, count, width), lambda i, s: ((1 - s[2]) * (zs // 2) + i, 0, 0))
    out = pl.BlockSpec((2, count, width), lambda i, s: (i, 0, 0))
    keep, give = call(
        halves_kernel,
        [shaped(zs, count, width)] * 2,
        scalars=1,
        grid=(zs // 2,),
        in_specs=[mine, mine, theirs, theirs],
        out_specs=[out, out],
        moved=12 * zs * count * width,
    )(where, keep, got, keep, got)
    got = shift(give, hi_pairs)

    def along_z(step):
        return [
            (h * 2 * zs + a * 2 + c, h * 2 * zs + (a + step) % zs * 2 + c)
            for h in range(2)
            for a in range(zs)
            for c in range(2)
        ]

    second = call(
        squares_kernel,
        shaped(adapters, 2, width, dtype=F32),
        scalars=1,
        grid=(1,),
        in_specs=[
            whole(size, HEAD, width),
            pl.BlockSpec((1, rank, width), lambda i, s: (s[0], 0, 0)),
        ],
        out_specs=whole(adapters, 2, width),
        moved=2 * size * HEAD * width,
    )(where, head, adapter_up)
    second = exchange(second, "dp")

    up3, down2, near = call(
        lift_kernel,
        [shaped(n, count, width) for n in (3, 2, 3)],
        scalars=1,
        grid=(1,),
        in_specs=[whole(zs, count, width)] * 2,
        out_specs=[whole(n, count, width) for n in (3, 2, 3)],
        moved=6 * zs * count * width,
    )(where, keep, got)
    up3 = shift(up3, along_z(1))
    down2 = shift(down2, along_z(-1))

    share, norms = call(
        scale_kernel,
        [shaped(count + 4 * rank, width), shaped(adapters, width, dtype=F32)],
        scalars=2,
        grid=(1,),
        in_specs=[
            whole(adapters, 2, width),
            whole(adapters, width),
            whole(count, width),
            whole(wide, width),
            whole(2 * rank, width),
        ],
        out_specs=[whole(count + 4 * rank, width), whole(adapters, width)],
        flops=2 * count * wide * width,
        moved=8 * count * width,
    )(where, seg_lengths, second, magnitude, cotangent, up_own, low)
    other = shift(share, hi_pairs)
    rank_rows = pl.BlockSpec((4 * rank, width), lambda i: (count // (4 * rank), 0))
    scaled = whole(count, width)
    third = call(
        third_kernel,
        shaped(zs, 4 * rank, width),
        grid=(1,),
        in_specs=[rank_rows, rank_rows],
        out_specs=whole(zs, 4 * rank, width),
        moved=2 * zs * 4 * rank * width,
    )(share, other)
    third = exchange(third, "tensor", z_groups)
    to_up, to_down, base = call(
        far_kernel,
        [shaped(3, count, width), shaped(3, count, width), shaped(count, width, dtype=F32)],
        grid=(1,),
        in_specs=[whole(n, count, width) for n in (3, 3, 2)] + [scaled] * 2,
        out_specs=[whole(3, count, width), whole(3, count, width), whole(count, width)],
        moved=36 * count * width,
    )(near, up3, down2, share, other)
    below = shift(to_up, along_z(3))
    above = shift(to_down, along_z(-3))
    ranks = call(
        sums_kernel,
        shaped(4 * rank, width),
        grid=(1,),
        in_specs=[whole(zs, 4 * rank, width)],
        out_specs=whole(4 * rank, width),
        moved=2 * zs * 4 * rank * width,
    )(third)
    other_ranks = shift(ranks, core_pairs)

    before, after = call(
        pack_kernel,
        [shaped(4, count, width), shaped(6, count, width)],
        grid=(1,),
        in_specs=[scaled] * 2 + [whole(3, count, width)] * 2,
        out_specs=[whole(4, count, width), whole(6, count, width)],
        moved=32 * count * width,
    )(share, other, below, above)
    from_below = shift(after, along_z(1))
    from_above = shift(before, along_z(-1))
    gather_a = call(
        join_kernel,
        shaped(2 * zs, count, width),
        grid=(1,),
        in_specs=[whole(n, count, width) for n in (6, 6, 4)],
        out_specs=whole(2 * zs, count, width),
        moved=8 * zs * count * width,
    )(after, from_below, from_above)
    gather_b = shift(gather_a, core_pairs)

    edge = own_rows + -own_rows % LANES
    blocks = edge + width
    fourth, low_wide, back_wide = call(
        grads_kernel,
        [shaped(adapters, rank, blocks), shaped(wide, count), shaped(wide, count)],
        scalars=2,
        grid=(1,),
        in_specs=[
            whole(4 * rank, width),
            whole(4 * rank, width),
            whole(count, width),
            whole(wide, width),
            whole(own_rows, count),
        ],
        out_specs=[whole(adapters, rank, blocks), whole(wide, count), whole(wide, count)],
        flops=2 * count * wide * (own_rows + width),
        moved=4 * adapters * rank * blocks,
    )(where, seg_lengths, ranks, other_ranks, share, up_own, turned)
    fourth = exchange(fourth, "dp")

    first_block = pl.BlockSpec((1, count, width), lambda i, *s: (0, 0, 0))
    projected, mag = call(
        hidden_kernel,
        [shaped(count, width), shaped(adapters, width)],
        scalars=2,
        grid=(1,),
        in_specs=[
            whole(count, width),
            first_block,
            first_block,
            whole(wide, count),
            whole(wide, width),
            whole(adapters, width),
            whole(adapters, width),
            whole(count, width),
        ],
        out_specs=[whole(count, width), whole(adapters, width)],
        flops=2 * count * wide * width,
        moved=16 * count * width,
    )(where, seg_lengths, base, below, above, low_wide, up_own, norms, magnitude,
      cotangent)

    fifth = call(
        total_kernel,
        shaped(adapters, rank, blocks + width),
        grid=(1,),
        in_specs=[whole(adapters, rank, blocks), whole(adapters, width)],
        out_specs=whole(adapters, rank, blocks + width),
        moved=4 * adapters * rank * blocks,
    )(fourth, mag)
    fifth = exchange(fifth, "dp")

    per = 4
    offsets = (0, -3, 3, -1, -4, 2, 1, -2)

    def column(k, x_bit, c_bit):
        def at(i, s):
            off = jnp.where(i == 0, offsets[k], offsets[per + k])
            block = (s[3] + off + zs) % zs
            return (0, (s[2] ^ x_bit) * (2 * zs) + block * 2 + (s[1] ^ c_bit))

        return pl.BlockSpec((own_rows, width), at)

    def columns(c_bit):
        return [column(k, x, c_bit) for k in range(per) for x in range(2)]

    block = pl.BlockSpec((2 * per, count, width), lambda i, s: (i, 0, 0))
    weights = [in_hbm(base_weight)] * (2 * per)
    part = call(
        tokens_kernel,
        shaped(own_rows, count, dtype=F32),
        scalars=1,
        grid=(zs // per,),
        in_specs=[block] + columns(0) + [whole(wide, own_rows), whole(wide, count)],
        out_specs=whole(own_rows, count),
        scratch=[pltpu.VMEM((own_rows, count), F32)],
        flops=count * own_rows * (full + 2 * wide),
        moved=own_rows * full,
    )(where, gather_a, *weights, down_flat, back_wide)
    grad_tokens = call(
        tokens_rest_kernel,
        shaped(own_rows, count),
        scalars=1,
        grid=(zs // per,),
        in_specs=[block] + columns(1) + [whole(own_rows, count)],
        out_specs=whole(own_rows, count),
        scratch=[pltpu.VMEM((own_rows, count), F32)],
        flops=count * own_rows * full,
        moved=own_rows * full,
    )(where, gather_b, *weights, part)

    grad_down, grad_up, grad_magnitude = call(
        final_kernel,
        [
            shaped(adapters, rank, own_rows),
            shaped(adapters, rank, width, dtype=F32),
            shaped(adapters, width, dtype=F32),
        ],
        grid=(1,),
        in_specs=[whole(adapters, rank, blocks + width), whole(adapters, width)],
        out_specs=[
            whole(adapters, rank, own_rows),
            whole(adapters, rank, width),
            whole(adapters, width),
        ],
        moved=4 * adapters * rank * blocks,
    )(fifth, norms)
    return (projected, grad_tokens.T, jnp.transpose(grad_down, (0, 2, 1)), grad_up, grad_magnitude)


def solution(mesh):
    placed = (
        P("dp", "tensor"),
        P("tensor", None),
        P(None, "tensor", None),
        P(None, None, "tensor"),
        P(None, "tensor"),
        P(),
        P("dp", "tensor"),
    )
    return jax.shard_map(
        local,
        mesh=mesh,
        in_specs=placed,
        out_specs=(
            P("dp", "tensor"),
            P("dp", "tensor"),
            P(None, "tensor", None),
            P(None, None, "tensor"),
            P(None, "tensor"),
        ),
        check_vma=False,
    )
```

```python
import jax
import jax.numpy as jnp
from jax import lax
from jax.experimental import pallas as pl
from jax.experimental.pallas import tpu as pltpu
from jax.sharding import PartitionSpec as P


EPSILON = 1e-06
F32 = jnp.float32
BF16 = jnp.bfloat16
I32 = jnp.int32
LANES = 128
HEAD = 24


def dot(a, b, ca, cb, precision=None):
    return lax.dot_general(
        a, b, (((ca,), (cb,)), ((), ())), precision=precision, preferred_element_type=F32
    )


def iota(shape, dim):
    return lax.broadcasted_iota(I32, shape, dim)


def shaped(*dims, dtype=BF16):
    return jax.ShapeDtypeStruct(dims, dtype)


def bounds(seg, adapters, first_token):
    marks, at = [], -first_token
    for a in range(adapters):
        marks.append((at, at + seg[a]))
        at = at + seg[a]
    return marks


def picked(spread, marks):
    rank = spread.shape[0] // len(marks)
    at = iota((rank, spread.shape[1]), 1)
    total = jnp.zeros((rank, spread.shape[1]), F32)
    for a, (lo, hi) in enumerate(marks):
        total += jnp.where((at >= lo) & (at < hi), spread[a * rank : (a + 1) * rank], 0.0)
    return total


def widened(rank_rows, marks):
    at = iota(rank_rows.shape, 1)
    wide = [jnp.where((at >= lo) & (at < hi), rank_rows, 0.0) for lo, hi in marks]
    return jnp.concatenate(wide, axis=0).astype(BF16)


def packed(rows):
    return jnp.concatenate([rows[:, :LANES], rows[:, LANES:]], axis=0)


def unpacked(rows):
    half = rows.shape[0] // 2
    return jnp.concatenate([rows[:half], rows[half:]], axis=1)


def token_scale_of(col_scale, marks, token_count):
    at = iota((token_count, LANES), 0)
    total = jnp.zeros((token_count, LANES), F32)
    for a, (lo, hi) in enumerate(marks):
        total += jnp.where((at >= lo) & (at < hi), col_scale[a : a + 1], 0.0)
    return total


def shift(block, pairs):
    return lax.ppermute(block, "tensor", pairs)


def call(kernel, out_shape, scalars=0, grid=(), in_specs=None, out_specs=None, scratch=(),
         flops=0, moved=0):
    return pl.pallas_call(
        kernel,
        out_shape=out_shape,
        grid_spec=pltpu.PrefetchScalarGridSpec(
            num_scalar_prefetch=scalars,
            grid=grid,
            in_specs=in_specs,
            out_specs=out_specs,
            scratch_shapes=list(scratch),
        ),
        cost_estimate=pl.CostEstimate(flops=flops, bytes_accessed=moved, transcendentals=0),
        compiler_params=pltpu.CompilerParams(vmem_limit_bytes=16 * 2**20),
    )


def in_hbm(array):
    return pltpu.with_memory_space_constraint(array, pltpu.HBM)


def whole(*dims):
    return pl.BlockSpec(dims, lambda *ids: (0,) * len(dims))


def first_kernel(where, tokens, weight, down, head, keep, give, gram, lines):
    rank = down.shape[1]
    count = tokens.shape[1]

    @pl.when(pl.program_id(0) == 0)
    def _():
        mine = down[0]
        lines[:count] = tokens[...].T
        lines[count:] = mine
        square = dot(mine, mine, 1, 1)
        tile = (iota((rank, LANES), 1) % rank == iota((rank, LANES), 0)).astype(BF16)
        spread = dot(square.astype(BF16), tile, 1, 0)
        rows, cols = iota((rank, LANES), 0), iota((rank, LANES), 1)
        spread = jnp.where(cols // rank == rows % 8, spread, 0.0)
        gram[0:1, :] = jnp.sum(spread[:8], axis=0, keepdims=True)
        gram[1:2, :] = jnp.sum(spread[8:], axis=0, keepdims=True)

    share = 32
    pieces = weight.shape[0] // share
    start = pl.multiple_of(jnp.minimum(where[0], pieces - 1) * share, share)
    mine = (where[0] < pieces).astype(F32)
    row = iota((8, LANES), 0)
    swap = where[1] != 0
    step = 8 * LANES
    for block in range(0, weight.shape[1], step):
        columns = slice(block, block + step)
        both = dot(lines[...], weight[:, columns], 1, 0)
        part = weight[pl.ds(start, share), columns].astype(F32)
        squares = jnp.sum(part * part, axis=0, keepdims=True) * mine
        for k in range(step // LANES):
            lanes = slice(k * LANES, (k + 1) * LANES)
            tail = jnp.where(
                row == 0,
                squares[:, lanes],
                jnp.where(row == 1, gram[0:1, :], jnp.where(row == 2, gram[1:2, :], 0.0)),
            )
            head[block // LANES + k] = jnp.concatenate([both[count:, lanes], tail], 0).astype(BF16)
        for k in range(step // LANES // 2):
            even = both[:count, 2 * k * LANES : (2 * k + 1) * LANES]
            odd = both[:count, (2 * k + 1) * LANES : (2 * k + 2) * LANES]
            at = block // LANES // 2 + k
            keep[at] = jnp.where(swap, odd, even).astype(BF16)
            give[at] = jnp.where(swap, even, odd).astype(BF16)


def low_kernel(where, seg, tokens, down, low):
    marks = bounds(seg, seg.shape[0], where[0] * tokens.shape[1])
    spread = dot(down[...], tokens[...], 1, 0)
    low[...] = packed(picked(spread, marks)).astype(BF16)


def halves_kernel(where, keep_a, got_a, keep_b, got_b, keep, give):
    keep[...] = (keep_a[...].astype(F32) + got_a[...].astype(F32)).astype(BF16)
    give[...] = (keep_b[...].astype(F32) + got_b[...].astype(F32)).astype(BF16)


def squares_kernel(where, head, up, second):
    rank = up.shape[1]
    total = jnp.sum(head[...].astype(F32), axis=0)
    factor = up[0].astype(F32)
    rows, cols = iota((rank, LANES), 0), iota((rank, LANES), 1)
    spread = jnp.where(rows < 8, total[rank + 1 : rank + 2], total[rank + 2 : rank + 3])
    spread = jnp.where(cols // rank == rows % 8, spread, 0.0)
    tiled = jnp.concatenate([up[0]] * (LANES // rank), axis=0)
    high = spread.astype(BF16)
    rest = (spread - high.astype(F32)).astype(BF16)
    gram_up = dot(high, tiled, 1, 0) + dot(rest, tiled, 1, 0)
    mine = jnp.sum(factor * (2.0 * total[:rank] + gram_up), axis=0, keepdims=True)
    both = jnp.concatenate([mine, total[rank : rank + 1]], axis=0)
    second[...] = jnp.broadcast_to(both[None], second.shape)


def lift_kernel(where, keep, got, up, down, near):
    count = keep.shape[0]
    for out, steps in ((up, (1, 4, -2)), (down, (-1, 2)), (near, (0, 3, -3))):
        for i, step in enumerate(steps):
            at = (where[3] + step + count) % count
            out[i] = (keep[at].astype(F32) + got[at].astype(F32)).astype(BF16)


def scale_kernel(where, seg, second, magnitude, cotangent, up, low, scaled, third, norms):
    count = cotangent.shape[0]
    marks = bounds(seg, seg.shape[0], where[0] * count)
    parts = second[...]
    squares = parts[:, 0, :] + jnp.sum(parts[:, 1, :], axis=0, keepdims=True)
    col_norms = jnp.sqrt(jnp.maximum(squares, 0.0) + EPSILON)
    norms[...] = col_norms
    scale = token_scale_of(magnitude[...].astype(F32) / col_norms, marks, count)
    grad = (cotangent[...].astype(F32) * scale).astype(BF16)
    scaled[...] = grad
    back = packed(picked(dot(up[...], grad, 1, 1), marks)).astype(BF16)
    every = jnp.concatenate([low[...], back], axis=0)
    third[...] = jnp.broadcast_to(every[None], third.shape)


def far_kernel(near, up, down, share, other, to_up, to_down, own):
    own[...] = near[0].astype(F32) + up[0].astype(F32) + down[0].astype(F32)
    to_up[0] = (near[1].astype(F32) + up[1].astype(F32) + down[1].astype(F32)).astype(BF16)
    to_down[0] = (near[2].astype(F32) + up[2].astype(F32)).astype(BF16)
    for out in (to_up, to_down):
        out[1] = share[...]
        out[2] = other[...]


def pack_kernel(share, other, below, above, before, after):
    for out in (before, after):
        out[0] = share[...]
        out[1] = other[...]
        out[2:4] = below[1:]
    after[4:6] = above[1:]


def join_kernel(after, from_below, from_above, out):
    out[:6] = after[...]
    out[6:12] = from_below[...]
    out[12:] = from_above[...]


def sums_kernel(rank_rows, ranks):
    ranks[...] = jnp.sum(rank_rows[...].astype(F32), axis=0).astype(BF16)


def grads_kernel(where, seg, ranks, got, scaled, up, tokens, fourth, low_wide, back_wide):
    adapters = seg.shape[0]
    own_rows, count = tokens.shape
    rank = up.shape[0] // adapters
    marks = bounds(seg, adapters, where[0] * count)
    total = ranks[...].astype(F32) + got[...].astype(F32)
    low = widened(unpacked(total[: 2 * rank]), marks)
    back = widened(unpacked(total[2 * rank :]), marks)
    low_wide[...] = low
    back_wide[...] = back
    down_part = dot(back, tokens[...], 1, 1).astype(BF16)
    up_part = dot(low, scaled[...], 1, 0).astype(BF16)
    pad = jnp.zeros((rank, -own_rows % LANES), BF16)
    for a in range(adapters):
        lines = slice(a * rank, (a + 1) * rank)
        fourth[a] = jnp.concatenate([down_part[lines], pad, up_part[lines]], axis=1)


def hidden_kernel(where, seg, base, base_a, base_b, low, up, norms, magnitude, cotangent,
                  projected, mag):
    count = cotangent.shape[0]
    marks = bounds(seg, seg.shape[0], where[0] * count)
    hidden = base[...] + base_a[0].astype(F32) + base_b[0].astype(F32)
    hidden = hidden + dot(low[...], up[...], 0, 0)
    scale = token_scale_of(magnitude[...].astype(F32) / norms[...], marks, count)
    projected[...] = (hidden * scale).astype(BF16)
    weighted = cotangent[...].astype(F32) * hidden
    at = iota((count, LANES), 0)
    sums = [
        jnp.sum(jnp.where((at >= lo) & (at < hi), weighted, 0.0), axis=0, keepdims=True)
        for lo, hi in marks
    ]
    mag[...] = jnp.concatenate(sums, axis=0).astype(BF16)


def total_kernel(arrived, mag, fifth):
    total = jnp.sum(arrived[...].astype(F32), axis=0).astype(BF16)
    both = jnp.concatenate([total, mag[...]], axis=1)
    fifth[...] = jnp.broadcast_to(both[None], fifth.shape)


def final_kernel(fifth, norms, grad_down, grad_up, grad_magnitude):
    own_rows = grad_down.shape[2]
    edge = own_rows + -own_rows % LANES
    grad_down[...] = fifth[:, :, :own_rows]
    grad_up[...] = fifth[:, :, edge : edge + LANES].astype(F32)
    total = jnp.sum(fifth[:, :, edge + LANES :].astype(F32), axis=0)
    grad_magnitude[...] = total / norms[...]


def tokens_kernel(where, blocks, *rest):
    *columns, first, second, out, total = rest
    step = pl.program_id(0)

    @pl.when(step == 0)
    def _():
        total[...] = dot(first[...], second[...], 0, 0)

    left = [blocks[i] for i in range(blocks.shape[0])]
    right = [column[...] for column in columns]
    total[...] += dot(jnp.concatenate(right, axis=1), jnp.concatenate(left, axis=1), 1, 1)

    @pl.when(step == pl.num_programs(0) - 1)
    def _():
        out[...] = total[...]


def tokens_rest_kernel(where, blocks, *rest):
    *columns, part, out, total = rest
    step = pl.program_id(0)

    @pl.when(step == 0)
    def _():
        total[...] = part[...]

    left = [blocks[i] for i in range(blocks.shape[0])]
    right = [column[...] for column in columns]
    total[...] += dot(jnp.concatenate(right, axis=1), jnp.concatenate(left, axis=1), 1, 1)

    @pl.when(step == pl.num_programs(0) - 1)
    def _():
        out[...] = total[...].astype(BF16)


def exchange(blocks, axis, groups=None):
    return lax.all_to_all(blocks, axis, 0, 0, tiled=True, axis_index_groups=groups)


def local(tokens, base_weight, adapter_down, adapter_up, magnitude, seg_lengths, cotangent):
    count, own_rows = tokens.shape
    adapters, _, rank = adapter_down.shape
    width = adapter_up.shape[2]
    full = base_weight.shape[1]
    size = full // width
    zs = size // 4
    wide = adapters * rank
    me_dp = lax.axis_index("dp")
    me = lax.axis_index("tensor")
    core, hi = me % 2, me // (2 * zs)
    z = (me // 2) % zs
    where = jnp.stack([me_dp, core, hi, z]).astype(I32)
    core_pairs = [(i, i ^ 1) for i in range(size)]
    hi_pairs = [(i, (i + size // 2) % size) for i in range(size)]

    turned = tokens.T
    core_groups = [list(range(c, size, 2)) for c in range(2)]
    down_rows = jnp.transpose(adapter_down, (0, 2, 1))
    down_flat = down_rows.reshape(wide, own_rows)
    up_own = adapter_up.reshape(wide, width)

    head, keep, give = call(
        first_kernel,
        [
            shaped(size, HEAD, width),
            shaped(size // 2, count, width),
            pltpu.HBM((size // 2, count, width), BF16),
        ],
        scalars=1,
        grid=(2,),
        in_specs=[
            whole(own_rows, count),
            pl.BlockSpec((own_rows, full // 2), lambda i, s: (0, i)),
            pl.BlockSpec((1, rank, own_rows), lambda i, s: (s[0], 0, 0)),
        ],
        out_specs=[
            pl.BlockSpec((size // 2, HEAD, width), lambda i, s: (i, 0, 0)),
            pl.BlockSpec((size // 4, count, width), lambda i, s: (i, 0, 0)),
            pl.BlockSpec((size // 4, count, width), lambda i, s: (i, 0, 0)),
        ],
        scratch=[pltpu.VMEM((8, width), F32), pltpu.VMEM((count + rank, own_rows), BF16)],
        flops=2 * count * own_rows * full,
        moved=2 * own_rows * full,
    )(where, in_hbm(turned), in_hbm(base_weight), in_hbm(down_rows))
    head = exchange(head, "tensor")
    got = shift(give, core_pairs)
    low = call(
        low_kernel,
        shaped(2 * rank, width),
        scalars=2,
        grid=(1,),
        in_specs=[whole(own_rows, count), whole(wide, own_rows)],
        out_specs=whole(2 * rank, width),
        flops=2 * count * own_rows * wide,
        moved=4 * count * own_rows,
    )(where, seg_lengths, turned, down_flat)

    mine = pl.BlockSpec((2, count, width), lambda i, s: (s[2] * (zs // 2) + i, 0, 0))
    theirs = pl.BlockSpec((2, count, width), lambda i, s: ((1 - s[2]) * (zs // 2) + i, 0, 0))
    out = pl.BlockSpec((2, count, width), lambda i, s: (i, 0, 0))
    keep, give = call(
        halves_kernel,
        [shaped(zs, count, width)] * 2,
        scalars=1,
        grid=(zs // 2,),
        in_specs=[mine, mine, theirs, theirs],
        out_specs=[out, out],
        moved=12 * zs * count * width,
    )(where, keep, got, keep, got)
    got = shift(give, hi_pairs)

    def along_z(step):
        return [
            (h * 2 * zs + a * 2 + c, h * 2 * zs + (a + step) % zs * 2 + c)
            for h in range(2)
            for a in range(zs)
            for c in range(2)
        ]

    second = call(
        squares_kernel,
        shaped(adapters, 2, width, dtype=F32),
        scalars=1,
        grid=(1,),
        in_specs=[
            whole(size, HEAD, width),
            pl.BlockSpec((1, rank, width), lambda i, s: (s[0], 0, 0)),
        ],
        out_specs=whole(adapters, 2, width),
        moved=2 * size * HEAD * width,
    )(where, head, adapter_up)
    second = exchange(second, "dp")

    up3, down2, near = call(
        lift_kernel,
        [shaped(n, count, width) for n in (3, 2, 3)],
        scalars=1,
        grid=(1,),
        in_specs=[whole(zs, count, width)] * 2,
        out_specs=[whole(n, count, width) for n in (3, 2, 3)],
        moved=6 * zs * count * width,
    )(where, keep, got)
    up3 = shift(up3, along_z(1))
    down2 = shift(down2, along_z(-1))

    share, third, norms = call(
        scale_kernel,
        [
            shaped(count, width),
            shaped(2 * zs, 4 * rank, width),
            shaped(adapters, width, dtype=F32),
        ],
        scalars=2,
        grid=(1,),
        in_specs=[
            whole(adapters, 2, width),
            whole(adapters, width),
            whole(count, width),
            whole(wide, width),
            whole(2 * rank, width),
        ],
        out_specs=[
            whole(count, width),
            whole(2 * zs, 4 * rank, width),
            whole(adapters, width),
        ],
        flops=2 * count * wide * width,
        moved=8 * count * width,
    )(where, seg_lengths, second, magnitude, cotangent, up_own, low)
    third = exchange(third, "tensor", core_groups)
    other = shift(share, hi_pairs)
    scaled = whole(count, width)
    to_up, to_down, base = call(
        far_kernel,
        [shaped(3, count, width), shaped(3, count, width), shaped(count, width, dtype=F32)],
        grid=(1,),
        in_specs=[whole(n, count, width) for n in (3, 3, 2)] + [scaled] * 2,
        out_specs=[whole(3, count, width), whole(3, count, width), whole(count, width)],
        moved=36 * count * width,
    )(near, up3, down2, share, other)
    below = shift(to_up, along_z(3))
    above = shift(to_down, along_z(-3))
    ranks = call(
        sums_kernel,
        shaped(4 * rank, width),
        grid=(1,),
        in_specs=[whole(2 * zs, 4 * rank, width)],
        out_specs=whole(4 * rank, width),
        moved=2 * zs * 4 * rank * width,
    )(third)
    other_ranks = shift(ranks, core_pairs)

    before, after = call(
        pack_kernel,
        [shaped(4, count, width), shaped(6, count, width)],
        grid=(1,),
        in_specs=[scaled] * 2 + [whole(3, count, width)] * 2,
        out_specs=[whole(4, count, width), whole(6, count, width)],
        moved=32 * count * width,
    )(share, other, below, above)
    from_below = shift(after, along_z(1))
    from_above = shift(before, along_z(-1))
    gather_a = call(
        join_kernel,
        shaped(2 * zs, count, width),
        grid=(1,),
        in_specs=[whole(n, count, width) for n in (6, 6, 4)],
        out_specs=whole(2 * zs, count, width),
        moved=8 * zs * count * width,
    )(after, from_below, from_above)
    gather_b = shift(gather_a, core_pairs)

    edge = own_rows + -own_rows % LANES
    blocks = edge + width
    fourth, low_wide, back_wide = call(
        grads_kernel,
        [shaped(adapters, rank, blocks), shaped(wide, count), shaped(wide, count)],
        scalars=2,
        grid=(1,),
        in_specs=[
            whole(4 * rank, width),
            whole(4 * rank, width),
            whole(count, width),
            whole(wide, width),
            whole(own_rows, count),
        ],
        out_specs=[whole(adapters, rank, blocks), whole(wide, count), whole(wide, count)],
        flops=2 * count * wide * (own_rows + width),
        moved=4 * adapters * rank * blocks,
    )(where, seg_lengths, ranks, other_ranks, share, up_own, turned)
    fourth = exchange(fourth, "dp")

    first_block = pl.BlockSpec((1, count, width), lambda i, *s: (0, 0, 0))
    projected, mag = call(
        hidden_kernel,
        [shaped(count, width), shaped(adapters, width)],
        scalars=2,
        grid=(1,),
        in_specs=[
            whole(count, width),
            first_block,
            first_block,
            whole(wide, count),
            whole(wide, width),
            whole(adapters, width),
            whole(adapters, width),
            whole(count, width),
        ],
        out_specs=[whole(count, width), whole(adapters, width)],
        flops=2 * count * wide * width,
        moved=16 * count * width,
    )(where, seg_lengths, base, below, above, low_wide, up_own, norms, magnitude,
      cotangent)

    fifth = call(
        total_kernel,
        shaped(adapters, rank, blocks + width),
        grid=(1,),
        in_specs=[whole(adapters, rank, blocks), whole(adapters, width)],
        out_specs=whole(adapters, rank, blocks + width),
        moved=4 * adapters * rank * blocks,
    )(fourth, mag)
    fifth = exchange(fifth, "dp")

    per = 4
    offsets = (0, -3, 3, -1, -4, 2, 1, -2)

    def column(k, x_bit, c_bit):
        def at(i, s):
            off = jnp.where(i == 0, offsets[k], offsets[per + k])
            block = (s[3] + off + zs) % zs
            return (0, (s[2] ^ x_bit) * (2 * zs) + block * 2 + (s[1] ^ c_bit))

        return pl.BlockSpec((own_rows, width), at)

    def columns(c_bit):
        return [column(k, x, c_bit) for k in range(per) for x in range(2)]

    block = pl.BlockSpec((2 * per, count, width), lambda i, s: (i, 0, 0))
    weights = [in_hbm(base_weight)] * (2 * per)
    part = call(
        tokens_kernel,
        shaped(own_rows, count, dtype=F32),
        scalars=1,
        grid=(zs // per,),
        in_specs=[block] + columns(0) + [whole(wide, own_rows), whole(wide, count)],
        out_specs=whole(own_rows, count),
        scratch=[pltpu.VMEM((own_rows, count), F32)],
        flops=count * own_rows * (full + 2 * wide),
        moved=own_rows * full,
    )(where, gather_a, *weights, down_flat, back_wide)
    grad_tokens = call(
        tokens_rest_kernel,
        shaped(own_rows, count),
        scalars=1,
        grid=(zs // per,),
        in_specs=[block] + columns(1) + [whole(own_rows, count)],
        out_specs=whole(own_rows, count),
        scratch=[pltpu.VMEM((own_rows, count), F32)],
        flops=count * own_rows * full,
        moved=own_rows * full,
    )(where, gather_b, *weights, part)

    grad_down, grad_up, grad_magnitude = call(
        final_kernel,
        [
            shaped(adapters, rank, own_rows),
            shaped(adapters, rank, width, dtype=F32),
            shaped(adapters, width, dtype=F32),
        ],
        grid=(1,),
        in_specs=[whole(adapters, rank, blocks + width), whole(adapters, width)],
        out_specs=[
            whole(adapters, rank, own_rows),
            whole(adapters, rank, width),
            whole(adapters, width),
        ],
        moved=4 * adapters * rank * blocks,
    )(fifth, norms)
    return (projected, grad_tokens.T, jnp.transpose(grad_down, (0, 2, 1)), grad_up, grad_magnitude)


def solution(mesh):
    placed = (
        P("dp", "tensor"),
        P("tensor", None),
        P(None, "tensor", None),
        P(None, None, "tensor"),
        P(None, "tensor"),
        P(),
        P("dp", "tensor"),
    )
    return jax.shard_map(
        local,
        mesh=mesh,
        in_specs=placed,
        out_specs=(
            P("dp", "tensor"),
            P("dp", "tensor"),
            P(None, "tensor", None),
            P(None, None, "tensor"),
            P(None, "tensor"),
        ),
        check_vma=False,
    )
```

```python
import jax
import jax.numpy as jnp
from jax import lax
from jax.experimental import pallas as pl
from jax.experimental.pallas import tpu as pltpu
from jax.sharding import PartitionSpec as P


EPSILON = 1e-06
F32 = jnp.float32
BF16 = jnp.bfloat16
I32 = jnp.int32
LANES = 128
HEAD = 24


def dot(a, b, ca, cb, precision=None):
    return lax.dot_general(
        a, b, (((ca,), (cb,)), ((), ())), precision=precision, preferred_element_type=F32
    )


def iota(shape, dim):
    return lax.broadcasted_iota(I32, shape, dim)


def shaped(*dims, dtype=BF16):
    return jax.ShapeDtypeStruct(dims, dtype)


def bounds(seg, adapters, first_token):
    marks, at = [], -first_token
    for a in range(adapters):
        marks.append((at, at + seg[a]))
        at = at + seg[a]
    return marks


def picked(spread, marks):
    rank = spread.shape[0] // len(marks)
    at = iota((rank, spread.shape[1]), 1)
    total = jnp.zeros((rank, spread.shape[1]), F32)
    for a, (lo, hi) in enumerate(marks):
        total += jnp.where((at >= lo) & (at < hi), spread[a * rank : (a + 1) * rank], 0.0)
    return total


def widened(rank_rows, marks):
    at = iota(rank_rows.shape, 1)
    wide = [jnp.where((at >= lo) & (at < hi), rank_rows, 0.0) for lo, hi in marks]
    return jnp.concatenate(wide, axis=0).astype(BF16)


def packed(rows):
    return jnp.concatenate([rows[:, :LANES], rows[:, LANES:]], axis=0)


def unpacked(rows):
    half = rows.shape[0] // 2
    return jnp.concatenate([rows[:half], rows[half:]], axis=1)


def token_scale_of(col_scale, marks, token_count):
    at = iota((token_count, LANES), 0)
    total = jnp.zeros((token_count, LANES), F32)
    for a, (lo, hi) in enumerate(marks):
        total += jnp.where((at >= lo) & (at < hi), col_scale[a : a + 1], 0.0)
    return total


def shift(block, pairs):
    return lax.ppermute(block, "tensor", pairs)


def call(kernel, out_shape, scalars=0, grid=(), in_specs=None, out_specs=None, scratch=(),
         flops=0, moved=0):
    return pl.pallas_call(
        kernel,
        out_shape=out_shape,
        grid_spec=pltpu.PrefetchScalarGridSpec(
            num_scalar_prefetch=scalars,
            grid=grid,
            in_specs=in_specs,
            out_specs=out_specs,
            scratch_shapes=list(scratch),
        ),
        cost_estimate=pl.CostEstimate(flops=flops, bytes_accessed=moved, transcendentals=0),
        compiler_params=pltpu.CompilerParams(vmem_limit_bytes=16 * 2**20),
    )


def in_hbm(array):
    return pltpu.with_memory_space_constraint(array, pltpu.HBM)


def whole(*dims):
    return pl.BlockSpec(dims, lambda *ids: (0,) * len(dims))


def first_kernel(where, tokens, weight, down, head, keep, give, gram, lines):
    rank = down.shape[1]
    count = tokens.shape[1]

    @pl.when(pl.program_id(0) == 0)
    def _():
        mine = down[0]
        lines[:count] = tokens[...].T
        lines[count:] = mine
        square = dot(mine, mine, 1, 1)
        tile = (iota((rank, LANES), 1) % rank == iota((rank, LANES), 0)).astype(BF16)
        spread = dot(square.astype(BF16), tile, 1, 0)
        rows, cols = iota((rank, LANES), 0), iota((rank, LANES), 1)
        spread = jnp.where(cols // rank == rows % 8, spread, 0.0)
        gram[0:1, :] = jnp.sum(spread[:8], axis=0, keepdims=True)
        gram[1:2, :] = jnp.sum(spread[8:], axis=0, keepdims=True)

    share = 32
    pieces = weight.shape[0] // share
    start = pl.multiple_of(jnp.minimum(where[0], pieces - 1) * share, share)
    mine = (where[0] < pieces).astype(F32)
    row = iota((8, LANES), 0)
    swap = where[1] != 0
    step = 8 * LANES
    for block in range(0, weight.shape[1], step):
        columns = slice(block, block + step)
        both = dot(lines[...], weight[:, columns], 1, 0)
        part = weight[pl.ds(start, share), columns].astype(F32)
        squares = jnp.sum(part * part, axis=0, keepdims=True) * mine
        for k in range(step // LANES):
            lanes = slice(k * LANES, (k + 1) * LANES)
            tail = jnp.where(
                row == 0,
                squares[:, lanes],
                jnp.where(row == 1, gram[0:1, :], jnp.where(row == 2, gram[1:2, :], 0.0)),
            )
            head[block // LANES + k] = jnp.concatenate([both[count:, lanes], tail], 0).astype(BF16)
        for k in range(step // LANES // 2):
            even = both[:count, 2 * k * LANES : (2 * k + 1) * LANES]
            odd = both[:count, (2 * k + 1) * LANES : (2 * k + 2) * LANES]
            at = block // LANES // 2 + k
            keep[at] = jnp.where(swap, odd, even).astype(BF16)
            give[at] = jnp.where(swap, even, odd).astype(BF16)


def halves_kernel(where, seg, tokens, down, keep_a, got_a, keep_b, got_b, low, keep, give):
    keep[...] = (keep_a[...].astype(F32) + got_a[...].astype(F32)).astype(BF16)
    give[...] = (keep_b[...].astype(F32) + got_b[...].astype(F32)).astype(BF16)

    @pl.when(pl.program_id(0) == 0)
    def _():
        marks = bounds(seg, seg.shape[0], where[0] * tokens.shape[1])
        spread = dot(down[...], tokens[...], 1, 0)
        low[...] = packed(picked(spread, marks)).astype(BF16)


def squares_kernel(where, head, up, second):
    rank = up.shape[1]
    total = jnp.sum(head[...].astype(F32), axis=0)
    factor = up[0].astype(F32)
    rows, cols = iota((rank, LANES), 0), iota((rank, LANES), 1)
    spread = jnp.where(rows < 8, total[rank + 1 : rank + 2], total[rank + 2 : rank + 3])
    spread = jnp.where(cols // rank == rows % 8, spread, 0.0)
    tiled = jnp.concatenate([up[0]] * (LANES // rank), axis=0)
    high = spread.astype(BF16)
    rest = (spread - high.astype(F32)).astype(BF16)
    gram_up = dot(jnp.concatenate([high, rest], axis=0), tiled, 1, 0)
    gram_up = gram_up[:rank] + gram_up[rank:]
    mine = jnp.sum(factor * (2.0 * total[:rank] + gram_up), axis=0, keepdims=True)
    both = jnp.concatenate([mine, total[rank : rank + 1]], axis=0)
    second[...] = jnp.broadcast_to(both[None], second.shape)


def lift_kernel(where, keep, got, up, down, near):
    count = keep.shape[0]
    for out, steps in ((up, (1, 4, -2)), (down, (-1, 2)), (near, (0, 3, -3))):
        for i, step in enumerate(steps):
            at = (where[3] + step + count) % count
            out[i] = (keep[at].astype(F32) + got[at].astype(F32)).astype(BF16)


def scale_kernel(where, seg, second, magnitude, cotangent, up, low, scaled, third, norms):
    count = cotangent.shape[0]
    marks = bounds(seg, seg.shape[0], where[0] * count)
    parts = second[...]
    squares = parts[:, 0, :] + jnp.sum(parts[:, 1, :], axis=0, keepdims=True)
    col_norms = jnp.sqrt(jnp.maximum(squares, 0.0) + EPSILON)
    norms[...] = col_norms
    scale = token_scale_of(magnitude[...].astype(F32) / col_norms, marks, count)
    grad = (cotangent[...].astype(F32) * scale).astype(BF16)
    scaled[...] = grad
    back = packed(picked(dot(up[...], grad, 1, 1), marks)).astype(BF16)
    every = jnp.concatenate([low[...], back], axis=0)
    third[...] = jnp.broadcast_to(every[None], third.shape)


def far_kernel(near, up, down, share, other, to_up, to_down, own):
    own[...] = near[0].astype(F32) + up[0].astype(F32) + down[0].astype(F32)
    to_up[0] = (near[1].astype(F32) + up[1].astype(F32) + down[1].astype(F32)).astype(BF16)
    to_down[0] = (near[2].astype(F32) + up[2].astype(F32)).astype(BF16)
    for out in (to_up, to_down):
        out[1] = share[...]
        out[2] = other[...]


def pack_kernel(share, other, below, above, before, after):
    for out in (before, after):
        out[0] = share[...]
        out[1] = other[...]
        out[2:4] = below[1:]
    after[4:6] = above[1:]


def join_kernel(after, from_below, from_above, out):
    out[:6] = after[...]
    out[6:12] = from_below[...]
    out[12:] = from_above[...]


def sums_kernel(rank_rows, ranks):
    ranks[...] = jnp.sum(rank_rows[...].astype(F32), axis=0).astype(BF16)


def grads_kernel(where, seg, ranks, got, scaled, up, tokens, fourth, low_wide, back_wide):
    adapters = seg.shape[0]
    own_rows, count = tokens.shape
    rank = up.shape[0] // adapters
    marks = bounds(seg, adapters, where[0] * count)
    total = ranks[...].astype(F32) + got[...].astype(F32)
    low = widened(unpacked(total[: 2 * rank]), marks)
    back = widened(unpacked(total[2 * rank :]), marks)
    low_wide[...] = low
    back_wide[...] = back
    down_part = dot(back, tokens[...], 1, 1).astype(BF16)
    up_part = dot(low, scaled[...], 1, 0).astype(BF16)
    pad = jnp.zeros((rank, -own_rows % LANES), BF16)
    for a in range(adapters):
        lines = slice(a * rank, (a + 1) * rank)
        fourth[a] = jnp.concatenate([down_part[lines], pad, up_part[lines]], axis=1)


def hidden_kernel(where, seg, base, base_a, base_b, low, up, norms, magnitude, cotangent,
                  projected, mag):
    count = cotangent.shape[0]
    marks = bounds(seg, seg.shape[0], where[0] * count)
    hidden = base[...] + base_a[0].astype(F32) + base_b[0].astype(F32)
    hidden = hidden + dot(low[...], up[...], 0, 0)
    scale = token_scale_of(magnitude[...].astype(F32) / norms[...], marks, count)
    projected[...] = (hidden * scale).astype(BF16)
    weighted = cotangent[...].astype(F32) * hidden
    at = iota((count, LANES), 0)
    sums = [
        jnp.sum(jnp.where((at >= lo) & (at < hi), weighted, 0.0), axis=0, keepdims=True)
        for lo, hi in marks
    ]
    mag[...] = jnp.concatenate(sums, axis=0).astype(BF16)


def total_kernel(arrived, mag, fifth):
    total = jnp.sum(arrived[...].astype(F32), axis=0).astype(BF16)
    both = jnp.concatenate([total, mag[...]], axis=1)
    fifth[...] = jnp.broadcast_to(both[None], fifth.shape)


def final_kernel(fifth, norms, grad_down, grad_up, grad_magnitude):
    own_rows = grad_down.shape[2]
    edge = own_rows + -own_rows % LANES
    grad_down[...] = fifth[:, :, :own_rows]
    grad_up[...] = fifth[:, :, edge : edge + LANES].astype(F32)
    total = jnp.sum(fifth[:, :, edge + LANES :].astype(F32), axis=0)
    grad_magnitude[...] = total / norms[...]


def tokens_kernel(where, blocks, *rest):
    *columns, first, second, out, total = rest
    step = pl.program_id(0)

    @pl.when(step == 0)
    def _():
        total[...] = dot(first[...], second[...], 0, 0)

    left = [blocks[i] for i in range(blocks.shape[0])]
    right = [column[...] for column in columns]
    total[...] += dot(jnp.concatenate(right, axis=1), jnp.concatenate(left, axis=1), 1, 1)

    @pl.when(step == pl.num_programs(0) - 1)
    def _():
        out[...] = total[...]


def tokens_rest_kernel(where, blocks, *rest):
    *columns, part, out, total = rest
    step = pl.program_id(0)

    @pl.when(step == 0)
    def _():
        total[...] = part[...]

    left = [blocks[i] for i in range(blocks.shape[0])]
    right = [column[...] for column in columns]
    total[...] += dot(jnp.concatenate(right, axis=1), jnp.concatenate(left, axis=1), 1, 1)

    @pl.when(step == pl.num_programs(0) - 1)
    def _():
        out[...] = total[...].astype(BF16)


def exchange(blocks, axis, groups=None):
    return lax.all_to_all(blocks, axis, 0, 0, tiled=True, axis_index_groups=groups)


def local(tokens, base_weight, adapter_down, adapter_up, magnitude, seg_lengths, cotangent):
    count, own_rows = tokens.shape
    adapters, _, rank = adapter_down.shape
    width = adapter_up.shape[2]
    full = base_weight.shape[1]
    size = full // width
    zs = size // 4
    wide = adapters * rank
    me_dp = lax.axis_index("dp")
    me = lax.axis_index("tensor")
    core, hi = me % 2, me // (2 * zs)
    z = (me // 2) % zs
    where = jnp.stack([me_dp, core, hi, z]).astype(I32)
    core_pairs = [(i, i ^ 1) for i in range(size)]
    hi_pairs = [(i, (i + size // 2) % size) for i in range(size)]

    turned = tokens.T
    core_groups = [list(range(c, size, 2)) for c in range(2)]
    down_rows = jnp.transpose(adapter_down, (0, 2, 1))
    down_flat = down_rows.reshape(wide, own_rows)
    up_own = adapter_up.reshape(wide, width)

    head, keep, give = call(
        first_kernel,
        [
            shaped(size, HEAD, width),
            shaped(size // 2, count, width),
            pltpu.HBM((size // 2, count, width), BF16),
        ],
        scalars=1,
        grid=(2,),
        in_specs=[
            whole(own_rows, count),
            pl.BlockSpec((own_rows, full // 2), lambda i, s: (0, i)),
            pl.BlockSpec((1, rank, own_rows), lambda i, s: (s[0], 0, 0)),
        ],
        out_specs=[
            pl.BlockSpec((size // 2, HEAD, width), lambda i, s: (i, 0, 0)),
            pl.BlockSpec((size // 4, count, width), lambda i, s: (i, 0, 0)),
            pl.BlockSpec((size // 4, count, width), lambda i, s: (i, 0, 0)),
        ],
        scratch=[pltpu.VMEM((8, width), F32), pltpu.VMEM((count + rank, own_rows), BF16)],
        flops=2 * count * own_rows * full,
        moved=2 * own_rows * full,
    )(where, in_hbm(turned), in_hbm(base_weight), in_hbm(down_rows))
    head = exchange(head, "tensor")
    got = shift(give, core_pairs)
    half = size // 4
    mine = pl.BlockSpec((half // 2, count, width), lambda i, s, t: (s[2] * 2 + i, 0, 0))
    theirs = pl.BlockSpec((half // 2, count, width), lambda i, s, t: ((1 - s[2]) * 2 + i, 0, 0))
    out = pl.BlockSpec((half // 2, count, width), lambda i, s, t: (i, 0, 0))
    low, keep, give = call(
        halves_kernel,
        [shaped(2 * rank, width), shaped(zs, count, width), shaped(zs, count, width)],
        scalars=2,
        grid=(2,),
        in_specs=[whole(own_rows, count), whole(wide, own_rows), mine, mine, theirs, theirs],
        out_specs=[whole(2 * rank, width), out, out],
        flops=2 * count * own_rows * wide,
        moved=12 * zs * count * width,
    )(where, seg_lengths, turned, down_flat, keep, got, keep, got)
    got = shift(give, hi_pairs)

    def along_z(step):
        return [
            (h * 2 * zs + a * 2 + c, h * 2 * zs + (a + step) % zs * 2 + c)
            for h in range(2)
            for a in range(zs)
            for c in range(2)
        ]

    second = call(
        squares_kernel,
        shaped(adapters, 2, width, dtype=F32),
        scalars=1,
        grid=(1,),
        in_specs=[
            whole(size, HEAD, width),
            pl.BlockSpec((1, rank, width), lambda i, s: (s[0], 0, 0)),
        ],
        out_specs=whole(adapters, 2, width),
        moved=2 * size * HEAD * width,
    )(where, head, adapter_up)
    second = exchange(second, "dp")

    up3, down2, near = call(
        lift_kernel,
        [shaped(n, count, width) for n in (3, 2, 3)],
        scalars=1,
        grid=(1,),
        in_specs=[whole(zs, count, width)] * 2,
        out_specs=[whole(n, count, width) for n in (3, 2, 3)],
        moved=6 * zs * count * width,
    )(where, keep, got)
    up3 = shift(up3, along_z(1))
    down2 = shift(down2, along_z(-1))

    share, third, norms = call(
        scale_kernel,
        [
            shaped(count, width),
            shaped(2 * zs, 4 * rank, width),
            shaped(adapters, width, dtype=F32),
        ],
        scalars=2,
        grid=(1,),
        in_specs=[
            whole(adapters, 2, width),
            whole(adapters, width),
            whole(count, width),
            whole(wide, width),
            whole(2 * rank, width),
        ],
        out_specs=[
            whole(count, width),
            whole(2 * zs, 4 * rank, width),
            whole(adapters, width),
        ],
        flops=2 * count * wide * width,
        moved=8 * count * width,
    )(where, seg_lengths, second, magnitude, cotangent, up_own, low)
    third = exchange(third, "tensor", core_groups)
    other = shift(share, hi_pairs)
    scaled = whole(count, width)
    to_up, to_down, base = call(
        far_kernel,
        [shaped(3, count, width), shaped(3, count, width), shaped(count, width, dtype=F32)],
        grid=(1,),
        in_specs=[whole(n, count, width) for n in (3, 3, 2)] + [scaled] * 2,
        out_specs=[whole(3, count, width), whole(3, count, width), whole(count, width)],
        moved=36 * count * width,
    )(near, up3, down2, share, other)
    below = shift(to_up, along_z(3))
    above = shift(to_down, along_z(-3))
    ranks = call(
        sums_kernel,
        shaped(4 * rank, width),
        grid=(1,),
        in_specs=[whole(2 * zs, 4 * rank, width)],
        out_specs=whole(4 * rank, width),
        moved=2 * zs * 4 * rank * width,
    )(third)
    other_ranks = shift(ranks, core_pairs)

    before, after = call(
        pack_kernel,
        [shaped(4, count, width), shaped(6, count, width)],
        grid=(1,),
        in_specs=[scaled] * 2 + [whole(3, count, width)] * 2,
        out_specs=[whole(4, count, width), whole(6, count, width)],
        moved=32 * count * width,
    )(share, other, below, above)
    from_below = shift(after, along_z(1))
    from_above = shift(before, along_z(-1))
    gather_a = call(
        join_kernel,
        shaped(2 * zs, count, width),
        grid=(1,),
        in_specs=[whole(n, count, width) for n in (6, 6, 4)],
        out_specs=whole(2 * zs, count, width),
        moved=8 * zs * count * width,
    )(after, from_below, from_above)
    gather_b = shift(gather_a, core_pairs)

    edge = own_rows + -own_rows % LANES
    blocks = edge + width
    fourth, low_wide, back_wide = call(
        grads_kernel,
        [shaped(adapters, rank, blocks), shaped(wide, count), shaped(wide, count)],
        scalars=2,
        grid=(1,),
        in_specs=[
            whole(4 * rank, width),
            whole(4 * rank, width),
            whole(count, width),
            whole(wide, width),
            whole(own_rows, count),
        ],
        out_specs=[whole(adapters, rank, blocks), whole(wide, count), whole(wide, count)],
        flops=2 * count * wide * (own_rows + width),
        moved=4 * adapters * rank * blocks,
    )(where, seg_lengths, ranks, other_ranks, share, up_own, turned)
    fourth = exchange(fourth, "dp")

    first_block = pl.BlockSpec((1, count, width), lambda i, *s: (0, 0, 0))
    projected, mag = call(
        hidden_kernel,
        [shaped(count, width), shaped(adapters, width)],
        scalars=2,
        grid=(1,),
        in_specs=[
            whole(count, width),
            first_block,
            first_block,
            whole(wide, count),
            whole(wide, width),
            whole(adapters, width),
            whole(adapters, width),
            whole(count, width),
        ],
        out_specs=[whole(count, width), whole(adapters, width)],
        flops=2 * count * wide * width,
        moved=16 * count * width,
    )(where, seg_lengths, base, below, above, low_wide, up_own, norms, magnitude,
      cotangent)

    fifth = call(
        total_kernel,
        shaped(adapters, rank, blocks + width),
        grid=(1,),
        in_specs=[whole(adapters, rank, blocks), whole(adapters, width)],
        out_specs=whole(adapters, rank, blocks + width),
        moved=4 * adapters * rank * blocks,
    )(fourth, mag)
    fifth = exchange(fifth, "dp")

    per = 4
    offsets = (0, -3, 3, -1, -4, 2, 1, -2)

    def column(k, x_bit, c_bit):
        def at(i, s):
            off = jnp.where(i == 0, offsets[k], offsets[per + k])
            block = (s[3] + off + zs) % zs
            return (0, (s[2] ^ x_bit) * (2 * zs) + block * 2 + (s[1] ^ c_bit))

        return pl.BlockSpec((own_rows, width), at)

    def columns(c_bit):
        return [column(k, x, c_bit) for k in range(per) for x in range(2)]

    block = pl.BlockSpec((2 * per, count, width), lambda i, s: (i, 0, 0))
    weights = [in_hbm(base_weight)] * (2 * per)
    part = call(
        tokens_kernel,
        shaped(own_rows, count, dtype=F32),
        scalars=1,
        grid=(zs // per,),
        in_specs=[block] + columns(0) + [whole(wide, own_rows), whole(wide, count)],
        out_specs=whole(own_rows, count),
        scratch=[pltpu.VMEM((own_rows, count), F32)],
        flops=count * own_rows * (full + 2 * wide),
        moved=own_rows * full,
    )(where, gather_a, *weights, down_flat, back_wide)
    grad_tokens = call(
        tokens_rest_kernel,
        shaped(own_rows, count),
        scalars=1,
        grid=(zs // per,),
        in_specs=[block] + columns(1) + [whole(own_rows, count)],
        out_specs=whole(own_rows, count),
        scratch=[pltpu.VMEM((own_rows, count), F32)],
        flops=count * own_rows * full,
        moved=own_rows * full,
    )(where, gather_b, *weights, part)

    grad_down, grad_up, grad_magnitude = call(
        final_kernel,
        [
            shaped(adapters, rank, own_rows),
            shaped(adapters, rank, width, dtype=F32),
            shaped(adapters, width, dtype=F32),
        ],
        grid=(1,),
        in_specs=[whole(adapters, rank, blocks + width), whole(adapters, width)],
        out_specs=[
            whole(adapters, rank, own_rows),
            whole(adapters, rank, width),
            whole(adapters, width),
        ],
        moved=4 * adapters * rank * blocks,
    )(fifth, norms)
    return (projected, grad_tokens.T, jnp.transpose(grad_down, (0, 2, 1)), grad_up, grad_magnitude)


def solution(mesh):
    placed = (
        P("dp", "tensor"),
        P("tensor", None),
        P(None, "tensor", None),
        P(None, None, "tensor"),
        P(None, "tensor"),
        P(),
        P("dp", "tensor"),
    )
    return jax.shard_map(
        local,
        mesh=mesh,
        in_specs=placed,
        out_specs=(
            P("dp", "tensor"),
            P("dp", "tensor"),
            P(None, "tensor", None),
            P(None, None, "tensor"),
            P(None, "tensor"),
        ),
        check_vma=False,
    )
```

```python
import jax
import jax.numpy as jnp
from jax import lax
from jax.experimental import pallas as pl
from jax.experimental.pallas import tpu as pltpu
from jax.sharding import PartitionSpec as P


EPSILON = 1e-06
F32 = jnp.float32
BF16 = jnp.bfloat16
I32 = jnp.int32
LANES = 128
HEAD = 24


def dot(a, b, ca, cb, precision=None):
    return lax.dot_general(
        a, b, (((ca,), (cb,)), ((), ())), precision=precision, preferred_element_type=F32
    )


def iota(shape, dim):
    return lax.broadcasted_iota(I32, shape, dim)


def shaped(*dims, dtype=BF16):
    return jax.ShapeDtypeStruct(dims, dtype)


def bounds(seg, adapters, first_token):
    marks, at = [], -first_token
    for a in range(adapters):
        marks.append((at, at + seg[a]))
        at = at + seg[a]
    return marks


def picked(spread, marks):
    rank = spread.shape[0] // len(marks)
    at = iota((rank, spread.shape[1]), 1)
    total = jnp.zeros((rank, spread.shape[1]), F32)
    for a, (lo, hi) in enumerate(marks):
        total += jnp.where((at >= lo) & (at < hi), spread[a * rank : (a + 1) * rank], 0.0)
    return total


def widened(rank_rows, marks):
    at = iota(rank_rows.shape, 1)
    wide = [jnp.where((at >= lo) & (at < hi), rank_rows, 0.0) for lo, hi in marks]
    return jnp.concatenate(wide, axis=0).astype(BF16)


def packed(rows):
    return jnp.concatenate([rows[:, :LANES], rows[:, LANES:]], axis=0)


def unpacked(rows):
    half = rows.shape[0] // 2
    return jnp.concatenate([rows[:half], rows[half:]], axis=1)


def token_scale_of(col_scale, marks, token_count):
    at = iota((token_count, LANES), 0)
    total = jnp.zeros((token_count, LANES), F32)
    for a, (lo, hi) in enumerate(marks):
        total += jnp.where((at >= lo) & (at < hi), col_scale[a : a + 1], 0.0)
    return total


def shift(block, pairs):
    return lax.ppermute(block, "tensor", pairs)


def call(kernel, out_shape, scalars=0, grid=(), in_specs=None, out_specs=None, scratch=(),
         flops=0, moved=0):
    return pl.pallas_call(
        kernel,
        out_shape=out_shape,
        grid_spec=pltpu.PrefetchScalarGridSpec(
            num_scalar_prefetch=scalars,
            grid=grid,
            in_specs=in_specs,
            out_specs=out_specs,
            scratch_shapes=list(scratch),
        ),
        cost_estimate=pl.CostEstimate(flops=flops, bytes_accessed=moved, transcendentals=0),
        compiler_params=pltpu.CompilerParams(vmem_limit_bytes=16 * 2**20),
    )


def in_hbm(array):
    return pltpu.with_memory_space_constraint(array, pltpu.HBM)


def whole(*dims):
    return pl.BlockSpec(dims, lambda *ids: (0,) * len(dims))


def first_kernel(where, tokens, weight, down, head, keep, give, gram, lines):
    rank = down.shape[1]
    count = tokens.shape[1]

    @pl.when(pl.program_id(0) == 0)
    def _():
        mine = down[0]
        lines[:count] = tokens[...].T
        lines[count:] = mine
        square = dot(mine, mine, 1, 1)
        tile = (iota((rank, LANES), 1) % rank == iota((rank, LANES), 0)).astype(BF16)
        spread = dot(square.astype(BF16), tile, 1, 0)
        rows, cols = iota((rank, LANES), 0), iota((rank, LANES), 1)
        spread = jnp.where(cols // rank == rows % 8, spread, 0.0)
        gram[0:1, :] = jnp.sum(spread[:8], axis=0, keepdims=True)
        gram[1:2, :] = jnp.sum(spread[8:], axis=0, keepdims=True)

    share = 32
    pieces = weight.shape[0] // share
    start = pl.multiple_of(jnp.minimum(where[0], pieces - 1) * share, share)
    mine = (where[0] < pieces).astype(F32)
    row = iota((8, LANES), 0)
    swap = where[1] != 0
    step = 8 * LANES
    for block in range(0, weight.shape[1], step):
        columns = slice(block, block + step)
        both = dot(lines[...], weight[:, columns], 1, 0)
        part = weight[pl.ds(start, share), columns].astype(F32)
        squares = jnp.sum(part * part, axis=0, keepdims=True) * mine
        for k in range(step // LANES):
            lanes = slice(k * LANES, (k + 1) * LANES)
            tail = jnp.where(
                row == 0,
                squares[:, lanes],
                jnp.where(row == 1, gram[0:1, :], jnp.where(row == 2, gram[1:2, :], 0.0)),
            )
            head[block // LANES + k] = jnp.concatenate([both[count:, lanes], tail], 0).astype(BF16)
        for k in range(step // LANES // 2):
            even = both[:count, 2 * k * LANES : (2 * k + 1) * LANES]
            odd = both[:count, (2 * k + 1) * LANES : (2 * k + 2) * LANES]
            at = block // LANES // 2 + k
            keep[at] = jnp.where(swap, odd, even).astype(BF16)
            give[at] = jnp.where(swap, even, odd).astype(BF16)


def halves_kernel(where, seg, tokens, down, keep_a, got_a, keep_b, got_b, low, keep, give):
    keep[...] = (keep_a[...].astype(F32) + got_a[...].astype(F32)).astype(BF16)
    give[...] = (keep_b[...].astype(F32) + got_b[...].astype(F32)).astype(BF16)

    @pl.when(pl.program_id(0) == 0)
    def _():
        marks = bounds(seg, seg.shape[0], where[0] * tokens.shape[1])
        spread = dot(down[...], tokens[...], 1, 0)
        low[...] = packed(picked(spread, marks)).astype(BF16)


def squares_kernel(where, head, up, second):
    rank = up.shape[1]
    total = jnp.sum(head[...].astype(F32), axis=0)
    factor = up[0].astype(F32)
    rows, cols = iota((rank, LANES), 0), iota((rank, LANES), 1)
    spread = jnp.where(rows < 8, total[rank + 1 : rank + 2], total[rank + 2 : rank + 3])
    spread = jnp.where(cols // rank == rows % 8, spread, 0.0)
    tiled = jnp.concatenate([up[0]] * (LANES // rank), axis=0)
    high = spread.astype(BF16)
    rest = (spread - high.astype(F32)).astype(BF16)
    gram_up = dot(jnp.concatenate([high, rest], axis=0), tiled, 1, 0)
    gram_up = gram_up[:rank] + gram_up[rank:]
    mine = jnp.sum(factor * (2.0 * total[:rank] + gram_up), axis=0, keepdims=True)
    both = jnp.concatenate([mine, total[rank : rank + 1]], axis=0)
    second[...] = jnp.broadcast_to(both[None], second.shape)


def lift_kernel(where, keep, got, up, down, near):
    count = keep.shape[0]
    for out, steps in ((up, (1, 4, -2)), (down, (-1, 2)), (near, (0, 3, -3))):
        for i, step in enumerate(steps):
            at = (where[3] + step + count) % count
            out[i] = (keep[at].astype(F32) + got[at].astype(F32)).astype(BF16)


def scale_kernel(where, seg, second, magnitude, cotangent, up, low, scaled, third, norms):
    count = cotangent.shape[0]
    marks = bounds(seg, seg.shape[0], where[0] * count)
    parts = second[...]
    squares = parts[:, 0, :] + jnp.sum(parts[:, 1, :], axis=0, keepdims=True)
    col_norms = jnp.sqrt(jnp.maximum(squares, 0.0) + EPSILON)
    norms[...] = col_norms
    scale = token_scale_of(magnitude[...].astype(F32) / col_norms, marks, count)
    grad = (cotangent[...].astype(F32) * scale).astype(BF16)
    scaled[...] = grad
    back = packed(picked(dot(up[...], grad, 1, 1), marks)).astype(BF16)
    every = jnp.concatenate([low[...], back], axis=0)
    third[...] = jnp.broadcast_to(every[None], third.shape)


def far_kernel(near, up, down, share, other, to_up, to_down, own):
    own[...] = near[0].astype(F32) + up[0].astype(F32) + down[0].astype(F32)
    to_up[0] = (near[1].astype(F32) + up[1].astype(F32) + down[1].astype(F32)).astype(BF16)
    to_down[0] = (near[2].astype(F32) + up[2].astype(F32)).astype(BF16)
    for out in (to_up, to_down):
        out[1] = share[...]
        out[2] = other[...]


def pack_kernel(share, other, below, above, before, after):
    for out in (before, after):
        out[0] = share[...]
        out[1] = other[...]
        out[2:4] = below[1:]
    after[4:6] = above[1:]


def join_kernel(after, from_below, from_above, out):
    out[:6] = after[...]
    out[6:12] = from_below[...]
    out[12:] = from_above[...]


def sums_kernel(rank_rows, ranks):
    ranks[...] = jnp.sum(rank_rows[...].astype(F32), axis=0).astype(BF16)


def grads_kernel(where, seg, ranks, got, scaled, up, tokens, fourth, low_wide, back_wide):
    adapters = seg.shape[0]
    own_rows, count = tokens.shape
    rank = up.shape[0] // adapters
    marks = bounds(seg, adapters, where[0] * count)
    total = ranks[...].astype(F32) + got[...].astype(F32)
    low = widened(unpacked(total[: 2 * rank]), marks)
    back = widened(unpacked(total[2 * rank :]), marks)
    low_wide[...] = low
    back_wide[...] = back
    down_part = dot(back, tokens[...], 1, 1).astype(BF16)
    up_part = dot(low, scaled[...], 1, 0).astype(BF16)
    for a in range(adapters):
        lines = down_part[a * rank : (a + 1) * rank]
        pieces = [lines[:, k : k + LANES] for k in range(0, own_rows - LANES + 1, LANES)]
        rest = lines[:, own_rows // LANES * LANES :]
        pieces.append(up_part[a * rank : (a + 1) * rank])
        pieces.append(jnp.concatenate([rest[: rank // 2], rest[rank // 2 :]], axis=1))
        fourth[a] = jnp.concatenate(pieces, axis=0)


def hidden_kernel(where, seg, base, base_a, base_b, low, up, norms, magnitude, cotangent,
                  projected, mag):
    count = cotangent.shape[0]
    marks = bounds(seg, seg.shape[0], where[0] * count)
    hidden = base[...] + base_a[0].astype(F32) + base_b[0].astype(F32)
    hidden = hidden + dot(low[...], up[...], 0, 0)
    scale = token_scale_of(magnitude[...].astype(F32) / norms[...], marks, count)
    projected[...] = (hidden * scale).astype(BF16)
    weighted = cotangent[...].astype(F32) * hidden
    at = iota((count, LANES), 0)
    sums = [
        jnp.sum(jnp.where((at >= lo) & (at < hi), weighted, 0.0), axis=0, keepdims=True)
        for lo, hi in marks
    ]
    mag[...] = jnp.concatenate(sums, axis=0).astype(BF16)


def total_kernel(arrived, mag, fifth):
    total = jnp.sum(arrived[...].astype(F32), axis=0).astype(BF16)
    edge = total.shape[0] - mag.shape[0] // 2
    both = jnp.concatenate([total[:edge], mag[...], total[edge:]], axis=0)
    fifth[...] = jnp.broadcast_to(both[None], fifth.shape)


def final_kernel(fifth, norms, grad_down, grad_up, grad_magnitude):
    _, rank, own_rows = grad_down.shape
    tiles = own_rows // LANES
    for k in range(tiles):
        grad_down[:, :, k * LANES : (k + 1) * LANES] = fifth[:, k * rank : (k + 1) * rank]
    up = tiles * rank
    grad_up[...] = fifth[:, up : up + rank].astype(F32)
    total = jnp.sum(fifth[:, up + rank : up + 2 * rank].astype(F32), axis=0)
    grad_magnitude[...] = total / norms[...]
    rest = fifth[:, up + 2 * rank :]
    half = own_rows - tiles * LANES
    grad_down[:, :, tiles * LANES :] = jnp.concatenate([rest[:, :, :half], rest[:, :, half:]], 1)


def tokens_kernel(where, blocks, *rest):
    *columns, first, second, out, total = rest
    step = pl.program_id(0)

    @pl.when(step == 0)
    def _():
        total[...] = dot(first[...], second[...], 0, 0)

    left = [blocks[i] for i in range(blocks.shape[0])]
    right = [column[...] for column in columns]
    total[...] += dot(jnp.concatenate(right, axis=1), jnp.concatenate(left, axis=1), 1, 1)

    @pl.when(step == pl.num_programs(0) - 1)
    def _():
        out[...] = total[...]


def tokens_rest_kernel(where, blocks, *rest):
    *columns, part, out, total = rest
    step = pl.program_id(0)

    @pl.when(step == 0)
    def _():
        total[...] = part[...]

    left = [blocks[i] for i in range(blocks.shape[0])]
    right = [column[...] for column in columns]
    total[...] += dot(jnp.concatenate(right, axis=1), jnp.concatenate(left, axis=1), 1, 1)

    @pl.when(step == pl.num_programs(0) - 1)
    def _():
        out[...] = total[...].astype(BF16)


def exchange(blocks, axis, groups=None):
    return lax.all_to_all(blocks, axis, 0, 0, tiled=True, axis_index_groups=groups)


def local(tokens, base_weight, adapter_down, adapter_up, magnitude, seg_lengths, cotangent):
    count, own_rows = tokens.shape
    adapters, _, rank = adapter_down.shape
    width = adapter_up.shape[2]
    full = base_weight.shape[1]
    size = full // width
    zs = size // 4
    wide = adapters * rank
    me_dp = lax.axis_index("dp")
    me = lax.axis_index("tensor")
    core, hi = me % 2, me // (2 * zs)
    z = (me // 2) % zs
    where = jnp.stack([me_dp, core, hi, z]).astype(I32)
    core_pairs = [(i, i ^ 1) for i in range(size)]
    hi_pairs = [(i, (i + size // 2) % size) for i in range(size)]

    turned = tokens.T
    core_groups = [list(range(c, size, 2)) for c in range(2)]
    down_rows = jnp.transpose(adapter_down, (0, 2, 1))
    down_flat = down_rows.reshape(wide, own_rows)
    up_own = adapter_up.reshape(wide, width)

    head, keep, give = call(
        first_kernel,
        [
            shaped(size, HEAD, width),
            shaped(size // 2, count, width),
            pltpu.HBM((size // 2, count, width), BF16),
        ],
        scalars=1,
        grid=(2,),
        in_specs=[
            whole(own_rows, count),
            pl.BlockSpec((own_rows, full // 2), lambda i, s: (0, i)),
            pl.BlockSpec((1, rank, own_rows), lambda i, s: (s[0], 0, 0)),
        ],
        out_specs=[
            pl.BlockSpec((size // 2, HEAD, width), lambda i, s: (i, 0, 0)),
            pl.BlockSpec((size // 4, count, width), lambda i, s: (i, 0, 0)),
            pl.BlockSpec((size // 4, count, width), lambda i, s: (i, 0, 0)),
        ],
        scratch=[pltpu.VMEM((8, width), F32), pltpu.VMEM((count + rank, own_rows), BF16)],
        flops=2 * count * own_rows * full,
        moved=2 * own_rows * full,
    )(where, in_hbm(turned), in_hbm(base_weight), in_hbm(down_rows))
    head = exchange(head, "tensor")
    got = shift(give, core_pairs)
    half = size // 4
    mine = pl.BlockSpec((half // 2, count, width), lambda i, s, t: (s[2] * 2 + i, 0, 0))
    theirs = pl.BlockSpec((half // 2, count, width), lambda i, s, t: ((1 - s[2]) * 2 + i, 0, 0))
    out = pl.BlockSpec((half // 2, count, width), lambda i, s, t: (i, 0, 0))
    low, keep, give = call(
        halves_kernel,
        [shaped(2 * rank, width), shaped(zs, count, width), shaped(zs, count, width)],
        scalars=2,
        grid=(2,),
        in_specs=[whole(own_rows, count), whole(wide, own_rows), mine, mine, theirs, theirs],
        out_specs=[whole(2 * rank, width), out, out],
        flops=2 * count * own_rows * wide,
        moved=12 * zs * count * width,
    )(where, seg_lengths, turned, down_flat, keep, got, keep, got)
    got = shift(give, hi_pairs)

    def along_z(step):
        return [
            (h * 2 * zs + a * 2 + c, h * 2 * zs + (a + step) % zs * 2 + c)
            for h in range(2)
            for a in range(zs)
            for c in range(2)
        ]

    second = call(
        squares_kernel,
        shaped(adapters, 2, width, dtype=F32),
        scalars=1,
        grid=(1,),
        in_specs=[
            whole(size, HEAD, width),
            pl.BlockSpec((1, rank, width), lambda i, s: (s[0], 0, 0)),
        ],
        out_specs=whole(adapters, 2, width),
        moved=2 * size * HEAD * width,
    )(where, head, adapter_up)
    second = exchange(second, "dp")

    up3, down2, near = call(
        lift_kernel,
        [shaped(n, count, width) for n in (3, 2, 3)],
        scalars=1,
        grid=(1,),
        in_specs=[whole(zs, count, width)] * 2,
        out_specs=[whole(n, count, width) for n in (3, 2, 3)],
        moved=6 * zs * count * width,
    )(where, keep, got)
    up3 = shift(up3, along_z(1))
    down2 = shift(down2, along_z(-1))

    share, third, norms = call(
        scale_kernel,
        [
            shaped(count, width),
            shaped(2 * zs, 4 * rank, width),
            shaped(adapters, width, dtype=F32),
        ],
        scalars=2,
        grid=(1,),
        in_specs=[
            whole(adapters, 2, width),
            whole(adapters, width),
            whole(count, width),
            whole(wide, width),
            whole(2 * rank, width),
        ],
        out_specs=[
            whole(count, width),
            whole(2 * zs, 4 * rank, width),
            whole(adapters, width),
        ],
        flops=2 * count * wide * width,
        moved=8 * count * width,
    )(where, seg_lengths, second, magnitude, cotangent, up_own, low)
    third = exchange(third, "tensor", core_groups)
    other = shift(share, hi_pairs)
    scaled = whole(count, width)
    to_up, to_down, base = call(
        far_kernel,
        [shaped(3, count, width), shaped(3, count, width), shaped(count, width, dtype=F32)],
        grid=(1,),
        in_specs=[whole(n, count, width) for n in (3, 3, 2)] + [scaled] * 2,
        out_specs=[whole(3, count, width), whole(3, count, width), whole(count, width)],
        moved=36 * count * width,
    )(near, up3, down2, share, other)
    below = shift(to_up, along_z(3))
    above = shift(to_down, along_z(-3))
    ranks = call(
        sums_kernel,
        shaped(4 * rank, width),
        grid=(1,),
        in_specs=[whole(2 * zs, 4 * rank, width)],
        out_specs=whole(4 * rank, width),
        moved=2 * zs * 4 * rank * width,
    )(third)
    other_ranks = shift(ranks, core_pairs)

    before, after = call(
        pack_kernel,
        [shaped(4, count, width), shaped(6, count, width)],
        grid=(1,),
        in_specs=[scaled] * 2 + [whole(3, count, width)] * 2,
        out_specs=[whole(4, count, width), whole(6, count, width)],
        moved=32 * count * width,
    )(share, other, below, above)
    from_below = shift(after, along_z(1))
    from_above = shift(before, along_z(-1))
    gather_a = call(
        join_kernel,
        shaped(2 * zs, count, width),
        grid=(1,),
        in_specs=[whole(n, count, width) for n in (6, 6, 4)],
        out_specs=whole(2 * zs, count, width),
        moved=8 * zs * count * width,
    )(after, from_below, from_above)
    gather_b = shift(gather_a, core_pairs)

    lines = own_rows // LANES * rank + rank + rank // 2
    fourth, low_wide, back_wide = call(
        grads_kernel,
        [shaped(adapters, lines, width), shaped(wide, count), shaped(wide, count)],
        scalars=2,
        grid=(1,),
        in_specs=[
            whole(4 * rank, width),
            whole(4 * rank, width),
            whole(count, width),
            whole(wide, width),
            whole(own_rows, count),
        ],
        out_specs=[whole(adapters, lines, width), whole(wide, count), whole(wide, count)],
        flops=2 * count * wide * (own_rows + width),
        moved=4 * adapters * lines * width,
    )(where, seg_lengths, ranks, other_ranks, share, up_own, turned)
    fourth = exchange(fourth, "dp")

    first_block = pl.BlockSpec((1, count, width), lambda i, *s: (0, 0, 0))
    projected, mag = call(
        hidden_kernel,
        [shaped(count, width), shaped(adapters, width)],
        scalars=2,
        grid=(1,),
        in_specs=[
            whole(count, width),
            first_block,
            first_block,
            whole(wide, count),
            whole(wide, width),
            whole(adapters, width),
            whole(adapters, width),
            whole(count, width),
        ],
        out_specs=[whole(count, width), whole(adapters, width)],
        flops=2 * count * wide * width,
        moved=16 * count * width,
    )(where, seg_lengths, base, below, above, low_wide, up_own, norms, magnitude,
      cotangent)

    fifth = call(
        total_kernel,
        shaped(adapters, lines + rank, width),
        grid=(1,),
        in_specs=[whole(adapters, lines, width), whole(adapters, width)],
        out_specs=whole(adapters, lines + rank, width),
        moved=4 * adapters * lines * width,
    )(fourth, mag)
    fifth = exchange(fifth, "dp")

    per = 4
    offsets = (0, -3, 3, -1, -4, 2, 1, -2)

    def column(k, x_bit, c_bit):
        def at(i, s):
            off = jnp.where(i == 0, offsets[k], offsets[per + k])
            block = (s[3] + off + zs) % zs
            return (0, (s[2] ^ x_bit) * (2 * zs) + block * 2 + (s[1] ^ c_bit))

        return pl.BlockSpec((own_rows, width), at)

    def columns(c_bit):
        return [column(k, x, c_bit) for k in range(per) for x in range(2)]

    block = pl.BlockSpec((2 * per, count, width), lambda i, s: (i, 0, 0))
    weights = [in_hbm(base_weight)] * (2 * per)
    part = call(
        tokens_kernel,
        shaped(own_rows, count, dtype=F32),
        scalars=1,
        grid=(zs // per,),
        in_specs=[block] + columns(0) + [whole(wide, own_rows), whole(wide, count)],
        out_specs=whole(own_rows, count),
        scratch=[pltpu.VMEM((own_rows, count), F32)],
        flops=count * own_rows * (full + 2 * wide),
        moved=own_rows * full,
    )(where, gather_a, *weights, down_flat, back_wide)
    grad_tokens = call(
        tokens_rest_kernel,
        shaped(own_rows, count),
        scalars=1,
        grid=(zs // per,),
        in_specs=[block] + columns(1) + [whole(own_rows, count)],
        out_specs=whole(own_rows, count),
        scratch=[pltpu.VMEM((own_rows, count), F32)],
        flops=count * own_rows * full,
        moved=own_rows * full,
    )(where, gather_b, *weights, part)

    grad_down, grad_up, grad_magnitude = call(
        final_kernel,
        [
            shaped(adapters, rank, own_rows),
            shaped(adapters, rank, width, dtype=F32),
            shaped(adapters, width, dtype=F32),
        ],
        grid=(1,),
        in_specs=[whole(adapters, lines + rank, width), whole(adapters, width)],
        out_specs=[
            whole(adapters, rank, own_rows),
            whole(adapters, rank, width),
            whole(adapters, width),
        ],
        moved=4 * adapters * lines * width,
    )(fifth, norms)
    return (projected, grad_tokens.T, jnp.transpose(grad_down, (0, 2, 1)), grad_up, grad_magnitude)


def solution(mesh):
    placed = (
        P("dp", "tensor"),
        P("tensor", None),
        P(None, "tensor", None),
        P(None, None, "tensor"),
        P(None, "tensor"),
        P(),
        P("dp", "tensor"),
    )
    return jax.shard_map(
        local,
        mesh=mesh,
        in_specs=placed,
        out_specs=(
            P("dp", "tensor"),
            P("dp", "tensor"),
            P(None, "tensor", None),
            P(None, None, "tensor"),
            P(None, "tensor"),
        ),
        check_vma=False,
    )
```

```python
import jax
import jax.numpy as jnp
from jax import lax
from jax.experimental import pallas as pl
from jax.experimental.pallas import tpu as pltpu
from jax.sharding import PartitionSpec as P


EPSILON = 1e-06
F32 = jnp.float32
BF16 = jnp.bfloat16
I32 = jnp.int32
LANES = 128
HEAD = 24


def dot(a, b, ca, cb, precision=None):
    return lax.dot_general(
        a, b, (((ca,), (cb,)), ((), ())), precision=precision, preferred_element_type=F32
    )


def iota(shape, dim):
    return lax.broadcasted_iota(I32, shape, dim)


def shaped(*dims, dtype=BF16):
    return jax.ShapeDtypeStruct(dims, dtype)


def bounds(seg, adapters, first_token):
    marks, at = [], -first_token
    for a in range(adapters):
        marks.append((at, at + seg[a]))
        at = at + seg[a]
    return marks


def picked(spread, marks):
    rank = spread.shape[0] // len(marks)
    at = iota((rank, spread.shape[1]), 1)
    total = jnp.zeros((rank, spread.shape[1]), F32)
    for a, (lo, hi) in enumerate(marks):
        total += jnp.where((at >= lo) & (at < hi), spread[a * rank : (a + 1) * rank], 0.0)
    return total


def widened(rank_rows, marks):
    at = iota(rank_rows.shape, 1)
    wide = [jnp.where((at >= lo) & (at < hi), rank_rows, 0.0) for lo, hi in marks]
    return jnp.concatenate(wide, axis=0).astype(BF16)


def packed(rows):
    return jnp.concatenate([rows[:, :LANES], rows[:, LANES:]], axis=0)


def unpacked(rows):
    half = rows.shape[0] // 2
    return jnp.concatenate([rows[:half], rows[half:]], axis=1)


def token_scale_of(col_scale, marks, token_count):
    at = iota((token_count, LANES), 0)
    total = jnp.zeros((token_count, LANES), F32)
    for a, (lo, hi) in enumerate(marks):
        total += jnp.where((at >= lo) & (at < hi), col_scale[a : a + 1], 0.0)
    return total


def shift(block, pairs):
    return lax.ppermute(block, "tensor", pairs)


def call(kernel, out_shape, scalars=0, grid=(), in_specs=None, out_specs=None, scratch=(),
         flops=0, moved=0):
    if grid == (1,):
        resident = pl.BlockSpec(memory_space=pltpu.VMEM)
        grid, in_specs = (), [resident] * len(in_specs)
        out_specs = [resident] * len(out_specs) if isinstance(out_specs, list) else resident
    return pl.pallas_call(
        kernel,
        out_shape=out_shape,
        grid_spec=pltpu.PrefetchScalarGridSpec(
            num_scalar_prefetch=scalars,
            grid=grid,
            in_specs=in_specs,
            out_specs=out_specs,
            scratch_shapes=list(scratch),
        ),
        cost_estimate=pl.CostEstimate(flops=flops, bytes_accessed=moved, transcendentals=0),
        compiler_params=pltpu.CompilerParams(vmem_limit_bytes=16 * 2**20),
    )


def in_hbm(array):
    return pltpu.with_memory_space_constraint(array, pltpu.HBM)


def whole(*dims):
    return pl.BlockSpec(dims, lambda *ids: (0,) * len(dims))


def first_kernel(where, tokens, weight, down, head, keep, give, gram, lines):
    rank = down.shape[1]
    count = tokens.shape[1]

    @pl.when(pl.program_id(0) == 0)
    def _():
        mine = down[0]
        lines[:count] = tokens[...].T
        lines[count:] = mine
        square = dot(mine, mine, 1, 1)
        tile = (iota((rank, LANES), 1) % rank == iota((rank, LANES), 0)).astype(BF16)
        spread = dot(square.astype(BF16), tile, 1, 0)
        rows, cols = iota((rank, LANES), 0), iota((rank, LANES), 1)
        spread = jnp.where(cols // rank == rows % 8, spread, 0.0)
        gram[0:1, :] = jnp.sum(spread[:8], axis=0, keepdims=True)
        gram[1:2, :] = jnp.sum(spread[8:], axis=0, keepdims=True)

    share = 32
    pieces = weight.shape[0] // share
    start = pl.multiple_of(jnp.minimum(where[0], pieces - 1) * share, share)
    mine = (where[0] < pieces).astype(F32)
    row = iota((8, LANES), 0)
    swap = where[1] != 0
    step = 8 * LANES
    for block in range(0, weight.shape[1], step):
        columns = slice(block, block + step)
        both = dot(lines[...], weight[:, columns], 1, 0)
        part = weight[pl.ds(start, share), columns].astype(F32)
        squares = jnp.sum(part * part, axis=0, keepdims=True) * mine
        for k in range(step // LANES):
            lanes = slice(k * LANES, (k + 1) * LANES)
            tail = jnp.where(
                row == 0,
                squares[:, lanes],
                jnp.where(row == 1, gram[0:1, :], jnp.where(row == 2, gram[1:2, :], 0.0)),
            )
            head[block // LANES + k] = jnp.concatenate([both[count:, lanes], tail], 0).astype(BF16)
        for k in range(step // LANES // 2):
            even = both[:count, 2 * k * LANES : (2 * k + 1) * LANES]
            odd = both[:count, (2 * k + 1) * LANES : (2 * k + 2) * LANES]
            at = block // LANES // 2 + k
            keep[at] = jnp.where(swap, odd, even).astype(BF16)
            give[at] = jnp.where(swap, even, odd).astype(BF16)


def halves_kernel(where, seg, tokens, down, keep_a, got_a, keep_b, got_b, low, keep, give):
    keep[...] = (keep_a[...].astype(F32) + got_a[...].astype(F32)).astype(BF16)
    give[...] = (keep_b[...].astype(F32) + got_b[...].astype(F32)).astype(BF16)

    @pl.when(pl.program_id(0) == 0)
    def _():
        marks = bounds(seg, seg.shape[0], where[0] * tokens.shape[1])
        spread = dot(down[...], tokens[...], 1, 0)
        low[...] = packed(picked(spread, marks)).astype(BF16)


def squares_kernel(where, head, up, second):
    rank = up.shape[1]
    own_up = up[where[0]]
    total = jnp.sum(head[...].astype(F32), axis=0)
    factor = own_up.astype(F32)
    rows, cols = iota((rank, LANES), 0), iota((rank, LANES), 1)
    spread = jnp.where(rows < 8, total[rank + 1 : rank + 2], total[rank + 2 : rank + 3])
    spread = jnp.where(cols // rank == rows % 8, spread, 0.0)
    tiled = jnp.concatenate([own_up] * (LANES // rank), axis=0)
    high = spread.astype(BF16)
    rest = (spread - high.astype(F32)).astype(BF16)
    gram_up = dot(jnp.concatenate([high, rest], axis=0), tiled, 1, 0)
    gram_up = gram_up[:rank] + gram_up[rank:]
    mine = jnp.sum(factor * (2.0 * total[:rank] + gram_up), axis=0, keepdims=True)
    both = jnp.concatenate([mine, total[rank : rank + 1]], axis=0)
    second[...] = jnp.broadcast_to(both[None], second.shape)


def lift_kernel(where, keep, got, up, down, near):
    count = keep.shape[0]
    for out, steps in ((up, (1, 4, -2)), (down, (-1, 2)), (near, (0, 3, -3))):
        for i, step in enumerate(steps):
            at = (where[3] + step + count) % count
            out[i] = (keep[at].astype(F32) + got[at].astype(F32)).astype(BF16)


def scale_kernel(where, seg, second, magnitude, cotangent, up, low, scaled, third, norms):
    count = cotangent.shape[0]
    marks = bounds(seg, seg.shape[0], where[0] * count)
    parts = second[...]
    squares = parts[:, 0, :] + jnp.sum(parts[:, 1, :], axis=0, keepdims=True)
    col_norms = jnp.sqrt(jnp.maximum(squares, 0.0) + EPSILON)
    norms[...] = col_norms
    scale = token_scale_of(magnitude[...].astype(F32) / col_norms, marks, count)
    grad = (cotangent[...].astype(F32) * scale).astype(BF16)
    scaled[...] = grad
    back = packed(picked(dot(up[...], grad, 1, 1), marks)).astype(BF16)
    every = jnp.concatenate([low[...], back], axis=0)
    third[...] = jnp.broadcast_to(every[None], third.shape)


def far_kernel(near, up, down, share, other, to_up, to_down, own):
    own[...] = near[0].astype(F32) + up[0].astype(F32) + down[0].astype(F32)
    to_up[0] = (near[1].astype(F32) + up[1].astype(F32) + down[1].astype(F32)).astype(BF16)
    to_down[0] = (near[2].astype(F32) + up[2].astype(F32)).astype(BF16)
    for out in (to_up, to_down):
        out[1] = share[...]
        out[2] = other[...]


def pack_kernel(share, other, below, above, before, after):
    for out in (before, after):
        out[0] = share[...]
        out[1] = other[...]
        out[2:4] = below[1:]
    after[4:6] = above[1:]


def join_kernel(after, from_below, from_above, out):
    out[:6] = after[...]
    out[6:12] = from_below[...]
    out[12:] = from_above[...]


def sums_kernel(rank_rows, ranks):
    ranks[...] = jnp.sum(rank_rows[...].astype(F32), axis=0).astype(BF16)


def grads_kernel(where, seg, ranks, got, scaled, up, tokens, fourth, low_wide, back_wide):
    adapters = seg.shape[0]
    own_rows, count = tokens.shape
    rank = up.shape[0] // adapters
    marks = bounds(seg, adapters, where[0] * count)
    total = ranks[...].astype(F32) + got[...].astype(F32)
    low = widened(unpacked(total[: 2 * rank]), marks)
    back = widened(unpacked(total[2 * rank :]), marks)
    low_wide[...] = low
    back_wide[...] = back
    down_part = dot(back, tokens[...], 1, 1).astype(BF16)
    up_part = dot(low, scaled[...], 1, 0).astype(BF16)
    for a in range(adapters):
        lines = down_part[a * rank : (a + 1) * rank]
        pieces = [lines[:, k : k + LANES] for k in range(0, own_rows - LANES + 1, LANES)]
        rest = lines[:, own_rows // LANES * LANES :]
        pieces.append(up_part[a * rank : (a + 1) * rank])
        pieces.append(jnp.concatenate([rest[: rank // 2], rest[rank // 2 :]], axis=1))
        fourth[a] = jnp.concatenate(pieces, axis=0)


def hidden_kernel(where, seg, base, base_a, base_b, low, up, norms, magnitude, cotangent,
                  projected, mag):
    count = cotangent.shape[0]
    marks = bounds(seg, seg.shape[0], where[0] * count)
    hidden = base[...] + base_a[0].astype(F32) + base_b[0].astype(F32)
    hidden = hidden + dot(low[...], up[...], 0, 0)
    scale = token_scale_of(magnitude[...].astype(F32) / norms[...], marks, count)
    projected[...] = (hidden * scale).astype(BF16)
    weighted = cotangent[...].astype(F32) * hidden
    at = iota((count, LANES), 0)
    sums = [
        jnp.sum(jnp.where((at >= lo) & (at < hi), weighted, 0.0), axis=0, keepdims=True)
        for lo, hi in marks
    ]
    mag[...] = jnp.concatenate(sums, axis=0).astype(BF16)


def total_kernel(arrived, mag, fifth):
    total = jnp.sum(arrived[...].astype(F32), axis=0).astype(BF16)
    edge = total.shape[0] - mag.shape[0] // 2
    both = jnp.concatenate([total[:edge], mag[...], total[edge:]], axis=0)
    fifth[...] = jnp.broadcast_to(both[None], fifth.shape)


def final_kernel(fifth, norms, grad_down, grad_up, grad_magnitude):
    _, rank, own_rows = grad_down.shape
    tiles = own_rows // LANES
    for k in range(tiles):
        grad_down[:, :, k * LANES : (k + 1) * LANES] = fifth[:, k * rank : (k + 1) * rank]
    up = tiles * rank
    grad_up[...] = fifth[:, up : up + rank].astype(F32)
    total = jnp.sum(fifth[:, up + rank : up + 2 * rank].astype(F32), axis=0)
    grad_magnitude[...] = total / norms[...]
    rest = fifth[:, up + 2 * rank :]
    half = own_rows - tiles * LANES
    grad_down[:, :, tiles * LANES :] = jnp.concatenate([rest[:, :, :half], rest[:, :, half:]], 1)


def tokens_kernel(where, blocks, *rest):
    *columns, first, second, out, total = rest
    step = pl.program_id(0)

    @pl.when(step == 0)
    def _():
        total[...] = dot(first[...], second[...], 0, 0)

    left = [blocks[i] for i in range(blocks.shape[0])]
    right = [column[...] for column in columns]
    total[...] += dot(jnp.concatenate(right, axis=1), jnp.concatenate(left, axis=1), 1, 1)

    @pl.when(step == pl.num_programs(0) - 1)
    def _():
        out[...] = total[...]


def tokens_rest_kernel(where, blocks, *rest):
    *columns, part, out, total = rest
    step = pl.program_id(0)

    @pl.when(step == 0)
    def _():
        total[...] = part[...]

    left = [blocks[i] for i in range(blocks.shape[0])]
    right = [column[...] for column in columns]
    total[...] += dot(jnp.concatenate(right, axis=1), jnp.concatenate(left, axis=1), 1, 1)

    @pl.when(step == pl.num_programs(0) - 1)
    def _():
        out[...] = total[...].astype(BF16)


def exchange(blocks, axis, groups=None):
    return lax.all_to_all(blocks, axis, 0, 0, tiled=True, axis_index_groups=groups)


def local(tokens, base_weight, adapter_down, adapter_up, magnitude, seg_lengths, cotangent):
    count, own_rows = tokens.shape
    adapters, _, rank = adapter_down.shape
    width = adapter_up.shape[2]
    full = base_weight.shape[1]
    size = full // width
    zs = size // 4
    wide = adapters * rank
    me_dp = lax.axis_index("dp")
    me = lax.axis_index("tensor")
    core, hi = me % 2, me // (2 * zs)
    z = (me // 2) % zs
    where = jnp.stack([me_dp, core, hi, z]).astype(I32)
    core_pairs = [(i, i ^ 1) for i in range(size)]
    hi_pairs = [(i, (i + size // 2) % size) for i in range(size)]

    turned = tokens.T
    core_groups = [list(range(c, size, 2)) for c in range(2)]
    down_rows = jnp.transpose(adapter_down, (0, 2, 1))
    down_flat = down_rows.reshape(wide, own_rows)
    up_own = adapter_up.reshape(wide, width)

    head, keep, give = call(
        first_kernel,
        [
            shaped(size, HEAD, width),
            shaped(size // 2, count, width),
            pltpu.HBM((size // 2, count, width), BF16),
        ],
        scalars=1,
        grid=(2,),
        in_specs=[
            whole(own_rows, count),
            pl.BlockSpec((own_rows, full // 2), lambda i, s: (0, i)),
            pl.BlockSpec((1, rank, own_rows), lambda i, s: (s[0], 0, 0)),
        ],
        out_specs=[
            pl.BlockSpec((size // 2, HEAD, width), lambda i, s: (i, 0, 0)),
            pl.BlockSpec((size // 4, count, width), lambda i, s: (i, 0, 0)),
            pl.BlockSpec((size // 4, count, width), lambda i, s: (i, 0, 0)),
        ],
        scratch=[pltpu.VMEM((8, width), F32), pltpu.VMEM((count + rank, own_rows), BF16)],
        flops=2 * count * own_rows * full,
        moved=2 * own_rows * full,
    )(where, in_hbm(turned), in_hbm(base_weight), in_hbm(down_rows))
    head = exchange(head, "tensor")
    got = shift(give, core_pairs)
    half = size // 4
    mine = pl.BlockSpec((half // 2, count, width), lambda i, s, t: (s[2] * 2 + i, 0, 0))
    theirs = pl.BlockSpec((half // 2, count, width), lambda i, s, t: ((1 - s[2]) * 2 + i, 0, 0))
    out = pl.BlockSpec((half // 2, count, width), lambda i, s, t: (i, 0, 0))
    low, keep, give = call(
        halves_kernel,
        [shaped(2 * rank, width), shaped(zs, count, width), shaped(zs, count, width)],
        scalars=2,
        grid=(2,),
        in_specs=[whole(own_rows, count), whole(wide, own_rows), mine, mine, theirs, theirs],
        out_specs=[whole(2 * rank, width), out, out],
        flops=2 * count * own_rows * wide,
        moved=12 * zs * count * width,
    )(where, seg_lengths, turned, down_flat, keep, got, keep, got)
    got = shift(give, hi_pairs)

    def along_z(step):
        return [
            (h * 2 * zs + a * 2 + c, h * 2 * zs + (a + step) % zs * 2 + c)
            for h in range(2)
            for a in range(zs)
            for c in range(2)
        ]

    second = call(
        squares_kernel,
        shaped(adapters, 2, width, dtype=F32),
        scalars=1,
        grid=(1,),
        in_specs=[
            whole(size, HEAD, width),
            pl.BlockSpec((1, rank, width), lambda i, s: (s[0], 0, 0)),
        ],
        out_specs=whole(adapters, 2, width),
        moved=2 * size * HEAD * width,
    )(where, head, adapter_up)
    second = exchange(second, "dp")

    up3, down2, near = call(
        lift_kernel,
        [shaped(n, count, width) for n in (3, 2, 3)],
        scalars=1,
        grid=(1,),
        in_specs=[whole(zs, count, width)] * 2,
        out_specs=[whole(n, count, width) for n in (3, 2, 3)],
        moved=6 * zs * count * width,
    )(where, keep, got)
    up3 = shift(up3, along_z(1))
    down2 = shift(down2, along_z(-1))

    share, third, norms = call(
        scale_kernel,
        [
            shaped(count, width),
            shaped(2 * zs, 4 * rank, width),
            shaped(adapters, width, dtype=F32),
        ],
        scalars=2,
        grid=(1,),
        in_specs=[
            whole(adapters, 2, width),
            whole(adapters, width),
            whole(count, width),
            whole(wide, width),
            whole(2 * rank, width),
        ],
        out_specs=[
            whole(count, width),
            whole(2 * zs, 4 * rank, width),
            whole(adapters, width),
        ],
        flops=2 * count * wide * width,
        moved=8 * count * width,
    )(where, seg_lengths, second, magnitude, cotangent, up_own, low)
    third = exchange(third, "tensor", core_groups)
    other = shift(share, hi_pairs)
    scaled = whole(count, width)
    to_up, to_down, base = call(
        far_kernel,
        [shaped(3, count, width), shaped(3, count, width), shaped(count, width, dtype=F32)],
        grid=(1,),
        in_specs=[whole(n, count, width) for n in (3, 3, 2)] + [scaled] * 2,
        out_specs=[whole(3, count, width), whole(3, count, width), whole(count, width)],
        moved=36 * count * width,
    )(near, up3, down2, share, other)
    below = shift(to_up, along_z(3))
    above = shift(to_down, along_z(-3))
    ranks = call(
        sums_kernel,
        shaped(4 * rank, width),
        grid=(1,),
        in_specs=[whole(2 * zs, 4 * rank, width)],
        out_specs=whole(4 * rank, width),
        moved=2 * zs * 4 * rank * width,
    )(third)
    other_ranks = shift(ranks, core_pairs)

    before, after = call(
        pack_kernel,
        [shaped(4, count, width), shaped(6, count, width)],
        grid=(1,),
        in_specs=[scaled] * 2 + [whole(3, count, width)] * 2,
        out_specs=[whole(4, count, width), whole(6, count, width)],
        moved=32 * count * width,
    )(share, other, below, above)
    from_below = shift(after, along_z(1))
    from_above = shift(before, along_z(-1))
    gather_a = call(
        join_kernel,
        shaped(2 * zs, count, width),
        grid=(1,),
        in_specs=[whole(n, count, width) for n in (6, 6, 4)],
        out_specs=whole(2 * zs, count, width),
        moved=8 * zs * count * width,
    )(after, from_below, from_above)
    gather_b = shift(gather_a, core_pairs)

    lines = own_rows // LANES * rank + rank + rank // 2
    fourth, low_wide, back_wide = call(
        grads_kernel,
        [shaped(adapters, lines, width), shaped(wide, count), shaped(wide, count)],
        scalars=2,
        grid=(1,),
        in_specs=[
            whole(4 * rank, width),
            whole(4 * rank, width),
            whole(count, width),
            whole(wide, width),
            whole(own_rows, count),
        ],
        out_specs=[whole(adapters, lines, width), whole(wide, count), whole(wide, count)],
        flops=2 * count * wide * (own_rows + width),
        moved=4 * adapters * lines * width,
    )(where, seg_lengths, ranks, other_ranks, share, up_own, turned)
    fourth = exchange(fourth, "dp")

    first_block = pl.BlockSpec((1, count, width), lambda i, *s: (0, 0, 0))
    projected, mag = call(
        hidden_kernel,
        [shaped(count, width), shaped(adapters, width)],
        scalars=2,
        grid=(1,),
        in_specs=[
            whole(count, width),
            first_block,
            first_block,
            whole(wide, count),
            whole(wide, width),
            whole(adapters, width),
            whole(adapters, width),
            whole(count, width),
        ],
        out_specs=[whole(count, width), whole(adapters, width)],
        flops=2 * count * wide * width,
        moved=16 * count * width,
    )(where, seg_lengths, base, below, above, low_wide, up_own, norms, magnitude,
      cotangent)

    fifth = call(
        total_kernel,
        shaped(adapters, lines + rank, width),
        grid=(1,),
        in_specs=[whole(adapters, lines, width), whole(adapters, width)],
        out_specs=whole(adapters, lines + rank, width),
        moved=4 * adapters * lines * width,
    )(fourth, mag)
    fifth = exchange(fifth, "dp")

    per = 4
    offsets = (0, -3, 3, -1, -4, 2, 1, -2)

    def column(k, x_bit, c_bit):
        def at(i, s):
            off = jnp.where(i == 0, offsets[k], offsets[per + k])
            block = (s[3] + off + zs) % zs
            return (0, (s[2] ^ x_bit) * (2 * zs) + block * 2 + (s[1] ^ c_bit))

        return pl.BlockSpec((own_rows, width), at)

    def columns(c_bit):
        return [column(k, x, c_bit) for k in range(per) for x in range(2)]

    block = pl.BlockSpec((2 * per, count, width), lambda i, s: (i, 0, 0))
    weights = [in_hbm(base_weight)] * (2 * per)
    part = call(
        tokens_kernel,
        shaped(own_rows, count, dtype=F32),
        scalars=1,
        grid=(zs // per,),
        in_specs=[block] + columns(0) + [whole(wide, own_rows), whole(wide, count)],
        out_specs=whole(own_rows, count),
        scratch=[pltpu.VMEM((own_rows, count), F32)],
        flops=count * own_rows * (full + 2 * wide),
        moved=own_rows * full,
    )(where, gather_a, *weights, down_flat, back_wide)
    grad_tokens = call(
        tokens_rest_kernel,
        shaped(own_rows, count),
        scalars=1,
        grid=(zs // per,),
        in_specs=[block] + columns(1) + [whole(own_rows, count)],
        out_specs=whole(own_rows, count),
        scratch=[pltpu.VMEM((own_rows, count), F32)],
        flops=count * own_rows * full,
        moved=own_rows * full,
    )(where, gather_b, *weights, part)

    grad_down, grad_up, grad_magnitude = call(
        final_kernel,
        [
            shaped(adapters, rank, own_rows),
            shaped(adapters, rank, width, dtype=F32),
            shaped(adapters, width, dtype=F32),
        ],
        grid=(1,),
        in_specs=[whole(adapters, lines + rank, width), whole(adapters, width)],
        out_specs=[
            whole(adapters, rank, own_rows),
            whole(adapters, rank, width),
            whole(adapters, width),
        ],
        moved=4 * adapters * lines * width,
    )(fifth, norms)
    return (projected, grad_tokens.T, jnp.transpose(grad_down, (0, 2, 1)), grad_up, grad_magnitude)


def solution(mesh):
    placed = (
        P("dp", "tensor"),
        P("tensor", None),
        P(None, "tensor", None),
        P(None, None, "tensor"),
        P(None, "tensor"),
        P(),
        P("dp", "tensor"),
    )
    return jax.shard_map(
        local,
        mesh=mesh,
        in_specs=placed,
        out_specs=(
            P("dp", "tensor"),
            P("dp", "tensor"),
            P(None, "tensor", None),
            P(None, None, "tensor"),
            P(None, "tensor"),
        ),
        check_vma=False,
    )
```

```python
import jax
import jax.numpy as jnp
from jax import lax
from jax.experimental import pallas as pl
from jax.experimental.pallas import tpu as pltpu
from jax.sharding import PartitionSpec as P


EPSILON = 1e-06
F32 = jnp.float32
BF16 = jnp.bfloat16
I32 = jnp.int32
LANES = 128
HEAD = 24


def dot(a, b, ca, cb, precision=None):
    return lax.dot_general(
        a, b, (((ca,), (cb,)), ((), ())), precision=precision, preferred_element_type=F32
    )


def iota(shape, dim):
    return lax.broadcasted_iota(I32, shape, dim)


def shaped(*dims, dtype=BF16):
    return jax.ShapeDtypeStruct(dims, dtype)


def bounds(seg, adapters, first_token):
    marks, at = [], -first_token
    for a in range(adapters):
        marks.append((at, at + seg[a]))
        at = at + seg[a]
    return marks


def picked(spread, marks):
    rank = spread.shape[0] // len(marks)
    at = iota((rank, spread.shape[1]), 1)
    total = jnp.zeros((rank, spread.shape[1]), F32)
    for a, (lo, hi) in enumerate(marks):
        total += jnp.where((at >= lo) & (at < hi), spread[a * rank : (a + 1) * rank], 0.0)
    return total


def widened(rank_rows, marks):
    at = iota(rank_rows.shape, 1)
    wide = [jnp.where((at >= lo) & (at < hi), rank_rows, 0.0) for lo, hi in marks]
    return jnp.concatenate(wide, axis=0).astype(BF16)


def packed(rows):
    return jnp.concatenate([rows[:, :LANES], rows[:, LANES:]], axis=0)


def unpacked(rows):
    half = rows.shape[0] // 2
    return jnp.concatenate([rows[:half], rows[half:]], axis=1)


def one_hot(marks, count):
    at = iota((1, count), 1)
    rows = [((at >= lo) & (at < hi)).astype(F32) for lo, hi in marks]
    return jnp.concatenate(rows, axis=0).astype(BF16)


def pieces(values, number):
    parts = []
    for _ in range(number):
        part = values.astype(BF16)
        parts.append(part)
        values = values - part.astype(F32)
    return parts


def token_scale_of(col_scale, marks, token_count):
    member = one_hot(marks, token_count)
    return dot(
        jnp.concatenate([member] * 3, axis=0),
        jnp.concatenate(pieces(col_scale, 3), axis=0),
        0,
        0,
    )


def shift(block, pairs):
    return lax.ppermute(block, "tensor", pairs)


def call(kernel, out_shape, scalars=0, grid=(), in_specs=None, out_specs=None, scratch=(),
         flops=0, moved=0):
    if grid == (1,):
        resident = pl.BlockSpec(memory_space=pltpu.VMEM)
        grid, in_specs = (), [resident] * len(in_specs)
        out_specs = [resident] * len(out_specs) if isinstance(out_specs, list) else resident
    return pl.pallas_call(
        kernel,
        out_shape=out_shape,
        grid_spec=pltpu.PrefetchScalarGridSpec(
            num_scalar_prefetch=scalars,
            grid=grid,
            in_specs=in_specs,
            out_specs=out_specs,
            scratch_shapes=list(scratch),
        ),
        cost_estimate=pl.CostEstimate(flops=flops, bytes_accessed=moved, transcendentals=0),
        compiler_params=pltpu.CompilerParams(vmem_limit_bytes=16 * 2**20),
    )


def in_hbm(array):
    return pltpu.with_memory_space_constraint(array, pltpu.HBM)


def whole(*dims):
    return pl.BlockSpec(dims, lambda *ids: (0,) * len(dims))


def first_kernel(where, tokens, weight, down, head, keep, give, gram, lines):
    rank = down.shape[1]
    count = tokens.shape[1]

    @pl.when(pl.program_id(0) == 0)
    def _():
        mine = down[0]
        lines[:count] = tokens[...].T
        lines[count:] = mine
        square = dot(mine, mine, 1, 1)
        tile = (iota((rank, LANES), 1) % rank == iota((rank, LANES), 0)).astype(BF16)
        spread = dot(square.astype(BF16), tile, 1, 0)
        rows, cols = iota((rank, LANES), 0), iota((rank, LANES), 1)
        spread = jnp.where(cols // rank == rows % 8, spread, 0.0)
        gram[0:1, :] = jnp.sum(spread[:8], axis=0, keepdims=True)
        gram[1:2, :] = jnp.sum(spread[8:], axis=0, keepdims=True)

    share = 32
    pieces = weight.shape[0] // share
    start = pl.multiple_of(jnp.minimum(where[0], pieces - 1) * share, share)
    mine = (where[0] < pieces).astype(F32)
    row = iota((8, LANES), 0)
    swap = where[1] != 0
    step = 8 * LANES
    for block in range(0, weight.shape[1], step):
        columns = slice(block, block + step)
        both = dot(lines[...], weight[:, columns], 1, 0)
        part = weight[pl.ds(start, share), columns].astype(F32)
        squares = jnp.sum(part * part, axis=0, keepdims=True) * mine
        for k in range(step // LANES):
            lanes = slice(k * LANES, (k + 1) * LANES)
            tail = jnp.where(
                row == 0,
                squares[:, lanes],
                jnp.where(row == 1, gram[0:1, :], jnp.where(row == 2, gram[1:2, :], 0.0)),
            )
            head[block // LANES + k] = jnp.concatenate([both[count:, lanes], tail], 0).astype(BF16)
        for k in range(step // LANES // 2):
            even = both[:count, 2 * k * LANES : (2 * k + 1) * LANES]
            odd = both[:count, (2 * k + 1) * LANES : (2 * k + 2) * LANES]
            at = block // LANES // 2 + k
            keep[at] = jnp.where(swap, odd, even).astype(BF16)
            give[at] = jnp.where(swap, even, odd).astype(BF16)


def halves_kernel(where, seg, tokens, down, keep_a, got_a, keep_b, got_b, low, keep, give):
    keep[...] = (keep_a[...].astype(F32) + got_a[...].astype(F32)).astype(BF16)
    give[...] = (keep_b[...].astype(F32) + got_b[...].astype(F32)).astype(BF16)

    @pl.when(pl.program_id(0) == 0)
    def _():
        marks = bounds(seg, seg.shape[0], where[0] * tokens.shape[1])
        spread = dot(down[...], tokens[...], 1, 0)
        low[...] = packed(picked(spread, marks)).astype(BF16)


def squares_kernel(where, head, up, second):
    rank = up.shape[1]
    own_up = up[where[0]]
    total = jnp.sum(head[...].astype(F32), axis=0)
    factor = own_up.astype(F32)
    rows, cols = iota((rank, LANES), 0), iota((rank, LANES), 1)
    spread = jnp.where(rows < 8, total[rank + 1 : rank + 2], total[rank + 2 : rank + 3])
    spread = jnp.where(cols // rank == rows % 8, spread, 0.0)
    tiled = jnp.concatenate([own_up] * (LANES // rank), axis=0)
    high = spread.astype(BF16)
    rest = (spread - high.astype(F32)).astype(BF16)
    gram_up = dot(jnp.concatenate([high, rest], axis=0), tiled, 1, 0)
    gram_up = gram_up[:rank] + gram_up[rank:]
    mine = jnp.sum(factor * (2.0 * total[:rank] + gram_up), axis=0, keepdims=True)
    both = jnp.concatenate([mine, total[rank : rank + 1]], axis=0)
    second[...] = jnp.broadcast_to(both[None], second.shape)


def lift_kernel(where, keep, got, up, down, near):
    count = keep.shape[0]
    for out, steps in ((up, (1, 4, -2)), (down, (-1, 2)), (near, (0, 3, -3))):
        for i, step in enumerate(steps):
            at = (where[3] + step + count) % count
            out[i] = (keep[at].astype(F32) + got[at].astype(F32)).astype(BF16)


def scale_kernel(where, seg, second, magnitude, cotangent, up, low, scaled, third, norms):
    count = cotangent.shape[0]
    marks = bounds(seg, seg.shape[0], where[0] * count)
    parts = second[...]
    squares = parts[:, 0, :] + jnp.sum(parts[:, 1, :], axis=0, keepdims=True)
    col_norms = jnp.sqrt(jnp.maximum(squares, 0.0) + EPSILON)
    norms[...] = col_norms
    scale = token_scale_of(magnitude[...].astype(F32) / col_norms, marks, count)
    grad = (cotangent[...].astype(F32) * scale).astype(BF16)
    scaled[...] = grad
    back = packed(picked(dot(up[...], grad, 1, 1), marks)).astype(BF16)
    every = jnp.concatenate([low[...], back], axis=0)
    third[...] = jnp.broadcast_to(every[None], third.shape)


def far_kernel(near, up, down, share, other, to_up, to_down, own):
    own[...] = near[0].astype(F32) + up[0].astype(F32) + down[0].astype(F32)
    to_up[0] = (near[1].astype(F32) + up[1].astype(F32) + down[1].astype(F32)).astype(BF16)
    to_down[0] = (near[2].astype(F32) + up[2].astype(F32)).astype(BF16)
    for out in (to_up, to_down):
        out[1] = share[...]
        out[2] = other[...]


def pack_kernel(share, other, below, above, before, after):
    for out in (before, after):
        out[0] = share[...]
        out[1] = other[...]
        out[2:4] = below[1:]
    after[4:6] = above[1:]


def join_kernel(after, from_below, from_above, out):
    out[:6] = after[...]
    out[6:12] = from_below[...]
    out[12:] = from_above[...]


def sums_kernel(rank_rows, ranks):
    ranks[...] = jnp.sum(rank_rows[...].astype(F32), axis=0).astype(BF16)


def grads_kernel(where, seg, ranks, got, scaled, up, tokens, fourth, low_wide, back_wide):
    adapters = seg.shape[0]
    own_rows, count = tokens.shape
    rank = up.shape[0] // adapters
    marks = bounds(seg, adapters, where[0] * count)
    total = ranks[...].astype(F32) + got[...].astype(F32)
    low = widened(unpacked(total[: 2 * rank]), marks)
    back = widened(unpacked(total[2 * rank :]), marks)
    low_wide[...] = low
    back_wide[...] = back
    down_part = dot(back, tokens[...], 1, 1).astype(BF16)
    up_part = dot(low, scaled[...], 1, 0).astype(BF16)
    for a in range(adapters):
        lines = down_part[a * rank : (a + 1) * rank]
        pieces = [lines[:, k : k + LANES] for k in range(0, own_rows - LANES + 1, LANES)]
        rest = lines[:, own_rows // LANES * LANES :]
        pieces.append(up_part[a * rank : (a + 1) * rank])
        pieces.append(jnp.concatenate([rest[: rank // 2], rest[rank // 2 :]], axis=1))
        fourth[a] = jnp.concatenate(pieces, axis=0)


def hidden_kernel(where, seg, base, base_a, base_b, low, up, norms, magnitude, cotangent,
                  projected, mag):
    count = cotangent.shape[0]
    marks = bounds(seg, seg.shape[0], where[0] * count)
    hidden = base[...] + base_a[0].astype(F32) + base_b[0].astype(F32)
    hidden = hidden + dot(low[...], up[...], 0, 0)
    scale = token_scale_of(magnitude[...].astype(F32) / norms[...], marks, count)
    projected[...] = (hidden * scale).astype(BF16)
    weighted = cotangent[...].astype(F32) * hidden
    member = one_hot(marks, count)
    high, rest = pieces(weighted, 2)
    mag[...] = (dot(member, high, 1, 0) + dot(member, rest, 1, 0)).astype(BF16)


def total_kernel(arrived, mag, fifth):
    total = jnp.sum(arrived[...].astype(F32), axis=0).astype(BF16)
    edge = total.shape[0] - mag.shape[0] // 2
    both = jnp.concatenate([total[:edge], mag[...], total[edge:]], axis=0)
    fifth[...] = jnp.broadcast_to(both[None], fifth.shape)


def final_kernel(fifth, norms, grad_down, grad_up, grad_magnitude):
    _, rank, own_rows = grad_down.shape
    tiles = own_rows // LANES
    for k in range(tiles):
        grad_down[:, :, k * LANES : (k + 1) * LANES] = fifth[:, k * rank : (k + 1) * rank]
    up = tiles * rank
    grad_up[...] = fifth[:, up : up + rank].astype(F32)
    total = jnp.sum(fifth[:, up + rank : up + 2 * rank].astype(F32), axis=0)
    grad_magnitude[...] = total / norms[...]
    rest = fifth[:, up + 2 * rank :]
    half = own_rows - tiles * LANES
    grad_down[:, :, tiles * LANES :] = jnp.concatenate([rest[:, :, :half], rest[:, :, half:]], 1)


def tokens_kernel(where, blocks, *rest):
    *columns, first, second, out, total = rest
    step = pl.program_id(0)

    @pl.when(step == 0)
    def _():
        total[...] = dot(first[...], second[...], 0, 0)

    left = [blocks[i] for i in range(blocks.shape[0])]
    right = [column[...] for column in columns]
    total[...] += dot(jnp.concatenate(right, axis=1), jnp.concatenate(left, axis=1), 1, 1)

    @pl.when(step == pl.num_programs(0) - 1)
    def _():
        out[...] = total[...]


def tokens_rest_kernel(where, blocks, *rest):
    *columns, part, out, total = rest
    step = pl.program_id(0)

    @pl.when(step == 0)
    def _():
        total[...] = part[...]

    left = [blocks[i] for i in range(blocks.shape[0])]
    right = [column[...] for column in columns]
    total[...] += dot(jnp.concatenate(right, axis=1), jnp.concatenate(left, axis=1), 1, 1)

    @pl.when(step == pl.num_programs(0) - 1)
    def _():
        out[...] = total[...].astype(BF16)


def exchange(blocks, axis, groups=None):
    return lax.all_to_all(blocks, axis, 0, 0, tiled=True, axis_index_groups=groups)


def local(tokens, base_weight, adapter_down, adapter_up, magnitude, seg_lengths, cotangent):
    count, own_rows = tokens.shape
    adapters, _, rank = adapter_down.shape
    width = adapter_up.shape[2]
    full = base_weight.shape[1]
    size = full // width
    zs = size // 4
    wide = adapters * rank
    me_dp = lax.axis_index("dp")
    me = lax.axis_index("tensor")
    core, hi = me % 2, me // (2 * zs)
    z = (me // 2) % zs
    where = jnp.stack([me_dp, core, hi, z]).astype(I32)
    core_pairs = [(i, i ^ 1) for i in range(size)]
    hi_pairs = [(i, (i + size // 2) % size) for i in range(size)]

    turned = tokens.T
    core_groups = [list(range(c, size, 2)) for c in range(2)]
    down_rows = jnp.transpose(adapter_down, (0, 2, 1))
    down_flat = down_rows.reshape(wide, own_rows)
    up_own = adapter_up.reshape(wide, width)

    head, keep, give = call(
        first_kernel,
        [
            shaped(size, HEAD, width),
            shaped(size // 2, count, width),
            pltpu.HBM((size // 2, count, width), BF16),
        ],
        scalars=1,
        grid=(2,),
        in_specs=[
            whole(own_rows, count),
            pl.BlockSpec((own_rows, full // 2), lambda i, s: (0, i)),
            pl.BlockSpec((1, rank, own_rows), lambda i, s: (s[0], 0, 0)),
        ],
        out_specs=[
            pl.BlockSpec((size // 2, HEAD, width), lambda i, s: (i, 0, 0)),
            pl.BlockSpec((size // 4, count, width), lambda i, s: (i, 0, 0)),
            pl.BlockSpec((size // 4, count, width), lambda i, s: (i, 0, 0)),
        ],
        scratch=[pltpu.VMEM((8, width), F32), pltpu.VMEM((count + rank, own_rows), BF16)],
        flops=2 * count * own_rows * full,
        moved=2 * own_rows * full,
    )(where, in_hbm(turned), in_hbm(base_weight), in_hbm(down_rows))
    head = exchange(head, "tensor")
    got = shift(give, core_pairs)
    half = size // 4
    mine = pl.BlockSpec((half // 2, count, width), lambda i, s, t: (s[2] * 2 + i, 0, 0))
    theirs = pl.BlockSpec((half // 2, count, width), lambda i, s, t: ((1 - s[2]) * 2 + i, 0, 0))
    out = pl.BlockSpec((half // 2, count, width), lambda i, s, t: (i, 0, 0))
    low, keep, give = call(
        halves_kernel,
        [shaped(2 * rank, width), shaped(zs, count, width), shaped(zs, count, width)],
        scalars=2,
        grid=(2,),
        in_specs=[whole(own_rows, count), whole(wide, own_rows), mine, mine, theirs, theirs],
        out_specs=[whole(2 * rank, width), out, out],
        flops=2 * count * own_rows * wide,
        moved=12 * zs * count * width,
    )(where, seg_lengths, turned, down_flat, keep, got, keep, got)
    got = shift(give, hi_pairs)

    def along_z(step):
        return [
            (h * 2 * zs + a * 2 + c, h * 2 * zs + (a + step) % zs * 2 + c)
            for h in range(2)
            for a in range(zs)
            for c in range(2)
        ]

    second = call(
        squares_kernel,
        shaped(adapters, 2, width, dtype=F32),
        scalars=1,
        grid=(1,),
        in_specs=[
            whole(size, HEAD, width),
            pl.BlockSpec((1, rank, width), lambda i, s: (s[0], 0, 0)),
        ],
        out_specs=whole(adapters, 2, width),
        moved=2 * size * HEAD * width,
    )(where, head, adapter_up)
    second = exchange(second, "dp")

    up3, down2, near = call(
        lift_kernel,
        [shaped(n, count, width) for n in (3, 2, 3)],
        scalars=1,
        grid=(1,),
        in_specs=[whole(zs, count, width)] * 2,
        out_specs=[whole(n, count, width) for n in (3, 2, 3)],
        moved=6 * zs * count * width,
    )(where, keep, got)
    up3 = shift(up3, along_z(1))
    down2 = shift(down2, along_z(-1))

    share, third, norms = call(
        scale_kernel,
        [
            shaped(count, width),
            shaped(2 * zs, 4 * rank, width),
            shaped(adapters, width, dtype=F32),
        ],
        scalars=2,
        grid=(1,),
        in_specs=[
            whole(adapters, 2, width),
            whole(adapters, width),
            whole(count, width),
            whole(wide, width),
            whole(2 * rank, width),
        ],
        out_specs=[
            whole(count, width),
            whole(2 * zs, 4 * rank, width),
            whole(adapters, width),
        ],
        flops=2 * count * wide * width,
        moved=8 * count * width,
    )(where, seg_lengths, second, magnitude, cotangent, up_own, low)
    third = exchange(third, "tensor", core_groups)
    other = shift(share, hi_pairs)
    scaled = whole(count, width)
    to_up, to_down, base = call(
        far_kernel,
        [shaped(3, count, width), shaped(3, count, width), shaped(count, width, dtype=F32)],
        grid=(1,),
        in_specs=[whole(n, count, width) for n in (3, 3, 2)] + [scaled] * 2,
        out_specs=[whole(3, count, width), whole(3, count, width), whole(count, width)],
        moved=36 * count * width,
    )(near, up3, down2, share, other)
    below = shift(to_up, along_z(3))
    above = shift(to_down, along_z(-3))
    ranks = call(
        sums_kernel,
        shaped(4 * rank, width),
        grid=(1,),
        in_specs=[whole(2 * zs, 4 * rank, width)],
        out_specs=whole(4 * rank, width),
        moved=2 * zs * 4 * rank * width,
    )(third)
    other_ranks = shift(ranks, core_pairs)

    before, after = call(
        pack_kernel,
        [shaped(4, count, width), shaped(6, count, width)],
        grid=(1,),
        in_specs=[scaled] * 2 + [whole(3, count, width)] * 2,
        out_specs=[whole(4, count, width), whole(6, count, width)],
        moved=32 * count * width,
    )(share, other, below, above)
    from_below = shift(after, along_z(1))
    from_above = shift(before, along_z(-1))
    gather_a = call(
        join_kernel,
        shaped(2 * zs, count, width),
        grid=(1,),
        in_specs=[whole(n, count, width) for n in (6, 6, 4)],
        out_specs=whole(2 * zs, count, width),
        moved=8 * zs * count * width,
    )(after, from_below, from_above)
    gather_b = shift(gather_a, core_pairs)

    lines = own_rows // LANES * rank + rank + rank // 2
    fourth, low_wide, back_wide = call(
        grads_kernel,
        [shaped(adapters, lines, width), shaped(wide, count), shaped(wide, count)],
        scalars=2,
        grid=(1,),
        in_specs=[
            whole(4 * rank, width),
            whole(4 * rank, width),
            whole(count, width),
            whole(wide, width),
            whole(own_rows, count),
        ],
        out_specs=[whole(adapters, lines, width), whole(wide, count), whole(wide, count)],
        flops=2 * count * wide * (own_rows + width),
        moved=4 * adapters * lines * width,
    )(where, seg_lengths, ranks, other_ranks, share, up_own, turned)
    fourth = exchange(fourth, "dp")

    first_block = pl.BlockSpec((1, count, width), lambda i, *s: (0, 0, 0))
    projected, mag = call(
        hidden_kernel,
        [shaped(count, width), shaped(adapters, width)],
        scalars=2,
        grid=(1,),
        in_specs=[
            whole(count, width),
            first_block,
            first_block,
            whole(wide, count),
            whole(wide, width),
            whole(adapters, width),
            whole(adapters, width),
            whole(count, width),
        ],
        out_specs=[whole(count, width), whole(adapters, width)],
        flops=2 * count * wide * width,
        moved=16 * count * width,
    )(where, seg_lengths, base, below, above, low_wide, up_own, norms, magnitude,
      cotangent)

    fifth = call(
        total_kernel,
        shaped(adapters, lines + rank, width),
        grid=(1,),
        in_specs=[whole(adapters, lines, width), whole(adapters, width)],
        out_specs=whole(adapters, lines + rank, width),
        moved=4 * adapters * lines * width,
    )(fourth, mag)
    fifth = exchange(fifth, "dp")

    per = 4
    offsets = (0, -3, 3, -1, -4, 2, 1, -2)

    def column(k, x_bit, c_bit):
        def at(i, s):
            off = jnp.where(i == 0, offsets[k], offsets[per + k])
            block = (s[3] + off + zs) % zs
            return (0, (s[2] ^ x_bit) * (2 * zs) + block * 2 + (s[1] ^ c_bit))

        return pl.BlockSpec((own_rows, width), at)

    def columns(c_bit):
        return [column(k, x, c_bit) for k in range(per) for x in range(2)]

    block = pl.BlockSpec((2 * per, count, width), lambda i, s: (i, 0, 0))
    weights = [in_hbm(base_weight)] * (2 * per)
    part = call(
        tokens_kernel,
        shaped(own_rows, count, dtype=F32),
        scalars=1,
        grid=(zs // per,),
        in_specs=[block] + columns(0) + [whole(wide, own_rows), whole(wide, count)],
        out_specs=whole(own_rows, count),
        scratch=[pltpu.VMEM((own_rows, count), F32)],
        flops=count * own_rows * (full + 2 * wide),
        moved=own_rows * full,
    )(where, gather_a, *weights, down_flat, back_wide)
    grad_tokens = call(
        tokens_rest_kernel,
        shaped(own_rows, count),
        scalars=1,
        grid=(zs // per,),
        in_specs=[block] + columns(1) + [whole(own_rows, count)],
        out_specs=whole(own_rows, count),
        scratch=[pltpu.VMEM((own_rows, count), F32)],
        flops=count * own_rows * full,
        moved=own_rows * full,
    )(where, gather_b, *weights, part)

    grad_down, grad_up, grad_magnitude = call(
        final_kernel,
        [
            shaped(adapters, rank, own_rows),
            shaped(adapters, rank, width, dtype=F32),
            shaped(adapters, width, dtype=F32),
        ],
        grid=(1,),
        in_specs=[whole(adapters, lines + rank, width), whole(adapters, width)],
        out_specs=[
            whole(adapters, rank, own_rows),
            whole(adapters, rank, width),
            whole(adapters, width),
        ],
        moved=4 * adapters * lines * width,
    )(fifth, norms)
    return (projected, grad_tokens.T, jnp.transpose(grad_down, (0, 2, 1)), grad_up, grad_magnitude)


def solution(mesh):
    placed = (
        P("dp", "tensor"),
        P("tensor", None),
        P(None, "tensor", None),
        P(None, None, "tensor"),
        P(None, "tensor"),
        P(),
        P("dp", "tensor"),
    )
    return jax.shard_map(
        local,
        mesh=mesh,
        in_specs=placed,
        out_specs=(
            P("dp", "tensor"),
            P("dp", "tensor"),
            P(None, "tensor", None),
            P(None, None, "tensor"),
            P(None, "tensor"),
        ),
        check_vma=False,
    )
```
